32 devices in a mesh: dp: 4 (over y, core), tm: 8 (over z, x).
Axes of the slice: x: 2, y: 2, z: 4, core: 2. Of those that a mesh axis runs over, the one named last changes fastest.
Arguments:
- latents: bfloat16 [4, 64, 64, 1280], P('dp', 'tm'), may hold values from -6 to 6
- conv_weight: bfloat16 [1280, 3840], replicated, may hold values from -0.09375 to 0.09375
- qkv_weight: bfloat16 [1280, 1920], replicated, may hold values from -2 to 2
- out_weight: bfloat16 [640, 1280], replicated, may hold values from -0.25 to 0.25
- out_cotangent: bfloat16 [4, 32, 64, 1280], P('dp', 'tm'), may hold values from -6 to 6
Outputs:
- input_grad: bfloat16 [4, 64, 64, 1280], P('dp', 'tm')
- conv_grad: bfloat16 [1280, 3840], P('tm')
- qkv_grad: bfloat16 [1280, 1920], P('tm')
- proj_grad: bfloat16 [640, 1280], P('tm')
The draws below stay inside these ranges and needn't reach their ends.
All inputs are finite; a program needn't handle non-finite values.
Results may differ from the reference program's by a relative error of at most 0.04.
Values may be sent and summed in bfloat16 or wider, within the bound.
A program may use at most 192 MiB of HBM per device.

```python
import math
import jax
import jax.numpy as jnp
from jax import lax

CH = 1280
HEADS = 10
HEAD = 64
S = 64
HD = 640
FRAMES = 64
OUTF = 32
VIDEOS = 4


def draw_qkv_weight(key, part):
    first_key = jax.random.fold_in(jax.random.fold_in(key, 17), 0)
    base = jax.random.normal(first_key, (CH, 3 * HD), jnp.float32) / math.sqrt(CH)
    result = base
    return result.astype(jnp.bfloat16)


def with_spikes(array, own_key, source, target, shards_of, factor):
    def block_of(axis_at):
        return (jnp.arange(array.shape[axis_at]) // (array.shape[axis_at] // shards_of)).reshape((-1,) + (1,) * (array.ndim - 1 - axis_at))

    first = jax.random.permutation(own_key, shards_of)[block_of(target)]
    second = (block_of(target) + shards_of // 2) % shards_of
    return jnp.where((block_of(source) == first) | (block_of(source) == second), factor * array, array)


def levels(own_key, shape, cuts, least, largest):
    def one(position, shards_of):
        draws = jax.random.uniform(jax.random.fold_in(jax.random.fold_in(own_key, 6), position), (shards_of,), jnp.float32, least / len(cuts), largest / len(cuts))
        return jnp.repeat(jnp.exp(draws), shape[position] // shards_of).reshape((-1,) + (1,) * (len(shape) - position - 1))

    factor_of = one(*cuts[0])
    for cut in cuts[1:]:
        factor_of = factor_of * one(*cut)
    return factor_of


def bell_draw(key, dims, scale, reach, cuts=(), dtype=jnp.bfloat16):
    values = jax.random.normal(key, dims, jnp.float32) * scale
    if len(cuts) > 0:
        values = levels(key, dims, cuts, -0.22, 0.18) * values
    return jnp.clip(values, min=-reach, max=reach).astype(dtype)


def gaussian_with(own_key, dims, deviation, most, shards, heavy, kind=jnp.bfloat16):
    drawn = deviation * jax.random.normal(own_key, dims, jnp.float32)
    if shards:
        drawn = drawn * levels(own_key, dims, shards, -0.22, 0.18)
    return jnp.clip(with_spikes(drawn, jax.random.fold_in(own_key, 3), *heavy), -most, most).astype(kind)


def setup_inputs(seed: int = 0) -> dict:
    splits = jax.random.split(jax.random.key(seed), 6)
    return {
        "latents": gaussian_with(splits[0], (VIDEOS, FRAMES, S, CH), 1.0, 6.0, ((0, 4), (1, 8)), (1, 3, 8, 2.0)),
        "conv_weight": bell_draw(splits[1], (CH, 3 * CH), (3 * CH) ** -0.5, 0.09375),
        "qkv_weight": draw_qkv_weight(jax.random.fold_in(splits[5], 71), 0),
        "out_weight": bell_draw(splits[3], (HD, CH), HD ** -0.5, 0.25),
        "out_cotangent": bell_draw(splits[4], (VIDEOS, OUTF, S, CH), 1.0, 6.0, ((0, 4), (1, 8))),
    }


EPSILON = 1e-05

def rounded(values):
    return lax.optimization_barrier(values.astype(jnp.bfloat16))

def dot_rows(left_side, right_side):
    return jnp.dot(left_side, right_side, preferred_element_type=jnp.float32)

def attend_location(packed):
    qkv_one, grad_one = packed
    width = qkv_one.shape[-1] // 3
    shape = qkv_one.shape[:2] + (HEADS, HEAD)
    queries = qkv_one[..., :width].reshape(shape).astype(jnp.float32)
    keys = qkv_one[..., width:2 * width].reshape(shape).astype(jnp.float32)
    values = qkv_one[..., 2 * width:].reshape(shape).astype(jnp.float32)
    grad_att = grad_one.reshape(shape).astype(jnp.float32)
    scores = jnp.einsum('vqhd,vkhd->vhqk', queries, keys) / math.sqrt(HEAD)
    highest = lax.optimization_barrier(jnp.max(scores, axis=-1, keepdims=True))
    expo = jnp.exp(scores - highest)
    probs = expo / lax.optimization_barrier(jnp.sum(expo, axis=-1, keepdims=True))
    probs_b = rounded(probs).astype(jnp.float32)
    attended = rounded(jnp.einsum('vhqk,vkhd->vqhd', probs_b, values))
    grad_values = rounded(jnp.einsum('vhqk,vqhd->vkhd', probs_b, grad_att))
    grad_probs = jnp.einsum('vqhd,vkhd->vhqk', grad_att, values)
    row_delta = lax.optimization_barrier(jnp.sum(grad_att * attended.astype(jnp.float32), axis=-1))
    row_delta = jnp.transpose(row_delta, (0, 2, 1))[..., None]
    grad_scores = rounded(probs * (grad_probs - row_delta) / math.sqrt(HEAD)).astype(jnp.float32)
    grad_queries = rounded(jnp.einsum('vhqk,vkhd->vqhd', grad_scores, keys))
    grad_keys = rounded(jnp.einsum('vhqk,vqhd->vkhd', grad_scores, queries))
    flat_shape = qkv_one.shape[:2] + (width,)
    grad_qkv = jnp.concatenate([grad_queries.reshape(flat_shape), grad_keys.reshape(flat_shape), grad_values.reshape(flat_shape)], axis=-1)
    return (attended.reshape(flat_shape), grad_qkv)

def reference(latents, conv_weight, qkv_weight, out_weight, out_cotangent):
    videos, frames, places, width = latents.shape
    half = frames // 2
    attn_width = out_weight.shape[0]
    split = latents.reshape(videos, half, 2, places, width)
    even_frames = split[:, :, 0]
    odd_frames = split[:, :, 1]
    prev_frames = jnp.concatenate([jnp.zeros_like(odd_frames[:, :1]), odd_frames[:, :-1]], axis=1)
    total_rows = videos * half * places

    def as_rows(values):
        return values.reshape(total_rows, values.shape[-1])
    tap_zero = conv_weight[:, :width]
    tap_one = conv_weight[:, width:2 * width]
    tap_two = conv_weight[:, 2 * width:]
    hidden = rounded(dot_rows(as_rows(prev_frames), tap_zero) + dot_rows(as_rows(even_frames), tap_one) + dot_rows(as_rows(odd_frames), tap_two))
    hidden_f = hidden.astype(jnp.float32)
    centred = hidden_f - lax.optimization_barrier(jnp.mean(hidden_f, axis=-1, keepdims=True))
    inv_std = lax.rsqrt(lax.optimization_barrier(jnp.mean(centred * centred, axis=-1, keepdims=True)) + EPSILON)
    unit_rows = centred * inv_std
    normed = rounded(unit_rows)
    qkv_rows = rounded(dot_rows(normed, qkv_weight))
    grad_rows = as_rows(out_cotangent)
    grad_att = rounded(dot_rows(grad_rows, out_weight.T))
    qkv_loc = jnp.transpose(qkv_rows.reshape(videos, half, places, 3 * attn_width), (2, 0, 1, 3))
    grad_loc = jnp.transpose(grad_att.reshape(videos, half, places, attn_width), (2, 0, 1, 3))
    attended_loc, grad_qkv_loc = lax.map(attend_location, (qkv_loc, grad_loc))
    attended = jnp.transpose(attended_loc, (1, 2, 0, 3)).reshape(total_rows, attn_width)
    grad_qkv = jnp.transpose(grad_qkv_loc, (1, 2, 0, 3)).reshape(total_rows, 3 * attn_width)
    grad_normed = dot_rows(grad_qkv, qkv_weight.T)
    correction = grad_normed - lax.optimization_barrier(jnp.mean(grad_normed, axis=-1, keepdims=True)) - unit_rows * lax.optimization_barrier(jnp.mean(grad_normed * unit_rows, axis=-1, keepdims=True))
    grad_hidden = rounded(grad_rows.astype(jnp.float32) + inv_std * correction)
    grad_four = grad_hidden.reshape(videos, half, places, width)
    grad_next = jnp.concatenate([grad_four[:, 1:], jnp.zeros_like(grad_four[:, :1])], axis=1)
    grad_even = dot_rows(grad_hidden, tap_one.T).astype(jnp.bfloat16)
    grad_odd = (dot_rows(grad_hidden, tap_two.T) + dot_rows(as_rows(grad_next), tap_zero.T)).astype(jnp.bfloat16)
    input_grad = jnp.stack([grad_even.reshape(videos, half, places, width), grad_odd.reshape(videos, half, places, width)], axis=2).reshape(latents.shape)
    grad_scale = 1.0 / math.sqrt(total_rows)
    conv_terms = jnp.concatenate([dot_rows(as_rows(prev_frames).T, grad_hidden), dot_rows(as_rows(even_frames).T, grad_hidden), dot_rows(as_rows(odd_frames).T, grad_hidden)], axis=1)
    conv_grad = (conv_terms * grad_scale).astype(jnp.bfloat16)
    qkv_grad = (dot_rows(normed.T, grad_qkv) * grad_scale).astype(jnp.bfloat16)
    proj_grad = (dot_rows(attended.T, grad_rows) * grad_scale).astype(jnp.bfloat16)
    return (input_grad, conv_grad, qkv_grad, proj_grad)
```

```python
import functools
import math

import jax
import jax.numpy as jnp
from jax import lax
from jax.experimental import pallas as pl
from jax.experimental.pallas import tpu as pltpu
from jax.sharding import PartitionSpec as P

HEADS = 10
HEAD = 64
EPSILON = 1e-05
TAPS = 3


def from_behind(shard, axis, by):
    devices = lax.axis_size(axis)
    pairs = [(i, i + by) for i in range(devices) if 0 <= i + by < devices]
    return lax.ppermute(shard, axis, pairs)


def swap(shard, axis, mask):
    devices = lax.axis_size(axis)
    return lax.ppermute(shard, axis, [(i, i ^ mask) for i in range(devices)])


def dot_rows(left_side, right_side):
    return jnp.dot(left_side, right_side, preferred_element_type=jnp.float32)


def dot_rows_t(left_side, right_side):
    return lax.dot_general(
        left_side, right_side, (((1,), (1,)), ((), ())), preferred_element_type=jnp.float32
    )


def dot_columns(left_side, right_side):
    return lax.dot_general(
        left_side, right_side, (((0,), (0,)), ((), ())), preferred_element_type=jnp.float32
    )


def flipped(index, mask, size):
    result = 0
    bit = 1
    while bit < size:
        own = index // bit % 2
        result += (1 - own if mask & bit else own) * bit
        bit *= 2
    return result


def attention_kernel(loc, width, qkv_ref, g_ref, grad_ref, attended_ref):
    rows = qkv_ref.shape[0]
    row_at = lax.broadcasted_iota(jnp.int32, (rows, rows), 0)
    column_at = lax.broadcasted_iota(jnp.int32, (rows, rows), 1)
    same = (row_at % loc) == (column_at % loc)
    lane = lax.broadcasted_iota(jnp.int32, (rows, 2 * HEAD), 1)
    scale = 1.0 / math.sqrt(HEAD)
    for pair in range(width // (2 * HEAD)):
        first = pair * 2 * HEAD
        q = qkv_ref[:, first : first + 2 * HEAD]
        k = qkv_ref[:, width + first : width + first + 2 * HEAD]
        v = qkv_ref[:, 2 * width + first : 2 * width + first + 2 * HEAD]
        g = g_ref[:, first : first + 2 * HEAD]
        zero = jnp.zeros_like(q)
        grad_q = grad_k = grad_v = attended = None
        kept = []
        for head in range(2):
            mine = (lane >= HEAD) if head else (lane < HEAD)
            q_h = jnp.where(mine, q, zero)
            v_h = jnp.where(mine, v, zero)
            g_h = jnp.where(mine, g, zero)
            scores = jnp.where(same, dot_rows_t(q_h, k) * scale, -1e30)
            expo = jnp.exp(scores - jnp.max(scores, axis=1, keepdims=True))
            probs = expo * (1.0 / jnp.sum(expo, axis=1, keepdims=True))
            probs_b = probs.astype(jnp.bfloat16)
            part = dot_rows(probs_b, v_h)
            attended = part if attended is None else attended + part
            part = dot_columns(probs_b, g_h)
            grad_v = part if grad_v is None else grad_v + part
            grad_probs = dot_rows_t(g_h, v)
            kept.append((mine, q_h, probs, grad_probs))
        attended_b = attended.astype(jnp.bfloat16)
        product = g.astype(jnp.float32) * attended_b.astype(jnp.float32)
        for mine, q_h, probs, grad_probs in kept:
            k_h = jnp.where(mine, k, zero)
            delta = jnp.sum(jnp.where(mine, product, 0.0), axis=1, keepdims=True)
            grad_scores = (probs * (grad_probs - delta) * scale).astype(jnp.bfloat16)
            part = dot_rows(grad_scores, k_h)
            grad_q = part if grad_q is None else grad_q + part
            part = dot_columns(grad_scores, q_h)
            grad_k = part if grad_k is None else grad_k + part
        grad_ref[:, first : first + 2 * HEAD] = grad_q.astype(jnp.bfloat16)
        grad_ref[:, width + first : width + first + 2 * HEAD] = grad_k.astype(jnp.bfloat16)
        grad_ref[:, 2 * width + first : 2 * width + first + 2 * HEAD] = grad_v.astype(
            jnp.bfloat16
        )
        attended_ref[:, first : first + 2 * HEAD] = attended_b


def attention(qkv_rows, grad_att, loc):
    rows, width = grad_att.shape
    vmem = pl.BlockSpec(memory_space=pltpu.VMEM)
    return pl.pallas_call(
        functools.partial(attention_kernel, loc, width),
        out_shape=[
            jax.ShapeDtypeStruct(qkv_rows.shape, jnp.bfloat16),
            jax.ShapeDtypeStruct(grad_att.shape, jnp.bfloat16),
        ],
        in_specs=[vmem, vmem],
        out_specs=[vmem, vmem],
        compiler_params=pltpu.CompilerParams(vmem_limit_bytes=40 * 1024 * 1024),
        cost_estimate=pl.CostEstimate(
            flops=14 * HEADS * rows * rows * 2 * HEAD,
            bytes_accessed=4 * (qkv_rows.size + grad_att.size),
            transcendentals=HEADS * rows * rows,
        ),
    )(qkv_rows, grad_att)


def tail_kernel(scale, tm_count, *refs):
    gh_loc, left_0, left_1, left_2, left_3, normed, gqkv, att, cot = refs[:9]
    gh_out, conv_out, qkv_out, proj_out = refs[9:13]
    ghf, ghx, normed_o, gqkv_o, att_o, cot_o, part = refs[13:20]
    share_c, conv_rx, conv_sx, conv_rz, conv_fin = refs[20:25]
    share_q, q_ry, q_sy, q_rx, q_sx, q_rz, q_fin = refs[25:32]
    share_p, p_ry, p_sy, p_rx, p_sx, p_rz, p_fin = refs[32:39]
    send_sem, recv_sem = refs[39:41]
    high = tm_count // 2
    hh = high // 2
    width = cot.shape[1]
    half = width // 2
    attn = att.shape[1]
    dp, tm = lax.axis_index("dp"), lax.axis_index("tm")
    core, my = dp % 2, dp // 2
    mx, mz = tm % 2, tm // 2
    x_peer = (dp, tm + 1 - 2 * mx)
    y_peer = (dp + 2 - 4 * my, tm)
    core_peer = (dp + 1 - 2 * core, tm)
    is_dest = mz // hh == core
    not_dest = mz // hh != core
    peers = [flipped(tm, d, tm_count) for d in range(1, tm_count)]

    barrier = pltpu.get_barrier_semaphore()
    for peer in [y_peer, core_peer] + [(dp, t) for t in peers]:
        pl.semaphore_signal(
            barrier, inc=1, device_id=peer, device_id_type=pl.DeviceIdType.MESH
        )
    pl.semaphore_wait(barrier, tm_count + 1)

    count = [0]

    def copy(source, target, peer):
        index = count[0]
        count[0] += 1
        return pltpu.make_async_remote_copy(
            src_ref=source,
            dst_ref=target,
            send_sem=send_sem.at[index],
            recv_sem=recv_sem.at[index],
            device_id=peer,
            device_id_type=pl.DeviceIdType.MESH,
        )

    def start(*copies):
        for one in copies:
            one.start()
        return copies

    sent = []

    def received(copies):
        for one in copies:
            one.wait_recv()
            sent.append(one)

    my_cols = pl.ds(pl.multiple_of(my * half, 128), half)
    other_cols = pl.ds(pl.multiple_of((1 - my) * half, 128), half)
    core_cols = pl.ds(pl.multiple_of(core * half, 128), half)
    peer_core_cols = pl.ds(pl.multiple_of((1 - core) * half, 128), half)

    swaps = start(
        copy(normed.at[:, peer_core_cols], normed_o, core_peer),
        copy(gqkv, gqkv_o, core_peer),
        copy(att, att_o, core_peer),
        copy(cot, cot_o, core_peer),
    )
    back = [copy(gh_loc.at[t], ghf.at[tm], (dp, t)) for t in peers]
    start(*back)
    ghf[tm] = gh_loc[tm]

    def spread(t):
        return (
            copy(ghf.at[t, :, other_cols], ghx.at[1, t], y_peer),
            copy(ghf.at[t, :, my_cols], ghx.at[0, t], core_peer),
        )

    spreads = [start(*spread(tm))]
    received(swaps)

    def add(a, b):
        return (a.astype(jnp.float32) + b.astype(jnp.float32)).astype(jnp.bfloat16)

    q_rows = share_q.shape[3]
    for tile in range(3):
        cols = slice(tile * attn, (tile + 1) * attn)
        result = dot_columns(normed[:, core_cols], gqkv[:, cols]) + dot_columns(
            normed_o[...], gqkv_o[:, cols]
        )
        for i in range(4 * hh):
            share_q[i // 4, i // 2 % 2, i % 2, :, cols] = result[
                i * q_rows : (i + 1) * q_rows
            ].astype(jnp.bfloat16)
    q_y = [copy(share_q.at[z, :, 1 - my], q_ry.at[z], y_peer) for z in range(hh)]
    start(q_y[0])
    p_rows = share_p.shape[3]
    step = attn // 2 // 128 * 128
    window = pl.ds(pl.multiple_of(core * step, 128), attn - step)
    for tile in range(2):
        cols = slice(tile * half, (tile + 1) * half)
        part[...] = dot_columns(att[:, window], cot[:, cols]) + dot_columns(
            att_o[:, window], cot_o[:, cols]
        )
        offset = pl.multiple_of(core * (attn // 2 - step), 8)
        result = part[pl.ds(offset, attn // 2), :]
        for i in range(2 * hh):
            share_p[i // 2, i % 2, tile] = result[i * p_rows : (i + 1) * p_rows].astype(
                jnp.bfloat16
            )
    p_y = copy(share_p.at[:, :, 1 - my], p_ry, y_peer)
    start(p_y)

    for one, t in zip(back, peers):
        received([one])
        spreads.append(start(*spread(t)))
    start(*q_y[1:])
    gh_out[...] = ghf[...]
    forwards = []
    for (by_y, by_core), t in zip(spreads, [tm] + peers):
        received([by_y])
        forwards += start(copy(ghx.at[1, t], ghx.at[2, t], core_peer))

    def y_add(stay, came, total):
        total[...] = add(stay[...], came[...])

    received([q_y[0]])
    y_add(share_q.at[0, :, my], q_ry.at[0], q_sy.at[0])
    q_x = [copy(q_sy.at[z, 1 - mx], q_rx.at[z], x_peer) for z in range(hh)]
    start(q_x[0])
    received([by_core for _, by_core in spreads] + forwards)

    rows = left_0.shape[0]
    c_rows = share_c.shape[3]
    conv_x = {}
    for tap in range(TAPS):
        cols = slice(tap * half, (tap + 1) * half)
        result = dot_columns(left_0[:, cols], ghf[:, :, my_cols].reshape(rows, half))
        for k, left in enumerate((left_1, left_2, left_3)):
            result += dot_columns(left[:, cols], ghx[k].reshape(rows, half))
        for i in range(2 * hh):
            share_c[tap, i // 2, i % 2] = result[i * c_rows : (i + 1) * c_rows].astype(
                jnp.bfloat16
            )
        for z in range(hh):
            conv_x[tap, z] = copy(share_c.at[tap, z, 1 - mx], conv_rx.at[tap, z], x_peer)
            start(conv_x[tap, z])

    received([p_y])
    y_add(share_p.at[:, :, my], p_ry, p_sy)
    p_x = copy(p_sy.at[:, 1 - mx], p_rx, x_peer)
    start(p_x)
    for z in range(1, hh):
        received([q_y[z]])
        y_add(share_q.at[z, :, my], q_ry.at[z], q_sy.at[z])
        start(q_x[z])

    def z_copies(total, came):
        copies = []
        for d in range(1, high):
            target = (mz + d) % high
            copies.append(
                (
                    target // hh == core,
                    copy(total.at[target % hh], came.at[d - 1], (dp, target * 2 + mx)),
                )
            )
        return copies

    def z_start(copies):
        for chosen, one in copies:
            pl.when(chosen)(one.start)

    z_sent = []

    def z_receive(copies, stay, came, place):
        z_sent.extend(copies)

        @pl.when(is_dest)
        def _():
            for _, one in copies:
                one.wait_recv()
            total = stay[mz % hh].astype(jnp.float32)
            for d in range(1, high):
                total += came[d - 1].astype(jnp.float32)
            place[...] = (total * scale).astype(jnp.bfloat16)

    received([q_x[0]])
    y_add(q_sy.at[0, mx], q_rx.at[0], q_sx.at[0])
    conv_z = []
    for tap in range(TAPS):
        for z in range(hh):
            received([conv_x[tap, z]])
            y_add(share_c.at[tap, z, mx], conv_rx.at[tap, z], conv_sx.at[tap, z])
        conv_z.append(z_copies(conv_sx.at[tap], conv_rz.at[tap]))
        z_start(conv_z[tap])
    received([p_x])
    y_add(p_sy.at[:, mx], p_rx, p_sx)
    p_z = z_copies(p_sx, p_rz)
    z_start(p_z)
    for z in range(1, hh):
        received([q_x[z]])
        y_add(q_sy.at[z, mx], q_rx.at[z], q_sx.at[z])
    q_z = z_copies(q_sx, q_rz)
    z_start(q_z)

    units = [
        (conv_z[tap], conv_sx.at[tap], conv_rz.at[tap], conv_fin.at[tap]) for tap in range(TAPS)
    ] + [(p_z, p_sx, p_rz, p_fin), (q_z, q_sx, q_rz, q_fin)]
    last = []
    for copies, stay, came, fin in units:
        z_receive(copies, stay, came, fin.at[my])
        to_y = copy(fin.at[my], fin.at[my], y_peer)
        own_to_core = copy(fin.at[my], fin.at[my], core_peer)
        other_to_core = copy(fin.at[1 - my], fin.at[1 - my], core_peer)
        last.append((to_y, own_to_core, other_to_core))

        @pl.when(is_dest)
        def _():
            to_y.start()
            own_to_core.start()

    for to_y, own_to_core, other_to_core in last:

        @pl.when(is_dest)
        def _():
            to_y.wait_recv()
            other_to_core.start()

        @pl.when(not_dest)
        def _():
            own_to_core.wait_recv()
            other_to_core.wait_recv()

    for tap in range(TAPS):
        for y in range(2):
            conv_out[:, tap * width + y * half : tap * width + (y + 1) * half] = conv_fin[tap, y]
    for y in range(2):
        proj_out[:, y * half : (y + 1) * half] = p_fin[y]
    qkv_out[...] = q_fin[...]

    for one in sent:
        one.wait_send()
    for chosen, one in z_sent:
        pl.when(chosen)(one.wait_send)

    @pl.when(is_dest)
    def _():
        for copies in last:
            for one in copies:
                one.wait_send()


def tail(gh_loc, lefts, normed, gqkv, att, cot, scale):
    tm_count, block, width = gh_loc.shape
    high = tm_count // 2
    hh = high // 2
    half = width // 2
    rows, attn = att.shape
    c_rows = width // tm_count
    q_rows = c_rows // 2
    p_rows = attn // tm_count
    bf16 = jnp.bfloat16

    def vmem(*shape, dtype=bf16):
        return pltpu.VMEM(shape, dtype)

    scratch = [
        vmem(tm_count, block, width),
        vmem(3, tm_count, block, half),
        vmem(rows, half),
        vmem(rows, 3 * attn),
        vmem(rows, attn),
        vmem(rows, width),
        vmem(attn - attn // 2 // 128 * 128, half, dtype=jnp.float32),
        vmem(TAPS, hh, 2, c_rows, half),
        vmem(TAPS, hh, c_rows, half),
        vmem(TAPS, hh, c_rows, half),
        vmem(TAPS, high - 1, c_rows, half),
        vmem(TAPS, 2, c_rows, half),
        vmem(hh, 2, 2, q_rows, 3 * attn),
        vmem(hh, 2, q_rows, 3 * attn),
        vmem(hh, 2, q_rows, 3 * attn),
        vmem(hh, q_rows, 3 * attn),
        vmem(hh, q_rows, 3 * attn),
        vmem(high - 1, q_rows, 3 * attn),
        vmem(2, q_rows, 3 * attn),
        vmem(hh, 2, 2, p_rows, half),
        vmem(hh, 2, p_rows, half),
        vmem(hh, 2, p_rows, half),
        vmem(hh, p_rows, half),
        vmem(hh, p_rows, half),
        vmem(high - 1, p_rows, half),
        vmem(2, p_rows, half),
    ]
    copies = 4 + (tm_count - 1) + 3 * tm_count + (2 + 5) * hh + 3 + 5 * (high - 1) + 15
    semaphores = pltpu.SemaphoreType.DMA((copies,))
    space = pl.BlockSpec(memory_space=pltpu.VMEM)
    flops = 2 * rows * 2 * (half * 3 * attn + attn * width + TAPS * 2 * half * half)
    return pl.pallas_call(
        functools.partial(tail_kernel, scale, tm_count),
        out_shape=[
            jax.ShapeDtypeStruct(gh_loc.shape, bf16),
            jax.ShapeDtypeStruct((c_rows, TAPS * width), bf16),
            jax.ShapeDtypeStruct((2, q_rows, 3 * attn), bf16),
            jax.ShapeDtypeStruct((p_rows, width), bf16),
        ],
        in_specs=[space] * 9,
        out_specs=[space] * 4,
        scratch_shapes=scratch + [semaphores, semaphores],
        compiler_params=pltpu.CompilerParams(
            collective_id=0, has_side_effects=True, vmem_limit_bytes=50 * 1024 * 1024
        ),
        cost_estimate=pl.CostEstimate(
            flops=flops, bytes_accessed=200_000_000, transcendentals=0
        ),
    )(gh_loc, *lefts, normed, gqkv, att, cot)


def local(latents, conv_weight, qkv_weight, out_weight, out_cotangent):
    videos, frames, places, width = latents.shape
    half = frames // 2
    attn_width = out_weight.shape[0]
    dp_count = lax.axis_size("dp")
    tm_count = lax.axis_size("tm")
    loc = places // tm_count
    rows = half * places
    core = lax.axis_index("dp") % 2

    def as_rows(values):
        return values.reshape(rows, values.shape[-1])

    def to_locations(values):
        blocks = values.reshape(tm_count, half * loc, width)
        return lax.all_to_all(blocks, "tm", split_axis=0, concat_axis=0, tiled=True).reshape(
            rows, width
        )

    split = latents.reshape(half, 2, tm_count, loc, width)
    rim_input = from_behind(split[half - 1, 1], "tm", 1)
    split = jnp.transpose(split, (1, 2, 0, 3, 4))
    even_frames, odd_frames = split[0], split[1]
    prev_frames = jnp.concatenate([rim_input[:, None], odd_frames[:, : half - 1]], axis=1)
    cotangent_rows = as_rows(
        jnp.transpose(out_cotangent.reshape(half, tm_count, loc, width), (1, 0, 2, 3))
    )
    cot = to_locations(cotangent_rows)

    tap_zero = conv_weight[:, :width]
    tap_one = conv_weight[:, width : 2 * width]
    tap_two = conv_weight[:, 2 * width :]
    taps = [as_rows(prev_frames), as_rows(even_frames), as_rows(odd_frames)]

    def columns_of(which):
        size = width // 2
        return jnp.concatenate(
            [lax.dynamic_slice_in_dim(one, which * size, size, axis=1) for one in taps], axis=1
        )

    mine, others = columns_of(core), columns_of(1 - core)
    lefts = [mine, swap(others, "dp", 1), swap(mine, "dp", 2), swap(others, "dp", 3)]

    hidden = (
        dot_rows(taps[0], tap_zero) + dot_rows(taps[1], tap_one) + dot_rows(taps[2], tap_two)
    ).astype(jnp.bfloat16)
    hidden = to_locations(hidden)
    grad_att = dot_rows_t(cot, out_weight).astype(jnp.bfloat16)
    hidden_f = hidden.astype(jnp.float32)
    centred = hidden_f - jnp.mean(hidden_f, axis=-1, keepdims=True)
    inv_std = lax.rsqrt(jnp.mean(centred * centred, axis=-1, keepdims=True) + EPSILON)
    unit_rows = centred * inv_std
    normed = unit_rows.astype(jnp.bfloat16)
    qkv_rows = dot_rows(normed, qkv_weight).astype(jnp.bfloat16)
    grad_qkv, attended = attention(qkv_rows, grad_att, loc)

    grad_normed = dot_rows_t(grad_qkv, qkv_weight)
    correction = (
        grad_normed
        - jnp.mean(grad_normed, axis=-1, keepdims=True)
        - unit_rows * jnp.mean(grad_normed * unit_rows, axis=-1, keepdims=True)
    )
    grad_hidden = (cot.astype(jnp.float32) + inv_std * correction).astype(jnp.bfloat16)

    grad_scale = 1.0 / math.sqrt(dp_count * tm_count * rows)
    grad_four, conv_grad, qkv_grad, proj_grad = tail(
        grad_hidden.reshape(tm_count, half * loc, width),
        lefts,
        normed,
        grad_qkv,
        attended,
        cot,
        grad_scale,
    )
    qkv_grad = qkv_grad.reshape(-1, qkv_grad.shape[-1])

    grad_hidden = as_rows(grad_four)
    grad_four = grad_four.reshape(tm_count, half, loc, width)
    rim_after = from_behind(grad_four[:, 0], "tm", -1)
    grad_next = jnp.concatenate([grad_four[:, 1:], rim_after[:, None]], axis=1)
    grad_even = dot_rows_t(grad_hidden, tap_one).astype(jnp.bfloat16)
    grad_odd = (dot_rows_t(grad_hidden, tap_two) + dot_rows_t(as_rows(grad_next), tap_zero)).astype(
        jnp.bfloat16
    )
    by_frame = (tm_count, half, loc, width)
    input_grad = jnp.transpose(
        jnp.stack([grad_even.reshape(by_frame), grad_odd.reshape(by_frame)], axis=0),
        (2, 0, 1, 3, 4),
    ).reshape(latents.shape)
    return (input_grad, conv_grad, qkv_grad, proj_grad)


def solution(mesh):
    return jax.shard_map(
        local,
        mesh=mesh,
        in_specs=(P("dp", "tm", None, None), P(), P(), P(), P("dp", "tm", None, None)),
        out_specs=(P("dp", "tm", None, None), P("tm", None), P("tm", None), P("tm", None)),
        check_vma=False,
    )
```

```python
import functools
import math

import jax
import jax.numpy as jnp
from jax import lax
from jax.experimental import pallas as pl
from jax.experimental.pallas import tpu as pltpu
from jax.sharding import PartitionSpec as P

HEADS = 10
HEAD = 64
EPSILON = 1e-05
TAPS = 3


def from_behind(shard, axis, by):
    devices = lax.axis_size(axis)
    pairs = [(i, i + by) for i in range(devices) if 0 <= i + by < devices]
    return lax.ppermute(shard, axis, pairs)


def swap(shard, axis, mask):
    devices = lax.axis_size(axis)
    return lax.ppermute(shard, axis, [(i, i ^ mask) for i in range(devices)])


def dot_rows(left_side, right_side):
    return jnp.dot(left_side, right_side, preferred_element_type=jnp.float32)


def dot_rows_t(left_side, right_side):
    return lax.dot_general(
        left_side, right_side, (((1,), (1,)), ((), ())), preferred_element_type=jnp.float32
    )


def dot_columns(left_side, right_side):
    return lax.dot_general(
        left_side, right_side, (((0,), (0,)), ((), ())), preferred_element_type=jnp.float32
    )


def flipped(index, mask, size):
    result = 0
    bit = 1
    while bit < size:
        own = index // bit % 2
        result += (1 - own if mask & bit else own) * bit
        bit *= 2
    return result


def attention_kernel(loc, width, qkv_ref, g_ref, grad_ref, attended_ref):
    rows = qkv_ref.shape[0]
    row_at = lax.broadcasted_iota(jnp.int32, (rows, rows), 0)
    column_at = lax.broadcasted_iota(jnp.int32, (rows, rows), 1)
    same = (row_at % loc) == (column_at % loc)
    lane = lax.broadcasted_iota(jnp.int32, (rows, 2 * HEAD), 1)
    scale = 1.0 / math.sqrt(HEAD)
    for pair in range(width // (2 * HEAD)):
        first = pair * 2 * HEAD
        q = qkv_ref[:, first : first + 2 * HEAD]
        k = qkv_ref[:, width + first : width + first + 2 * HEAD]
        v = qkv_ref[:, 2 * width + first : 2 * width + first + 2 * HEAD]
        g = g_ref[:, first : first + 2 * HEAD]
        zero = jnp.zeros_like(q)
        grad_q = grad_k = grad_v = attended = None
        kept = []
        for head in range(2):
            mine = (lane >= HEAD) if head else (lane < HEAD)
            q_h = jnp.where(mine, q, zero)
            v_h = jnp.where(mine, v, zero)
            g_h = jnp.where(mine, g, zero)
            scores = jnp.where(same, dot_rows_t(q_h, k) * scale, -1e30)
            expo = jnp.exp(scores - jnp.max(scores, axis=1, keepdims=True))
            probs = expo * (1.0 / jnp.sum(expo, axis=1, keepdims=True))
            probs_b = probs.astype(jnp.bfloat16)
            part = dot_rows(probs_b, v_h)
            attended = part if attended is None else attended + part
            part = dot_columns(probs_b, g_h)
            grad_v = part if grad_v is None else grad_v + part
            grad_probs = dot_rows_t(g_h, v)
            kept.append((mine, q_h, probs, grad_probs))
        attended_b = attended.astype(jnp.bfloat16)
        product = g.astype(jnp.float32) * attended_b.astype(jnp.float32)
        for mine, q_h, probs, grad_probs in kept:
            k_h = jnp.where(mine, k, zero)
            delta = jnp.sum(jnp.where(mine, product, 0.0), axis=1, keepdims=True)
            grad_scores = (probs * (grad_probs - delta) * scale).astype(jnp.bfloat16)
            part = dot_rows(grad_scores, k_h)
            grad_q = part if grad_q is None else grad_q + part
            part = dot_columns(grad_scores, q_h)
            grad_k = part if grad_k is None else grad_k + part
        grad_ref[:, first : first + 2 * HEAD] = grad_q.astype(jnp.bfloat16)
        grad_ref[:, width + first : width + first + 2 * HEAD] = grad_k.astype(jnp.bfloat16)
        grad_ref[:, 2 * width + first : 2 * width + first + 2 * HEAD] = grad_v.astype(
            jnp.bfloat16
        )
        attended_ref[:, first : first + 2 * HEAD] = attended_b


def attention(qkv_rows, grad_att, loc):
    rows, width = grad_att.shape
    vmem = pl.BlockSpec(memory_space=pltpu.VMEM)
    return pl.pallas_call(
        functools.partial(attention_kernel, loc, width),
        out_shape=[
            jax.ShapeDtypeStruct(qkv_rows.shape, jnp.bfloat16),
            jax.ShapeDtypeStruct(grad_att.shape, jnp.bfloat16),
        ],
        in_specs=[vmem, vmem],
        out_specs=[vmem, vmem],
        compiler_params=pltpu.CompilerParams(vmem_limit_bytes=40 * 1024 * 1024),
        cost_estimate=pl.CostEstimate(
            flops=14 * HEADS * rows * rows * 2 * HEAD,
            bytes_accessed=4 * (qkv_rows.size + grad_att.size),
            transcendentals=HEADS * rows * rows,
        ),
    )(qkv_rows, grad_att)


def tail_kernel(scale, tm_count, *refs):
    gh_loc, left_0, left_1, left_2, left_3, normed, gqkv, att, cot, weight_hbm = refs[:10]
    even_out, odd_out, conv_out, qkv_out, proj_out = refs[10:15]
    ghf, ghx, normed_o, gqkv_o, att_o, cot_o, part = refs[15:22]
    share_c, conv_rx, conv_sx, conv_rz, conv_fin = refs[22:27]
    share_q, q_r1, q_s1, q_r2, q_sx, q_rz, q_fin = refs[27:34]
    share_p, p_r1, p_s1, p_r2, p_sx, p_rz, p_fin = refs[34:41]
    weight, rim_out, rim_in = refs[41:44]
    send_sem, recv_sem, weight_sem = refs[44:47]
    high = tm_count // 2
    hh = high // 2
    width = cot.shape[1]
    half = width // 2
    attn = att.shape[1]
    dp, tm = lax.axis_index("dp"), lax.axis_index("tm")
    core, my = dp % 2, dp // 2
    mx, mz = tm % 2, tm // 2
    x_peer = (dp, tm + 1 - 2 * mx)
    y_peer = (dp + 2 - 4 * my, tm)
    core_peer = (dp + 1 - 2 * core, tm)
    is_dest = mz // hh == core
    not_dest = mz // hh != core
    peers = [flipped(tm, d, tm_count) for d in range(1, tm_count)]

    barrier = pltpu.get_barrier_semaphore()
    for peer in [y_peer, core_peer] + [(dp, t) for t in peers]:
        pl.semaphore_signal(
            barrier, inc=1, device_id=peer, device_id_type=pl.DeviceIdType.MESH
        )
    pl.semaphore_wait(barrier, tm_count + 1)

    count = [0]

    def copy(source, target, peer):
        index = count[0]
        count[0] += 1
        return pltpu.make_async_remote_copy(
            src_ref=source,
            dst_ref=target,
            send_sem=send_sem.at[index],
            recv_sem=recv_sem.at[index],
            device_id=peer,
            device_id_type=pl.DeviceIdType.MESH,
        )

    def start(*copies):
        for one in copies:
            one.start()
        return copies

    sent = []

    def received(copies):
        for one in copies:
            one.wait_recv()
            sent.append(one)

    my_cols = pl.ds(pl.multiple_of(my * half, 128), half)
    other_cols = pl.ds(pl.multiple_of((1 - my) * half, 128), half)
    core_cols = pl.ds(pl.multiple_of(core * half, 128), half)
    peer_core_cols = pl.ds(pl.multiple_of((1 - core) * half, 128), half)

    copied = pltpu.make_async_copy(weight_hbm, weight, weight_sem)
    copied.start()

    swaps = start(
        copy(normed.at[:, peer_core_cols], normed_o, core_peer),
        copy(gqkv, gqkv_o, core_peer),
        copy(att, att_o, core_peer),
        copy(cot, cot_o, core_peer),
    )
    back = [copy(gh_loc.at[t], ghf.at[tm], (dp, t)) for t in peers]
    start(*back)
    ghf[tm] = gh_loc[tm]

    def spread(t):
        return (
            copy(ghf.at[t, :, other_cols], ghx.at[1, t], y_peer),
            copy(ghf.at[t, :, my_cols], ghx.at[0, t], core_peer),
        )

    spreads = [start(*spread(tm))]
    received(swaps)

    def add(a, b):
        return (a.astype(jnp.float32) + b.astype(jnp.float32)).astype(jnp.bfloat16)

    q_rows = share_q.shape[3]
    for tile in range(3):
        cols = slice(tile * attn, (tile + 1) * attn)
        result = dot_columns(normed[:, core_cols], gqkv[:, cols]) + dot_columns(
            normed_o[...], gqkv_o[:, cols]
        )
        for i in range(4 * hh):
            share_q[i // 4, i // 2 % 2, i % 2, :, cols] = result[
                i * q_rows : (i + 1) * q_rows
            ].astype(jnp.bfloat16)

    def sums(share, first, total, second, result):
        steps = []
        for z in range(hh):
            if z < hh // 2:
                away, peer, stay = share.at[z, :, 1 - my], y_peer, share.at[z, :, my]
                away_2, peer_2, stay_2 = 1 - mx, x_peer, mx
            else:
                away, peer, stay = share.at[z, 1 - mx], x_peer, share.at[z, mx]
                away_2, peer_2, stay_2 = 1 - my, y_peer, my
            one = copy(away, first.at[z], peer)
            two = copy(total.at[z, away_2], second.at[z], peer_2)
            steps.append((one, stay, first.at[z], total.at[z], two, stay_2, second.at[z], result.at[z]))
        return steps

    q_steps = sums(share_q, q_r1, q_s1, q_r2, q_sx)
    start(*[one[0] for one in q_steps])
    p_rows = share_p.shape[3]
    step = attn // 2 // 128 * 128
    window = pl.ds(pl.multiple_of(core * step, 128), attn - step)
    for tile in range(2):
        cols = slice(tile * half, (tile + 1) * half)
        part[...] = dot_columns(att[:, window], cot[:, cols]) + dot_columns(
            att_o[:, window], cot_o[:, cols]
        )
        offset = pl.multiple_of(core * (attn // 2 - step), 8)
        result = part[pl.ds(offset, attn // 2), :]
        for i in range(2 * hh):
            share_p[i // 2, i % 2, tile] = result[i * p_rows : (i + 1) * p_rows].astype(
                jnp.bfloat16
            )
    p_steps = sums(share_p, p_r1, p_s1, p_r2, p_sx)
    start(*[one[0] for one in p_steps])

    for one, t in zip(back, peers):
        received([one])
        spreads.append(start(*spread(t)))
    loc = rim_in.shape[0] // tm_count
    rim_out[...] = (
        ghf[...].astype(jnp.float32)[:, :loc].reshape(tm_count * loc, width).astype(jnp.bfloat16)
    )
    rim = copy(rim_out, rim_in, (dp, (tm + tm_count - 1) % tm_count))
    pl.when(tm > 0)(rim.start)

    for one, stay, came, total, two, _, _, _ in q_steps + p_steps:
        received([one])
        total[...] = add(stay[...], came[...])
        start(two)
    forwards = []
    for (by_y, by_core), t in zip(spreads, [tm] + peers):
        received([by_y])
        forwards += start(copy(ghx.at[1, t], ghx.at[2, t], core_peer))
    received([by_core for _, by_core in spreads] + forwards)

    rows = left_0.shape[0]
    c_rows = share_c.shape[3]
    conv_x = {}
    for tap in range(TAPS):
        cols = slice(tap * half, (tap + 1) * half)
        result = dot_columns(left_0[:, cols], ghf[:, :, my_cols].reshape(rows, half))
        for k, left in enumerate((left_1, left_2, left_3)):
            result += dot_columns(left[:, cols], ghx[k].reshape(rows, half))
        for i in range(2 * hh):
            share_c[tap, i // 2, i % 2] = result[i * c_rows : (i + 1) * c_rows].astype(
                jnp.bfloat16
            )
        for z in range(hh):
            conv_x[tap, z] = copy(share_c.at[tap, z, 1 - mx], conv_rx.at[tap, z], x_peer)
            start(conv_x[tap, z])

    def z_copies(total, came):
        copies = []
        for d in range(1, high):
            target = (mz + d) % high
            copies.append(
                (
                    target // hh == core,
                    copy(total.at[target % hh], came.at[d - 1], (dp, target * 2 + mx)),
                )
            )
        return copies

    def z_start(copies):
        for chosen, one in copies:
            pl.when(chosen)(one.start)

    z_sent = []

    def z_receive(copies, stay, came, place):
        z_sent.extend(copies)

        @pl.when(is_dest)
        def _():
            for _, one in copies:
                one.wait_recv()
            total = stay[mz % hh].astype(jnp.float32)
            for d in range(1, high):
                total += came[d - 1].astype(jnp.float32)
            place[...] = (total * scale).astype(jnp.bfloat16)

    for _, _, _, total, two, stay, came, result in q_steps + p_steps:
        received([two])
        result[...] = add(total[stay], came[...])
    p_z = z_copies(p_sx, p_rz)
    z_start(p_z)
    q_z = z_copies(q_sx, q_rz)
    z_start(q_z)

    def conv_sum(tap):
        for z in range(hh):
            received([conv_x[tap, z]])
            conv_sx[tap, z] = add(share_c[tap, z, mx], conv_rx[tap, z])
        copies = z_copies(conv_sx.at[tap], conv_rz.at[tap])
        z_start(copies)
        return copies

    copied.wait()
    pl.when(tm > 0)(rim.wait_send)
    pl.when(tm < tm_count - 1)(rim.wait_recv)

    @pl.when(tm == tm_count - 1)
    def _():
        rim_in[...] = jnp.zeros_like(rim_in)

    gh_rows = ghf[...].reshape(rows, width)
    block = ghf.shape[1]

    def even_part(tile):
        part_of = slice(tile * half, (tile + 1) * half)
        grad = dot_rows_t(gh_rows, weight[part_of, width : 2 * width])
        even_out[:, :, part_of] = grad.astype(jnp.bfloat16).reshape(tm_count, block, half)

    def odd_part(tile):
        part_of = slice(tile * half, (tile + 1) * half)
        before = dot_rows_t(gh_rows, weight[part_of, :width]).reshape(tm_count, block, half)
        rims = dot_rows_t(rim_in[...], weight[part_of, :width]).reshape(tm_count, loc, half)
        grad = dot_rows_t(gh_rows, weight[part_of, 2 * width :]).reshape(tm_count, block, half)
        grad += jnp.concatenate([before[:, loc:], rims], axis=1)
        odd_out[:, :, part_of] = grad.astype(jnp.bfloat16)

    even_part(0)
    even_part(1)
    conv_z = [conv_sum(0)]
    odd_part(0)
    odd_part(1)

    last = []

    def gather(copies, stay, came, fin):
        z_receive(copies, stay, came, fin.at[my])
        to_y = copy(fin.at[my], fin.at[my], y_peer)
        own_to_core = copy(fin.at[my], fin.at[my], core_peer)
        other_to_core = copy(fin.at[1 - my], fin.at[1 - my], core_peer)
        last.append((to_y, own_to_core, other_to_core))

        @pl.when(is_dest)
        def _():
            to_y.start()
            own_to_core.start()

    gather(p_z, p_sx, p_rz, p_fin)
    conv_z.append(conv_sum(1))
    gather(q_z, q_sx, q_rz, q_fin)
    conv_z.append(conv_sum(2))
    for tap in range(TAPS):
        gather(conv_z[tap], conv_sx.at[tap], conv_rz.at[tap], conv_fin.at[tap])

    for to_y, own_to_core, other_to_core in last:

        @pl.when(is_dest)
        def _():
            to_y.wait_recv()
            other_to_core.start()

        @pl.when(not_dest)
        def _():
            own_to_core.wait_recv()
            other_to_core.wait_recv()

    for tap in range(TAPS):
        for y in range(2):
            conv_out[:, tap * width + y * half : tap * width + (y + 1) * half] = conv_fin[tap, y]
    for y in range(2):
        proj_out[:, y * half : (y + 1) * half] = p_fin[y]
    qkv_out[...] = q_fin[...]

    for one in sent:
        one.wait_send()
    for chosen, one in z_sent:
        pl.when(chosen)(one.wait_send)

    @pl.when(is_dest)
    def _():
        for copies in last:
            for one in copies:
                one.wait_send()


def tail(gh_loc, lefts, normed, gqkv, att, cot, conv_weight, loc, scale):
    tm_count, block, width = gh_loc.shape
    high = tm_count // 2
    hh = high // 2
    half = width // 2
    rows, attn = att.shape
    c_rows = width // tm_count
    q_rows = c_rows // 2
    p_rows = attn // tm_count
    bf16 = jnp.bfloat16

    def vmem(*shape, dtype=bf16):
        return pltpu.VMEM(shape, dtype)

    scratch = [
        vmem(tm_count, block, width),
        vmem(3, tm_count, block, half),
        vmem(rows, half),
        vmem(rows, 3 * attn),
        vmem(rows, attn),
        vmem(rows, width),
        vmem(attn - attn // 2 // 128 * 128, half, dtype=jnp.float32),
        vmem(TAPS, hh, 2, c_rows, half),
        vmem(TAPS, hh, c_rows, half),
        vmem(TAPS, hh, c_rows, half),
        vmem(TAPS, high - 1, c_rows, half),
        vmem(TAPS, 2, c_rows, half),
        vmem(hh, 2, 2, q_rows, 3 * attn),
        vmem(hh, 2, q_rows, 3 * attn),
        vmem(hh, 2, q_rows, 3 * attn),
        vmem(hh, q_rows, 3 * attn),
        vmem(hh, q_rows, 3 * attn),
        vmem(high - 1, q_rows, 3 * attn),
        vmem(2, q_rows, 3 * attn),
        vmem(hh, 2, 2, p_rows, half),
        vmem(hh, 2, p_rows, half),
        vmem(hh, 2, p_rows, half),
        vmem(hh, p_rows, half),
        vmem(hh, p_rows, half),
        vmem(high - 1, p_rows, half),
        vmem(2, p_rows, half),
        vmem(*conv_weight.shape),
        vmem(tm_count * loc, width),
        vmem(tm_count * loc, width),
    ]
    copies = 4 + (tm_count - 1) + 3 * tm_count + 7 * hh + 1 + 5 * (high - 1) + 15
    semaphores = pltpu.SemaphoreType.DMA((copies,))
    space = pl.BlockSpec(memory_space=pltpu.VMEM)
    flops = 2 * rows * 2 * (half * 3 * attn + attn * width + TAPS * 2 * half * half)
    return pl.pallas_call(
        functools.partial(tail_kernel, scale, tm_count),
        out_shape=[
            jax.ShapeDtypeStruct(gh_loc.shape, bf16),
            jax.ShapeDtypeStruct(gh_loc.shape, bf16),
            jax.ShapeDtypeStruct((c_rows, TAPS * width), bf16),
            jax.ShapeDtypeStruct((2, q_rows, 3 * attn), bf16),
            jax.ShapeDtypeStruct((p_rows, width), bf16),
        ],
        in_specs=[space] * 9 + [pl.BlockSpec(memory_space=pl.ANY)],
        out_specs=[space] * 5,
        scratch_shapes=scratch + [semaphores, semaphores, pltpu.SemaphoreType.DMA],
        compiler_params=pltpu.CompilerParams(
            collective_id=0, has_side_effects=True, vmem_limit_bytes=50 * 1024 * 1024
        ),
        cost_estimate=pl.CostEstimate(
            flops=flops, bytes_accessed=200_000_000, transcendentals=0
        ),
    )(gh_loc, *lefts, normed, gqkv, att, cot, conv_weight)


def local(latents, conv_weight, qkv_weight, out_weight, out_cotangent):
    videos, frames, places, width = latents.shape
    half = frames // 2
    attn_width = out_weight.shape[0]
    dp_count = lax.axis_size("dp")
    tm_count = lax.axis_size("tm")
    loc = places // tm_count
    rows = half * places
    core = lax.axis_index("dp") % 2

    def as_rows(values):
        return values.reshape(rows, values.shape[-1])

    def to_locations(values):
        blocks = values.reshape(tm_count, half * loc, width)
        return lax.all_to_all(blocks, "tm", split_axis=0, concat_axis=0, tiled=True).reshape(
            rows, width
        )

    split = latents.reshape(half, 2, tm_count, loc, width)
    rim_input = from_behind(split[half - 1, 1], "tm", 1)
    split = jnp.transpose(split, (1, 2, 0, 3, 4))
    even_frames, odd_frames = split[0], split[1]
    prev_frames = jnp.concatenate([rim_input[:, None], odd_frames[:, : half - 1]], axis=1)
    cotangent_rows = as_rows(
        jnp.transpose(out_cotangent.reshape(half, tm_count, loc, width), (1, 0, 2, 3))
    )
    cot = to_locations(cotangent_rows)

    tap_zero = conv_weight[:, :width]
    tap_one = conv_weight[:, width : 2 * width]
    tap_two = conv_weight[:, 2 * width :]
    taps = [as_rows(prev_frames), as_rows(even_frames), as_rows(odd_frames)]

    def columns_of(which):
        size = width // 2
        return jnp.concatenate(
            [lax.dynamic_slice_in_dim(one, which * size, size, axis=1) for one in taps], axis=1
        )

    mine, others = columns_of(core), columns_of(1 - core)
    lefts = [mine, swap(others, "dp", 1), swap(mine, "dp", 2), swap(others, "dp", 3)]

    hidden = (
        dot_rows(taps[0], tap_zero) + dot_rows(taps[1], tap_one) + dot_rows(taps[2], tap_two)
    ).astype(jnp.bfloat16)
    hidden = to_locations(hidden)
    grad_att = dot_rows_t(cot, out_weight).astype(jnp.bfloat16)
    hidden_f = hidden.astype(jnp.float32)
    centred = hidden_f - jnp.mean(hidden_f, axis=-1, keepdims=True)
    inv_std = lax.rsqrt(jnp.mean(centred * centred, axis=-1, keepdims=True) + EPSILON)
    unit_rows = centred * inv_std
    normed = unit_rows.astype(jnp.bfloat16)
    qkv_rows = dot_rows(normed, qkv_weight).astype(jnp.bfloat16)
    grad_qkv, attended = attention(qkv_rows, grad_att, loc)

    grad_normed = dot_rows_t(grad_qkv, qkv_weight)
    correction = (
        grad_normed
        - jnp.mean(grad_normed, axis=-1, keepdims=True)
        - unit_rows * jnp.mean(grad_normed * unit_rows, axis=-1, keepdims=True)
    )
    grad_hidden = (cot.astype(jnp.float32) + inv_std * correction).astype(jnp.bfloat16)

    grad_scale = 1.0 / math.sqrt(dp_count * tm_count * rows)
    grad_even, grad_odd, conv_grad, qkv_grad, proj_grad = tail(
        grad_hidden.reshape(tm_count, half * loc, width),
        lefts,
        normed,
        grad_qkv,
        attended,
        cot,
        conv_weight,
        loc,
        grad_scale,
    )
    qkv_grad = qkv_grad.reshape(-1, qkv_grad.shape[-1])

    by_frame = (tm_count, half, loc, width)
    input_grad = jnp.transpose(
        jnp.stack([grad_even.reshape(by_frame), grad_odd.reshape(by_frame)], axis=0),
        (2, 0, 1, 3, 4),
    ).reshape(latents.shape)
    return (input_grad, conv_grad, qkv_grad, proj_grad)


def solution(mesh):
    return jax.shard_map(
        local,
        mesh=mesh,
        in_specs=(P("dp", "tm", None, None), P(), P(), P(), P("dp", "tm", None, None)),
        out_specs=(P("dp", "tm", None, None), P("tm", None), P("tm", None), P("tm", None)),
        check_vma=False,
    )
```

```python
import functools
import math

import jax
import jax.numpy as jnp
from jax import lax
from jax.experimental import pallas as pl
from jax.experimental.pallas import tpu as pltpu
from jax.sharding import PartitionSpec as P

HEADS = 10
HEAD = 64
EPSILON = 1e-05
TAPS = 3
VMEM_LIMIT = 62 * 1024 * 1024


def dot_rows(left_side, right_side):
    return jnp.dot(left_side, right_side, preferred_element_type=jnp.float32)


def dot_rows_t(left_side, right_side):
    return lax.dot_general(
        left_side, right_side, (((1,), (1,)), ((), ())), preferred_element_type=jnp.float32
    )


def dot_columns(left_side, right_side):
    return lax.dot_general(
        left_side, right_side, (((0,), (0,)), ((), ())), preferred_element_type=jnp.float32
    )


def flipped(index, mask, size):
    result = 0
    bit = 1
    while bit < size:
        own = index // bit % 2
        result += (1 - own if mask & bit else own) * bit
        bit *= 2
    return result


def attend(loc, width, qkv_ref, g_ref, grad_ref, attended_ref):
    rows = qkv_ref.shape[0]
    row_at = lax.broadcasted_iota(jnp.int32, (rows, rows), 0)
    column_at = lax.broadcasted_iota(jnp.int32, (rows, rows), 1)
    same = (row_at % loc) == (column_at % loc)
    lane = lax.broadcasted_iota(jnp.int32, (rows, 2 * HEAD), 1)
    scale = 1.0 / math.sqrt(HEAD)
    for pair in range(width // (2 * HEAD)):
        first = pair * 2 * HEAD
        q = qkv_ref[:, first : first + 2 * HEAD]
        k = qkv_ref[:, width + first : width + first + 2 * HEAD]
        v = qkv_ref[:, 2 * width + first : 2 * width + first + 2 * HEAD]
        g = g_ref[:, first : first + 2 * HEAD]
        zero = jnp.zeros_like(q)
        grad_q = grad_k = grad_v = attended = None
        kept = []
        for head in range(2):
            mine = (lane >= HEAD) if head else (lane < HEAD)
            q_h = jnp.where(mine, q, zero)
            v_h = jnp.where(mine, v, zero)
            g_h = jnp.where(mine, g, zero)
            scores = jnp.where(same, dot_rows_t(q_h, k) * scale, -1e30)
            expo = jnp.exp(scores - jnp.max(scores, axis=1, keepdims=True))
            probs = expo * (1.0 / jnp.sum(expo, axis=1, keepdims=True))
            probs_b = probs.astype(jnp.bfloat16)
            part = dot_rows(probs_b, v_h)
            attended = part if attended is None else attended + part
            part = dot_columns(probs_b, g_h)
            grad_v = part if grad_v is None else grad_v + part
            grad_probs = dot_rows_t(g_h, v)
            kept.append((mine, q_h, probs, grad_probs))
        attended_b = attended.astype(jnp.bfloat16)
        product = g.astype(jnp.float32) * attended_b.astype(jnp.float32)
        for mine, q_h, probs, grad_probs in kept:
            k_h = jnp.where(mine, k, zero)
            delta = jnp.sum(jnp.where(mine, product, 0.0), axis=1, keepdims=True)
            grad_scores = (probs * (grad_probs - delta) * scale).astype(jnp.bfloat16)
            part = dot_rows(grad_scores, k_h)
            grad_q = part if grad_q is None else grad_q + part
            part = dot_columns(grad_scores, q_h)
            grad_k = part if grad_k is None else grad_k + part
        grad_ref[:, first : first + 2 * HEAD] = grad_q.astype(jnp.bfloat16)
        grad_ref[:, width + first : width + first + 2 * HEAD] = grad_k.astype(jnp.bfloat16)
        grad_ref[:, 2 * width + first : 2 * width + first + 2 * HEAD] = grad_v.astype(
            jnp.bfloat16
        )
        attended_ref[:, first : first + 2 * HEAD] = attended_b


def block_kernel(scale, tm_count, *refs):
    even, odd, cot_rows, rim_rows, weight_hbm, qkv_hbm, out_hbm = refs[:7]
    even_out, odd_out, conv_out, qkv_out, proj_out = refs[7:12]
    weight, qkv_weight, out_weight = refs[12:15]
    odd_rim, swapped, swapped_rim, left, left_rim, hid_own, hid, cot_in = refs[15:23]
    unit, normed, qkv_rows, grad_att, gqkv, att, gh_loc = refs[23:30]
    ghf, ghx, normed_o, gqkv_o, att_o, cot_o, part = refs[30:37]
    share_c, conv_rc, conv_sx, conv_rz, conv_fin = refs[37:42]
    share_q, q_r1, q_s1, q_r2, q_sx, q_rz, q_fin = refs[42:49]
    share_p, p_r1, p_s1, p_r2, p_sx, p_rz, p_fin = refs[49:56]
    rim_out, rim_in = refs[56:58]
    send_sem, recv_sem, load_sem = refs[58:61]
    high = tm_count // 2
    hh = high // 2
    block, width = even.shape[1:]
    rows = tm_count * block
    half = width // 2
    attn = att.shape[1]
    loc = rim_rows.shape[0] // tm_count
    dp, tm = lax.axis_index("dp"), lax.axis_index("tm")
    core, my = dp % 2, dp // 2
    mx, mz = tm % 2, tm // 2
    x_peer = (dp, tm + 1 - 2 * mx)
    y_peer = (dp + 2 - 4 * my, tm)
    diagonal = (dp + 2 - 4 * my, tm + 1 - 2 * mx)
    core_peer = (dp + 1 - 2 * core, tm)
    is_dest = mz // hh == core
    not_dest = mz // hh != core
    peers = [flipped(tm, d, tm_count) for d in range(1, tm_count)]

    loads = []
    for i, tap in enumerate((1, 2, 0)):
        cols = pl.ds(tap * width, width)
        loads.append(
            pltpu.make_async_copy(weight_hbm.at[:, cols], weight.at[:, cols], load_sem.at[i])
        )
    loads.append(pltpu.make_async_copy(out_hbm, out_weight, load_sem.at[3]))
    loads.append(pltpu.make_async_copy(qkv_hbm, qkv_weight, load_sem.at[4]))
    for one in loads:
        one.start()

    barrier = pltpu.get_barrier_semaphore()
    for peer in [y_peer, core_peer, diagonal] + [(dp, t) for t in peers]:
        pl.semaphore_signal(
            barrier, inc=1, device_id=peer, device_id_type=pl.DeviceIdType.MESH
        )
    pl.semaphore_wait(barrier, tm_count + 2)

    count = [0]

    def copy(source, target, peer):
        index = count[0]
        count[0] += 1
        return pltpu.make_async_remote_copy(
            src_ref=source,
            dst_ref=target,
            send_sem=send_sem.at[index],
            recv_sem=recv_sem.at[index],
            device_id=peer,
            device_id_type=pl.DeviceIdType.MESH,
        )

    def start(*copies):
        for one in copies:
            one.start()
        return copies

    sent = []

    def received(copies):
        for one in copies:
            one.wait_recv()
            sent.append(one)

    my_cols = pl.ds(pl.multiple_of(my * half, 128), half)
    other_cols = pl.ds(pl.multiple_of((1 - my) * half, 128), half)
    core_cols = pl.ds(pl.multiple_of(core * half, 128), half)
    peer_core_cols = pl.ds(pl.multiple_of((1 - core) * half, 128), half)

    def add(a, b):
        return (a.astype(jnp.float32) + b.astype(jnp.float32)).astype(jnp.bfloat16)

    odd_next = copy(rim_rows, odd_rim, (dp, (tm + 1) % tm_count))
    pl.when(tm < tm_count - 1)(odd_next.start)
    cot_flights = start(*[copy(cot_rows.at[t], cot_in.at[tm], (dp, t)) for t in peers])
    cot_in[tm] = cot_rows[tm]

    c_rows = share_c.shape[3]

    def of_x(values, x):
        pieces = [
            values[:, (2 * z + x) * c_rows : (2 * z + x + 1) * c_rows] for z in range(high)
        ]
        return jnp.concatenate(pieces, axis=1).astype(jnp.bfloat16)

    for which, frames in enumerate((even, odd)):
        values = frames[...].reshape(rows, width).astype(jnp.float32)
        for x in range(2):
            chosen = of_x(values, x)

            @pl.when(mx == x)
            def _():
                left[0, 1 + which] = chosen

            @pl.when(mx != x)
            def _():
                swapped[which] = chosen

    lefts = []
    for which in range(2):
        lefts.append(copy(left.at[0, 1 + which], left.at[1, 1 + which], y_peer))
    start(*lefts)

    for one in loads[:2]:
        one.wait()
    even_rows = even[...].reshape(rows, width)
    odd_rows = odd[...].reshape(rows, width)
    for tile in range(2):
        cols = slice(tile * half, (tile + 1) * half)
        total = dot_rows(even_rows, weight[:, width + tile * half : width + (tile + 1) * half])
        total += dot_rows(
            odd_rows, weight[:, 2 * width + tile * half : 2 * width + (tile + 1) * half]
        )
        if tile == 0:
            loads[2].wait()
        before = dot_rows(odd_rows, weight[:, cols])
        if tile == 0:
            pl.when(tm < tm_count - 1)(odd_next.wait_send)
            pl.when(tm > 0)(odd_next.wait_recv)

            @pl.when(tm == 0)
            def _():
                odd_rim[...] = jnp.zeros_like(odd_rim)

        rims = dot_rows(odd_rim[...], weight[:, cols]).reshape(tm_count, loc, half)
        before = before.reshape(tm_count, block, half)
        total = total.reshape(tm_count, block, half)
        total += jnp.concatenate([rims, before[:, : block - loc]], axis=1)
        hid_own[:, :, cols] = total.astype(jnp.bfloat16)
    hid_flights = start(*[copy(hid_own.at[t], hid.at[tm], (dp, t)) for t in peers])
    hid[tm] = hid_own[tm]

    values = odd_rim[...].astype(jnp.float32)
    for x in range(2):
        chosen = of_x(values, x)

        @pl.when(mx == x)
        def _():
            left_rim[0] = chosen

        @pl.when(mx != x)
        def _():
            swapped_rim[...] = chosen

    rims = [copy(left_rim.at[0], left_rim.at[1], y_peer)]
    start(*rims)
    for k, peer in ((2, x_peer), (3, diagonal)):
        for which in range(2):
            lefts += start(copy(swapped.at[which], left.at[k, 1 + which], peer))
        rims += start(copy(swapped_rim, left_rim.at[k], peer))

    def previous(k):
        frames = left[k, 2].astype(jnp.float32).reshape(tm_count, block, half)
        edge = left_rim[k].astype(jnp.float32).reshape(tm_count, loc, half)
        frames = jnp.concatenate([edge, frames[:, : block - loc]], axis=1)
        left[k, 0] = frames.reshape(rows, half).astype(jnp.bfloat16)

    previous(0)
    received(cot_flights)
    loads[3].wait()
    cot = cot_in.reshape(rows, width)
    swaps = list(start(copy(cot, cot_o, core_peer)))
    grad_att[...] = dot_rows_t(cot[...], out_weight[...]).astype(jnp.bfloat16)
    loads[4].wait()

    received(hid_flights)
    hidden = hid[...].reshape(rows, width).astype(jnp.float32)
    centred = hidden - jnp.mean(hidden, axis=-1, keepdims=True)
    inv_std = lax.rsqrt(jnp.mean(centred * centred, axis=-1, keepdims=True) + EPSILON)
    unit[...] = centred * inv_std
    normed[...] = unit[...].astype(jnp.bfloat16)
    swaps += start(copy(normed.at[:, peer_core_cols], normed_o, core_peer))
    for tile in range(3):
        cols = slice(tile * attn, (tile + 1) * attn)
        qkv_rows[:, cols] = dot_rows(normed[...], qkv_weight[:, cols]).astype(jnp.bfloat16)
    attend(loc, attn, qkv_rows, grad_att, gqkv, att)
    swaps += start(copy(gqkv, gqkv_o, core_peer), copy(att, att_o, core_peer))
    grad_normed = dot_rows_t(gqkv[...], qkv_weight[...])
    unit_rows = unit[...]
    correction = (
        grad_normed
        - jnp.mean(grad_normed, axis=-1, keepdims=True)
        - unit_rows * jnp.mean(grad_normed * unit_rows, axis=-1, keepdims=True)
    )
    grad_hidden = (cot[...].astype(jnp.float32) + inv_std * correction).astype(jnp.bfloat16)
    gh_loc[...] = grad_hidden.reshape(tm_count, block, width)

    back = [copy(gh_loc.at[t], ghf.at[tm], (dp, t)) for t in peers]
    start(*back)
    ghf[tm] = gh_loc[tm]

    def spread(t):
        return (
            copy(ghf.at[t, :, other_cols], ghx.at[0, t], y_peer),
            copy(ghf.at[t, :, my_cols], ghx.at[1, t], x_peer),
            copy(ghf.at[t, :, other_cols], ghx.at[2, t], diagonal),
        )

    spreads = [start(*spread(tm))]
    received(swaps)

    q_rows = share_q.shape[3]
    for tile in range(3):
        cols = slice(tile * attn, (tile + 1) * attn)
        result = dot_columns(normed[:, core_cols], gqkv[:, cols]) + dot_columns(
            normed_o[...], gqkv_o[:, cols]
        )
        for i in range(4 * hh):
            share_q[i // 4, i // 2 % 2, i % 2, :, cols] = result[
                i * q_rows : (i + 1) * q_rows
            ].astype(jnp.bfloat16)

    def sums(share, first, total, second, result):
        steps = []
        for z in range(hh):
            if z < hh // 2:
                away, peer, stay = share.at[z, :, 1 - my], y_peer, share.at[z, :, my]
                away_2, peer_2, stay_2 = 1 - mx, x_peer, mx
            else:
                away, peer, stay = share.at[z, 1 - mx], x_peer, share.at[z, mx]
                away_2, peer_2, stay_2 = 1 - my, y_peer, my
            one = copy(away, first.at[z], peer)
            two = copy(total.at[z, away_2], second.at[z], peer_2)
            steps.append((one, stay, first.at[z], total.at[z], two, stay_2, second.at[z], result.at[z]))
        return steps

    q_steps = sums(share_q, q_r1, q_s1, q_r2, q_sx)
    p_rows = share_p.shape[3]
    step = attn // 2 // 128 * 128
    window = pl.ds(pl.multiple_of(core * step, 128), attn - step)
    for tile in range(2):
        cols = slice(tile * half, (tile + 1) * half)
        part[...] = dot_columns(att[:, window], cot[:, cols]) + dot_columns(
            att_o[:, window], cot_o[:, cols]
        )
        offset = pl.multiple_of(core * (attn // 2 - step), 8)
        result = part[pl.ds(offset, attn // 2), :]
        for i in range(2 * hh):
            share_p[i // 2, i % 2, tile] = result[i * p_rows : (i + 1) * p_rows].astype(
                jnp.bfloat16
            )
    p_steps = sums(share_p, p_r1, p_s1, p_r2, p_sx)

    for one, t in zip(back, peers):
        received([one])
        spreads.append(start(*spread(t)))
    start(*[one[0] for one in q_steps + p_steps])
    rim_out[...] = (
        ghf[...].astype(jnp.float32)[:, :loc].reshape(tm_count * loc, width).astype(jnp.bfloat16)
    )
    rim = copy(rim_out, rim_in, (dp, (tm + tm_count - 1) % tm_count))
    pl.when(tm > 0)(rim.start)

    received(lefts + rims)
    for k in range(1, 4):
        previous(k)
    received([one for flights in spreads for one in flights])

    conv_c = []
    for tap in range(TAPS):
        result = dot_columns(left[0, tap], ghf[:, :, my_cols].reshape(rows, half))
        for k in range(1, 4):
            result += dot_columns(left[k, tap], ghx[k - 1].reshape(rows, half))
        for z in range(high):
            share_c[tap, z // hh, z % hh] = result[z * c_rows : (z + 1) * c_rows].astype(
                jnp.bfloat16
            )
        conv_c += start(copy(share_c.at[tap, 1 - core], conv_rc.at[tap], core_peer))

    def z_copies(total, came):
        copies = []
        for d in range(1, high):
            target = (mz + d) % high
            copies.append(
                (
                    target // hh == core,
                    copy(total.at[target % hh], came.at[d - 1], (dp, target * 2 + mx)),
                )
            )
        return copies

    def z_start(copies):
        for chosen, one in copies:
            pl.when(chosen)(one.start)

    z_sent = []

    def z_receive(copies, stay, came, place):
        z_sent.extend(copies)

        @pl.when(is_dest)
        def _():
            for _, one in copies:
                one.wait_recv()
            total = stay[mz % hh].astype(jnp.float32)
            for d in range(1, high):
                total += came[d - 1].astype(jnp.float32)
            place[...] = (total * scale).astype(jnp.bfloat16)

    def conv_sum(tap):
        received([conv_c[tap]])
        conv_sx[tap] = add(share_c[tap, core], conv_rc[tap])
        copies = z_copies(conv_sx.at[tap], conv_rz.at[tap])
        z_start(copies)
        return copies

    conv_z = [conv_sum(tap) for tap in range(TAPS)]
    for one, stay, came, total, two, _, _, _ in q_steps + p_steps:
        received([one])
        total[...] = add(stay[...], came[...])
        start(two)

    pl.when(tm > 0)(rim.wait_send)
    pl.when(tm < tm_count - 1)(rim.wait_recv)

    @pl.when(tm == tm_count - 1)
    def _():
        rim_in[...] = jnp.zeros_like(rim_in)

    gh_rows = ghf[...].reshape(rows, width)

    def even_part(tile):
        part_of = slice(tile * half, (tile + 1) * half)
        grad = dot_rows_t(gh_rows, weight[part_of, width : 2 * width])
        even_out[:, :, part_of] = grad.astype(jnp.bfloat16).reshape(tm_count, block, half)

    def odd_part(tile):
        part_of = slice(tile * half, (tile + 1) * half)
        before = dot_rows_t(gh_rows, weight[part_of, :width]).reshape(tm_count, block, half)
        rims = dot_rows_t(rim_in[...], weight[part_of, :width]).reshape(tm_count, loc, half)
        grad = dot_rows_t(gh_rows, weight[part_of, 2 * width :]).reshape(tm_count, block, half)
        grad += jnp.concatenate([before[:, loc:], rims], axis=1)
        odd_out[:, :, part_of] = grad.astype(jnp.bfloat16)

    even_part(0)
    even_part(1)
    for _, _, _, total, two, stay, came, result in q_steps + p_steps:
        received([two])
        result[...] = add(total[stay], came[...])
    p_z = z_copies(p_sx, p_rz)
    z_start(p_z)
    q_z = z_copies(q_sx, q_rz)
    z_start(q_z)

    odd_part(0)
    odd_part(1)
    last = []

    def gather(copies, stay, came, fin):
        z_receive(copies, stay, came, fin.at[my])
        to_y = copy(fin.at[my], fin.at[my], y_peer)
        own_to_core = copy(fin.at[my], fin.at[my], core_peer)
        other_to_core = copy(fin.at[1 - my], fin.at[1 - my], core_peer)
        last.append((to_y, own_to_core, other_to_core))

        @pl.when(is_dest)
        def _():
            to_y.start()
            own_to_core.start()

    for tap in range(TAPS):
        gather(conv_z[tap], conv_sx.at[tap], conv_rz.at[tap], conv_fin.at[tap])
    gather(p_z, p_sx, p_rz, p_fin)
    gather(q_z, q_sx, q_rz, q_fin)

    for to_y, own_to_core, other_to_core in last:

        @pl.when(is_dest)
        def _():
            to_y.wait_recv()
            other_to_core.start()

        @pl.when(not_dest)
        def _():
            own_to_core.wait_recv()
            other_to_core.wait_recv()

    for tap in range(TAPS):
        for y in range(2):
            conv_out[:, tap * width + y * half : tap * width + (y + 1) * half] = conv_fin[tap, y]
    for y in range(2):
        proj_out[:, y * half : (y + 1) * half] = p_fin[y]
    qkv_out[...] = q_fin[...]

    for one in sent:
        one.wait_send()
    for chosen, one in z_sent:
        pl.when(chosen)(one.wait_send)

    @pl.when(is_dest)
    def _():
        for copies in last:
            for one in copies:
                one.wait_send()


def block(even, odd, cot, rim, conv_weight, qkv_weight, out_weight, scale):
    tm_count, block_rows, width = even.shape
    high = tm_count // 2
    hh = high // 2
    half = width // 2
    rows = tm_count * block_rows
    attn = out_weight.shape[0]
    c_rows = width // tm_count
    q_rows = c_rows // 2
    p_rows = attn // tm_count
    edge = rim.shape[0]
    bf16 = jnp.bfloat16

    def vmem(*shape, dtype=bf16):
        return pltpu.VMEM(shape, dtype)

    scratch = [
        vmem(*conv_weight.shape),
        vmem(*qkv_weight.shape),
        vmem(*out_weight.shape),
        vmem(edge, width),
        vmem(2, rows, half),
        vmem(edge, half),
        vmem(4, TAPS, rows, half),
        vmem(4, edge, half),
        vmem(*even.shape),
        vmem(*even.shape),
        vmem(*even.shape),
        vmem(rows, width, dtype=jnp.float32),
        vmem(rows, width),
        vmem(rows, 3 * attn),
        vmem(rows, attn),
        vmem(rows, 3 * attn),
        vmem(rows, attn),
        vmem(*even.shape),
        vmem(*even.shape),
        vmem(3, tm_count, block_rows, half),
        vmem(rows, half),
        vmem(rows, 3 * attn),
        vmem(rows, attn),
        vmem(rows, width),
        vmem(attn - attn // 2 // 128 * 128, half, dtype=jnp.float32),
        vmem(TAPS, 2, hh, c_rows, half),
        vmem(TAPS, hh, c_rows, half),
        vmem(TAPS, hh, c_rows, half),
        vmem(TAPS, high - 1, c_rows, half),
        vmem(TAPS, 2, c_rows, half),
        vmem(hh, 2, 2, q_rows, 3 * attn),
        vmem(hh, 2, q_rows, 3 * attn),
        vmem(hh, 2, q_rows, 3 * attn),
        vmem(hh, q_rows, 3 * attn),
        vmem(hh, q_rows, 3 * attn),
        vmem(high - 1, q_rows, 3 * attn),
        vmem(2, q_rows, 3 * attn),
        vmem(hh, 2, 2, p_rows, half),
        vmem(hh, 2, p_rows, half),
        vmem(hh, 2, p_rows, half),
        vmem(hh, p_rows, half),
        vmem(hh, p_rows, half),
        vmem(high - 1, p_rows, half),
        vmem(2, p_rows, half),
        vmem(edge, width),
        vmem(edge, width),
    ]
    copies = 2 + 3 * (tm_count - 1) + 9 + 4 + 3 * tm_count + TAPS + 4 * hh + 5 * (high - 1) + 15
    semaphores = pltpu.SemaphoreType.DMA((copies,))
    space = pl.BlockSpec(memory_space=pltpu.VMEM)
    return pl.pallas_call(
        functools.partial(block_kernel, scale, tm_count),
        out_shape=[
            jax.ShapeDtypeStruct(even.shape, bf16),
            jax.ShapeDtypeStruct(even.shape, bf16),
            jax.ShapeDtypeStruct((c_rows, TAPS * width), bf16),
            jax.ShapeDtypeStruct((2, q_rows, 3 * attn), bf16),
            jax.ShapeDtypeStruct((p_rows, width), bf16),
        ],
        in_specs=[space] * 4 + [pl.BlockSpec(memory_space=pl.ANY)] * 3,
        out_specs=[space] * 5,
        scratch_shapes=scratch + [semaphores, semaphores, pltpu.SemaphoreType.DMA((5,))],
        compiler_params=pltpu.CompilerParams(
            collective_id=0, has_side_effects=True, vmem_limit_bytes=VMEM_LIMIT
        ),
        cost_estimate=pl.CostEstimate(
            flops=12_000_000_000, bytes_accessed=200_000_000, transcendentals=0
        ),
    )(even, odd, cot, rim, conv_weight, qkv_weight, out_weight)


def local(latents, conv_weight, qkv_weight, out_weight, out_cotangent):
    videos, frames, places, width = latents.shape
    half = frames // 2
    dp_count = lax.axis_size("dp")
    tm_count = lax.axis_size("tm")
    loc = places // tm_count
    rows = half * places

    split = latents.reshape(half, 2, tm_count, loc, width)
    rim = split[half - 1, 1].reshape(places, width)
    split = jnp.transpose(split, (1, 2, 0, 3, 4)).reshape(2, tm_count, half * loc, width)
    cotangent = jnp.transpose(out_cotangent.reshape(half, tm_count, loc, width), (1, 0, 2, 3))
    grad_scale = 1.0 / math.sqrt(dp_count * tm_count * rows)
    grad_even, grad_odd, conv_grad, qkv_grad, proj_grad = block(
        split[0],
        split[1],
        cotangent.reshape(tm_count, half * loc, width),
        rim,
        conv_weight,
        qkv_weight,
        out_weight,
        grad_scale,
    )
    qkv_grad = qkv_grad.reshape(-1, qkv_grad.shape[-1])
    by_frame = (tm_count, half, loc, width)
    input_grad = jnp.transpose(
        jnp.stack([grad_even.reshape(by_frame), grad_odd.reshape(by_frame)], axis=0),
        (2, 0, 1, 3, 4),
    ).reshape(latents.shape)
    return (input_grad, conv_grad, qkv_grad, proj_grad)


def solution(mesh):
    return jax.shard_map(
        local,
        mesh=mesh,
        in_specs=(P("dp", "tm", None, None), P(), P(), P(), P("dp", "tm", None, None)),
        out_specs=(P("dp", "tm", None, None), P("tm", None), P("tm", None), P("tm", None)),
        check_vma=False,
    )
```

```python
import functools
import math

import jax
import jax.numpy as jnp
from jax import lax
from jax.experimental import pallas as pl
from jax.experimental.pallas import tpu as pltpu
from jax.sharding import PartitionSpec as P

HEADS = 10
HEAD = 64
EPSILON = 1e-05
TAPS = 3
VMEM_LIMIT = 62 * 1024 * 1024


def dot_rows(left_side, right_side):
    return jnp.dot(left_side, right_side, preferred_element_type=jnp.float32)


def dot_rows_t(left_side, right_side):
    return lax.dot_general(
        left_side, right_side, (((1,), (1,)), ((), ())), preferred_element_type=jnp.float32
    )


def dot_columns(left_side, right_side):
    return lax.dot_general(
        left_side, right_side, (((0,), (0,)), ((), ())), preferred_element_type=jnp.float32
    )


def flipped(index, mask, size):
    result = 0
    bit = 1
    while bit < size:
        own = index // bit % 2
        result += (1 - own if mask & bit else own) * bit
        bit *= 2
    return result


def attend(loc, width, qkv_ref, g_ref, grad_ref, attended_ref):
    rows = qkv_ref.shape[0]
    row_at = lax.broadcasted_iota(jnp.int32, (rows, rows), 0)
    column_at = lax.broadcasted_iota(jnp.int32, (rows, rows), 1)
    same = (row_at % loc) == (column_at % loc)
    lane = lax.broadcasted_iota(jnp.int32, (rows, 2 * HEAD), 1)
    scale = 1.0 / math.sqrt(HEAD)
    for pair in range(width // (2 * HEAD)):
        first = pair * 2 * HEAD
        q = qkv_ref[:, first : first + 2 * HEAD]
        k = qkv_ref[:, width + first : width + first + 2 * HEAD]
        v = qkv_ref[:, 2 * width + first : 2 * width + first + 2 * HEAD]
        g = g_ref[:, first : first + 2 * HEAD]
        zero = jnp.zeros_like(q)
        grad_q = grad_k = grad_v = attended = None
        kept = []
        for head in range(2):
            mine = (lane >= HEAD) if head else (lane < HEAD)
            q_h = jnp.where(mine, q, zero)
            v_h = jnp.where(mine, v, zero)
            g_h = jnp.where(mine, g, zero)
            scores = jnp.where(same, dot_rows_t(q_h, k) * scale, -1e30)
            expo = jnp.exp(scores - jnp.max(scores, axis=1, keepdims=True))
            probs = expo * (1.0 / jnp.sum(expo, axis=1, keepdims=True))
            probs_b = probs.astype(jnp.bfloat16)
            part = dot_rows(probs_b, v_h)
            attended = part if attended is None else attended + part
            part = dot_columns(probs_b, g_h)
            grad_v = part if grad_v is None else grad_v + part
            grad_probs = dot_rows_t(g_h, v)
            kept.append((mine, q_h, probs, grad_probs))
        attended_b = attended.astype(jnp.bfloat16)
        product = g.astype(jnp.float32) * attended_b.astype(jnp.float32)
        for mine, q_h, probs, grad_probs in kept:
            k_h = jnp.where(mine, k, zero)
            delta = jnp.sum(jnp.where(mine, product, 0.0), axis=1, keepdims=True)
            grad_scores = (probs * (grad_probs - delta) * scale).astype(jnp.bfloat16)
            part = dot_rows(grad_scores, k_h)
            grad_q = part if grad_q is None else grad_q + part
            part = dot_columns(grad_scores, q_h)
            grad_k = part if grad_k is None else grad_k + part
        grad_ref[:, first : first + 2 * HEAD] = grad_q.astype(jnp.bfloat16)
        grad_ref[:, width + first : width + first + 2 * HEAD] = grad_k.astype(jnp.bfloat16)
        grad_ref[:, 2 * width + first : 2 * width + first + 2 * HEAD] = grad_v.astype(
            jnp.bfloat16
        )
        attended_ref[:, first : first + 2 * HEAD] = attended_b


def block_kernel(scale, tm_count, *refs):
    frames, cot_rows, weight_hbm, qkv_hbm, out_hbm = refs[:5]
    frames_out, conv_out, qkv_out, proj_out = refs[5:9]
    weight, qkv_weight, out_weight = refs[9:12]
    rim_rows, odd_rim, swapped, swapped_rim, left, left_rim, hid_own, hid, cot_in = refs[12:21]
    unit, normed, qkv_rows, grad_att, gqkv, att, gh_loc = refs[21:28]
    ghf, ghx, normed_o, gqkv_o, att_o, cot_o, part = refs[28:35]
    share_c, conv_rc, conv_sx, conv_rz, conv_fin = refs[35:40]
    share_q, q_r1, q_s1, q_r2, q_sx, q_rz, q_fin = refs[40:47]
    share_p, p_r1, p_s1, p_r2, p_sx, p_rz, p_fin = refs[47:54]
    rim_out, rim_in = refs[54:56]
    send_sem, recv_sem, load_sem = refs[56:59]
    high = tm_count // 2
    hh = high // 2
    block, width = cot_rows.shape[1:]
    even, odd = frames.at[0], frames.at[1]
    rows = tm_count * block
    half = width // 2
    attn = att.shape[1]
    loc = rim_in.shape[0] // tm_count
    dp, tm = lax.axis_index("dp"), lax.axis_index("tm")
    core, my = dp % 2, dp // 2
    mx, mz = tm % 2, tm // 2
    x_peer = (dp, tm + 1 - 2 * mx)
    y_peer = (dp + 2 - 4 * my, tm)
    diagonal = (dp + 2 - 4 * my, tm + 1 - 2 * mx)
    core_peer = (dp + 1 - 2 * core, tm)
    is_dest = mz // hh == core
    not_dest = mz // hh != core
    peers = [flipped(tm, d, tm_count) for d in range(1, tm_count)]

    loads = []
    for i, tap in enumerate((1, 2, 0)):
        cols = pl.ds(tap * width, width)
        loads.append(
            pltpu.make_async_copy(weight_hbm.at[:, cols], weight.at[:, cols], load_sem.at[i])
        )
    loads.append(pltpu.make_async_copy(out_hbm, out_weight, load_sem.at[3]))
    loads.append(pltpu.make_async_copy(qkv_hbm, qkv_weight, load_sem.at[4]))
    for one in loads:
        one.start()

    barrier = pltpu.get_barrier_semaphore()
    for peer in [y_peer, core_peer, diagonal] + [(dp, t) for t in peers]:
        pl.semaphore_signal(
            barrier, inc=1, device_id=peer, device_id_type=pl.DeviceIdType.MESH
        )
    pl.semaphore_wait(barrier, tm_count + 2)

    count = [0]

    def copy(source, target, peer):
        index = count[0]
        count[0] += 1
        return pltpu.make_async_remote_copy(
            src_ref=source,
            dst_ref=target,
            send_sem=send_sem.at[index],
            recv_sem=recv_sem.at[index],
            device_id=peer,
            device_id_type=pl.DeviceIdType.MESH,
        )

    def start(*copies):
        for one in copies:
            one.start()
        return copies

    sent = []

    def received(copies):
        for one in copies:
            one.wait_recv()
            sent.append(one)

    my_cols = pl.ds(pl.multiple_of(my * half, 128), half)
    other_cols = pl.ds(pl.multiple_of((1 - my) * half, 128), half)
    core_cols = pl.ds(pl.multiple_of(core * half, 128), half)
    peer_core_cols = pl.ds(pl.multiple_of((1 - core) * half, 128), half)

    def add(a, b):
        return (a.astype(jnp.float32) + b.astype(jnp.float32)).astype(jnp.bfloat16)

    last_rows = odd[...].astype(jnp.float32)[:, block - loc :]
    rim_rows[...] = last_rows.reshape(tm_count * loc, width).astype(jnp.bfloat16)
    odd_next = copy(rim_rows, odd_rim, (dp, (tm + 1) % tm_count))
    pl.when(tm < tm_count - 1)(odd_next.start)
    cot_flights = start(*[copy(cot_rows.at[t], cot_in.at[tm], (dp, t)) for t in peers])
    cot_in[tm] = cot_rows[tm]

    c_rows = share_c.shape[3]

    def of_x(values, x):
        pieces = [
            values[:, (2 * z + x) * c_rows : (2 * z + x + 1) * c_rows] for z in range(high)
        ]
        return jnp.concatenate(pieces, axis=1).astype(jnp.bfloat16)

    for which in range(2):
        values = frames[which].reshape(rows, width).astype(jnp.float32)
        for x in range(2):
            chosen = of_x(values, x)

            @pl.when(mx == x)
            def _():
                left[0, 1 + which] = chosen

            @pl.when(mx != x)
            def _():
                swapped[which] = chosen

    lefts = []
    for which in range(2):
        lefts.append(copy(left.at[0, 1 + which], left.at[1, 1 + which], y_peer))
    start(*lefts)

    for one in loads[:2]:
        one.wait()
    even_rows = even[...].reshape(rows, width)
    odd_rows = odd[...].reshape(rows, width)
    for tile in range(2):
        cols = slice(tile * half, (tile + 1) * half)
        total = dot_rows(even_rows, weight[:, width + tile * half : width + (tile + 1) * half])
        total += dot_rows(
            odd_rows, weight[:, 2 * width + tile * half : 2 * width + (tile + 1) * half]
        )
        if tile == 0:
            loads[2].wait()
        before = dot_rows(odd_rows, weight[:, cols])
        if tile == 0:
            pl.when(tm < tm_count - 1)(odd_next.wait_send)
            pl.when(tm > 0)(odd_next.wait_recv)

            @pl.when(tm == 0)
            def _():
                odd_rim[...] = jnp.zeros_like(odd_rim)

        rims = dot_rows(odd_rim[...], weight[:, cols]).reshape(tm_count, loc, half)
        before = before.reshape(tm_count, block, half)
        total = total.reshape(tm_count, block, half)
        total += jnp.concatenate([rims, before[:, : block - loc]], axis=1)
        hid_own[:, :, cols] = total.astype(jnp.bfloat16)
    hid_flights = start(*[copy(hid_own.at[t], hid.at[tm], (dp, t)) for t in peers])
    hid[tm] = hid_own[tm]

    values = odd_rim[...].astype(jnp.float32)
    for x in range(2):
        chosen = of_x(values, x)

        @pl.when(mx == x)
        def _():
            left_rim[0] = chosen

        @pl.when(mx != x)
        def _():
            swapped_rim[...] = chosen

    rims = [copy(left_rim.at[0], left_rim.at[1], y_peer)]
    start(*rims)
    for k, peer in ((2, x_peer), (3, diagonal)):
        for which in range(2):
            lefts += start(copy(swapped.at[which], left.at[k, 1 + which], peer))
        rims += start(copy(swapped_rim, left_rim.at[k], peer))

    def previous(k):
        later = left[k, 2].astype(jnp.float32).reshape(tm_count, block, half)
        edge = left_rim[k].astype(jnp.float32).reshape(tm_count, loc, half)
        later = jnp.concatenate([edge, later[:, : block - loc]], axis=1)
        left[k, 0] = later.reshape(rows, half).astype(jnp.bfloat16)

    previous(0)
    received(cot_flights)
    loads[3].wait()
    cot = cot_in.reshape(rows, width)
    swaps = list(start(copy(cot, cot_o, core_peer)))
    grad_att[...] = dot_rows_t(cot[...], out_weight[...]).astype(jnp.bfloat16)
    loads[4].wait()

    received(hid_flights)
    hidden = hid[...].reshape(rows, width).astype(jnp.float32)
    centred = hidden - jnp.mean(hidden, axis=-1, keepdims=True)
    inv_std = lax.rsqrt(jnp.mean(centred * centred, axis=-1, keepdims=True) + EPSILON)
    unit[...] = centred * inv_std
    normed[...] = unit[...].astype(jnp.bfloat16)
    swaps += start(copy(normed.at[:, peer_core_cols], normed_o, core_peer))
    for tile in range(3):
        cols = slice(tile * attn, (tile + 1) * attn)
        qkv_rows[:, cols] = dot_rows(normed[...], qkv_weight[:, cols]).astype(jnp.bfloat16)
    attend(loc, attn, qkv_rows, grad_att, gqkv, att)
    swaps += start(copy(gqkv, gqkv_o, core_peer), copy(att, att_o, core_peer))
    grad_normed = dot_rows_t(gqkv[...], qkv_weight[...])
    unit_rows = unit[...]
    correction = (
        grad_normed
        - jnp.mean(grad_normed, axis=-1, keepdims=True)
        - unit_rows * jnp.mean(grad_normed * unit_rows, axis=-1, keepdims=True)
    )
    grad_hidden = (cot[...].astype(jnp.float32) + inv_std * correction).astype(jnp.bfloat16)
    gh_loc[...] = grad_hidden.reshape(tm_count, block, width)

    back = [copy(gh_loc.at[t], ghf.at[tm], (dp, t)) for t in peers]
    start(*back)
    ghf[tm] = gh_loc[tm]

    def spread(t):
        return (
            copy(ghf.at[t, :, other_cols], ghx.at[0, t], y_peer),
            copy(ghf.at[t, :, my_cols], ghx.at[1, t], x_peer),
            copy(ghf.at[t, :, other_cols], ghx.at[2, t], diagonal),
        )

    spreads = [start(*spread(tm))]
    received(swaps)

    q_rows = share_q.shape[3]
    for tile in range(3):
        cols = slice(tile * attn, (tile + 1) * attn)
        result = dot_columns(normed[:, core_cols], gqkv[:, cols]) + dot_columns(
            normed_o[...], gqkv_o[:, cols]
        )
        for i in range(4 * hh):
            share_q[i // 4, i // 2 % 2, i % 2, :, cols] = result[
                i * q_rows : (i + 1) * q_rows
            ].astype(jnp.bfloat16)

    def sums(share, first, total, second, result):
        steps = []
        for z in range(hh):
            if z < hh // 2:
                away, peer, stay = share.at[z, :, 1 - my], y_peer, share.at[z, :, my]
                away_2, peer_2, stay_2 = 1 - mx, x_peer, mx
            else:
                away, peer, stay = share.at[z, 1 - mx], x_peer, share.at[z, mx]
                away_2, peer_2, stay_2 = 1 - my, y_peer, my
            one = copy(away, first.at[z], peer)
            two = copy(total.at[z, away_2], second.at[z], peer_2)
            steps.append((one, stay, first.at[z], total.at[z], two, stay_2, second.at[z], result.at[z]))
        return steps

    q_steps = sums(share_q, q_r1, q_s1, q_r2, q_sx)
    start(*[one[0] for one in q_steps])
    p_rows = share_p.shape[3]
    step = attn // 2 // 128 * 128
    window = pl.ds(pl.multiple_of(core * step, 128), attn - step)
    for tile in range(2):
        cols = slice(tile * half, (tile + 1) * half)
        part[...] = dot_columns(att[:, window], cot[:, cols]) + dot_columns(
            att_o[:, window], cot_o[:, cols]
        )
        offset = pl.multiple_of(core * (attn // 2 - step), 8)
        result = part[pl.ds(offset, attn // 2), :]
        for i in range(2 * hh):
            share_p[i // 2, i % 2, tile] = result[i * p_rows : (i + 1) * p_rows].astype(
                jnp.bfloat16
            )
    p_steps = sums(share_p, p_r1, p_s1, p_r2, p_sx)
    start(*[one[0] for one in p_steps])

    for one, t in zip(back, peers):
        received([one])
        spreads.append(start(*spread(t)))
    rim_out[...] = (
        ghf[...].astype(jnp.float32)[:, :loc].reshape(tm_count * loc, width).astype(jnp.bfloat16)
    )
    rim = copy(rim_out, rim_in, (dp, (tm + tm_count - 1) % tm_count))
    pl.when(tm > 0)(rim.start)

    received(lefts + rims)
    for k in range(1, 4):
        previous(k)
    received([one for flights in spreads for one in flights])

    conv_c = []
    for tap in range(TAPS):
        result = dot_columns(left[0, tap], ghf[:, :, my_cols].reshape(rows, half))
        for k in range(1, 4):
            result += dot_columns(left[k, tap], ghx[k - 1].reshape(rows, half))
        for z in range(high):
            share_c[tap, z // hh, z % hh] = result[z * c_rows : (z + 1) * c_rows].astype(
                jnp.bfloat16
            )
        conv_c += start(copy(share_c.at[tap, 1 - core], conv_rc.at[tap], core_peer))

    above = (dp, (mz + 1) % high * 2 + mx)
    below = (dp, (mz + high - 1) % high * 2 + mx)
    chains = []

    def chain(total, came):
        links = []
        for z in range(hh):
            up = copy(total.at[z], came.at[0, z], above)
            down = copy(total.at[z], came.at[1, z], below)
            links.append((core * hh + z, up, down))

            @pl.when((mz == 0) & (core * hh + z > mz))
            def _():
                up.start()

            @pl.when((mz == high - 1) & (core * hh + z < mz))
            def _():
                down.start()

        chains.append(links)
        return links, total, came

    def chain_on(links, total, came):
        for z, (owner, up, down) in enumerate(links):
            for inner, one, side in (
                ((mz > 0) & (owner > mz), up, 0),
                ((mz < high - 1) & (owner < mz), down, 1),
            ):

                @pl.when(inner)
                def _():
                    one.wait_recv()
                    total[z] = add(total[z], came[side, z])
                    one.start()

    def chain_end(links, total, came, place):
        for z, (owner, up, down) in enumerate(links):
            @pl.when((owner == mz) & (mz > 0))
            def _():
                up.wait_recv()
                total[z] = add(total[z], came[0, z])

            @pl.when((owner == mz) & (mz < high - 1))
            def _():
                down.wait_recv()
                total[z] = add(total[z], came[1, z])

            @pl.when(owner == mz)
            def _():
                place[...] = (total[z].astype(jnp.float32) * scale).astype(jnp.bfloat16)

    def conv_sum(tap):
        received([conv_c[tap]])
        conv_sx[tap] = add(share_c[tap, core], conv_rc[tap])
        return chain(conv_sx.at[tap], conv_rz.at[tap])

    conv_z = [conv_sum(0), conv_sum(1)]
    chain_on(*conv_z[0])
    conv_z.append(conv_sum(2))
    for one, stay, came, total, two, _, _, _ in q_steps + p_steps:
        received([one])
        total[...] = add(stay[...], came[...])
        start(two)
    chain_on(*conv_z[1])
    chain_on(*conv_z[2])

    pl.when(tm > 0)(rim.wait_send)
    pl.when(tm < tm_count - 1)(rim.wait_recv)

    @pl.when(tm == tm_count - 1)
    def _():
        rim_in[...] = jnp.zeros_like(rim_in)

    gh_rows = ghf[...].reshape(rows, width)

    def even_part(tile):
        part_of = slice(tile * half, (tile + 1) * half)
        grad = dot_rows_t(gh_rows, weight[part_of, width : 2 * width])
        frames_out[0, :, :, part_of] = grad.astype(jnp.bfloat16).reshape(tm_count, block, half)

    def odd_part(tile):
        part_of = slice(tile * half, (tile + 1) * half)
        before = dot_rows_t(gh_rows, weight[part_of, :width]).reshape(tm_count, block, half)
        rims = dot_rows_t(rim_in[...], weight[part_of, :width]).reshape(tm_count, loc, half)
        grad = dot_rows_t(gh_rows, weight[part_of, 2 * width :]).reshape(tm_count, block, half)
        grad += jnp.concatenate([before[:, loc:], rims], axis=1)
        frames_out[1, :, :, part_of] = grad.astype(jnp.bfloat16)

    even_part(0)
    even_part(1)
    last = []

    def gather(links, total, came, fin):
        chain_end(links, total, came, fin.at[my])
        to_y = copy(fin.at[my], fin.at[my], y_peer)
        own_to_core = copy(fin.at[my], fin.at[my], core_peer)
        other_to_core = copy(fin.at[1 - my], fin.at[1 - my], core_peer)
        last.append((to_y, own_to_core, other_to_core))

        @pl.when(is_dest)
        def _():
            to_y.start()
            own_to_core.start()

    sums_z = []
    for steps, totals, came_z in ((p_steps, p_sx, p_rz), (q_steps, q_sx, q_rz)):
        for _, _, _, total, two, stay, came, result in steps:
            received([two])
            result[...] = add(total[stay], came[...])
        sums_z.append(chain(totals, came_z))
    for tap in range(TAPS):
        gather(*conv_z[tap], conv_fin.at[tap])
    for one in sums_z:
        chain_on(*one)
    odd_part(0)
    odd_part(1)
    gather(*sums_z[0], p_fin)
    gather(*sums_z[1], q_fin)

    for to_y, own_to_core, other_to_core in last:

        @pl.when(is_dest)
        def _():
            to_y.wait_recv()
            other_to_core.start()

        @pl.when(not_dest)
        def _():
            own_to_core.wait_recv()
            other_to_core.wait_recv()

    for tap in range(TAPS):
        for y in range(2):
            conv_out[:, tap * width + y * half : tap * width + (y + 1) * half] = conv_fin[tap, y]
    for y in range(2):
        proj_out[:, y * half : (y + 1) * half] = p_fin[y]
    qkv_out[...] = q_fin[...]

    for one in sent:
        one.wait_send()
    for links in chains:
        for owner, up, down in links:
            pl.when(owner > mz)(up.wait_send)
            pl.when(owner < mz)(down.wait_send)

    @pl.when(is_dest)
    def _():
        for copies in last:
            for one in copies:
                one.wait_send()


def block(frames, cot, loc, conv_weight, qkv_weight, out_weight, scale):
    tm_count, block_rows, width = cot.shape
    high = tm_count // 2
    hh = high // 2
    half = width // 2
    rows = tm_count * block_rows
    attn = out_weight.shape[0]
    c_rows = width // tm_count
    q_rows = c_rows // 2
    p_rows = attn // tm_count
    edge = tm_count * loc
    bf16 = jnp.bfloat16

    def vmem(*shape, dtype=bf16):
        return pltpu.VMEM(shape, dtype)

    scratch = [
        vmem(*conv_weight.shape),
        vmem(*qkv_weight.shape),
        vmem(*out_weight.shape),
        vmem(edge, width),
        vmem(edge, width),
        vmem(2, rows, half),
        vmem(edge, half),
        vmem(4, TAPS, rows, half),
        vmem(4, edge, half),
        vmem(*cot.shape),
        vmem(*cot.shape),
        vmem(*cot.shape),
        vmem(rows, width, dtype=jnp.float32),
        vmem(rows, width),
        vmem(rows, 3 * attn),
        vmem(rows, attn),
        vmem(rows, 3 * attn),
        vmem(rows, attn),
        vmem(*cot.shape),
        vmem(*cot.shape),
        vmem(3, tm_count, block_rows, half),
        vmem(rows, half),
        vmem(rows, 3 * attn),
        vmem(rows, attn),
        vmem(rows, width),
        vmem(attn - attn // 2 // 128 * 128, half, dtype=jnp.float32),
        vmem(TAPS, 2, hh, c_rows, half),
        vmem(TAPS, hh, c_rows, half),
        vmem(TAPS, hh, c_rows, half),
        vmem(TAPS, 2, hh, c_rows, half),
        vmem(TAPS, 2, c_rows, half),
        vmem(hh, 2, 2, q_rows, 3 * attn),
        vmem(hh, 2, q_rows, 3 * attn),
        vmem(hh, 2, q_rows, 3 * attn),
        vmem(hh, q_rows, 3 * attn),
        vmem(hh, q_rows, 3 * attn),
        vmem(2, hh, q_rows, 3 * attn),
        vmem(2, q_rows, 3 * attn),
        vmem(hh, 2, 2, p_rows, half),
        vmem(hh, 2, p_rows, half),
        vmem(hh, 2, p_rows, half),
        vmem(hh, p_rows, half),
        vmem(hh, p_rows, half),
        vmem(2, hh, p_rows, half),
        vmem(2, p_rows, half),
        vmem(edge, width),
        vmem(edge, width),
    ]
    copies = 2 + 3 * (tm_count - 1) + 9 + 4 + 3 * tm_count + TAPS + 4 * hh + 10 * hh + 15
    semaphores = pltpu.SemaphoreType.DMA((copies,))
    space = pl.BlockSpec(memory_space=pltpu.VMEM)
    return pl.pallas_call(
        functools.partial(block_kernel, scale, tm_count),
        out_shape=[
            jax.ShapeDtypeStruct(frames.shape, bf16),
            jax.ShapeDtypeStruct((c_rows, TAPS * width), bf16),
            jax.ShapeDtypeStruct((2, q_rows, 3 * attn), bf16),
            jax.ShapeDtypeStruct((p_rows, width), bf16),
        ],
        in_specs=[space] * 2 + [pl.BlockSpec(memory_space=pl.ANY)] * 3,
        out_specs=[space] * 4,
        scratch_shapes=scratch + [semaphores, semaphores, pltpu.SemaphoreType.DMA((5,))],
        compiler_params=pltpu.CompilerParams(
            collective_id=0, has_side_effects=True, vmem_limit_bytes=VMEM_LIMIT
        ),
        cost_estimate=pl.CostEstimate(
            flops=12_000_000_000, bytes_accessed=200_000_000, transcendentals=0
        ),
    )(frames, cot, conv_weight, qkv_weight, out_weight)


def local(latents, conv_weight, qkv_weight, out_weight, out_cotangent):
    videos, frames, places, width = latents.shape
    half = frames // 2
    dp_count = lax.axis_size("dp")
    tm_count = lax.axis_size("tm")
    loc = places // tm_count
    rows = half * places

    split = latents.reshape(half, 2, tm_count, loc, width)
    split = jnp.transpose(split, (1, 2, 0, 3, 4)).reshape(2, tm_count, half * loc, width)
    cotangent = jnp.transpose(out_cotangent.reshape(half, tm_count, loc, width), (1, 0, 2, 3))
    grad_scale = 1.0 / math.sqrt(dp_count * tm_count * rows)
    grad_frames, conv_grad, qkv_grad, proj_grad = block(
        split,
        cotangent.reshape(tm_count, half * loc, width),
        loc,
        conv_weight,
        qkv_weight,
        out_weight,
        grad_scale,
    )
    qkv_grad = qkv_grad.reshape(-1, qkv_grad.shape[-1])
    input_grad = jnp.transpose(
        grad_frames.reshape(2, tm_count, half, loc, width), (2, 0, 1, 3, 4)
    ).reshape(latents.shape)
    return (input_grad, conv_grad, qkv_grad, proj_grad)


def solution(mesh):
    return jax.shard_map(
        local,
        mesh=mesh,
        in_specs=(P("dp", "tm", None, None), P(), P(), P(), P("dp", "tm", None, None)),
        out_specs=(P("dp", "tm", None, None), P("tm", None), P("tm", None), P("tm", None)),
        check_vma=False,
    )
```

```python
import functools
import math

import jax
import jax.numpy as jnp
from jax import lax
from jax.experimental import pallas as pl
from jax.experimental.pallas import tpu as pltpu
from jax.sharding import PartitionSpec as P

HEADS = 10
HEAD = 64
EPSILON = 1e-05
TAPS = 3
VMEM_LIMIT = 62 * 1024 * 1024


def dot_rows(left_side, right_side):
    return jnp.dot(left_side, right_side, preferred_element_type=jnp.float32)


def dot_rows_t(left_side, right_side):
    return lax.dot_general(
        left_side, right_side, (((1,), (1,)), ((), ())), preferred_element_type=jnp.float32
    )


def dot_columns(left_side, right_side):
    return lax.dot_general(
        left_side, right_side, (((0,), (0,)), ((), ())), preferred_element_type=jnp.float32
    )


def flipped(index, mask, size):
    result = 0
    bit = 1
    while bit < size:
        own = index // bit % 2
        result += (1 - own if mask & bit else own) * bit
        bit *= 2
    return result


def attend(loc, width, qkv_ref, g_ref, grad_ref, attended_ref):
    rows = qkv_ref.shape[0]
    row_at = lax.broadcasted_iota(jnp.int32, (rows, rows), 0)
    column_at = lax.broadcasted_iota(jnp.int32, (rows, rows), 1)
    same = (row_at % loc) == (column_at % loc)
    lane = lax.broadcasted_iota(jnp.int32, (rows, 2 * HEAD), 1)
    scale = 1.0 / math.sqrt(HEAD)
    for pair in range(width // (2 * HEAD)):
        first = pair * 2 * HEAD
        q = qkv_ref[:, first : first + 2 * HEAD]
        k = qkv_ref[:, width + first : width + first + 2 * HEAD]
        v = qkv_ref[:, 2 * width + first : 2 * width + first + 2 * HEAD]
        g = g_ref[:, first : first + 2 * HEAD]
        zero = jnp.zeros_like(q)
        grad_q = grad_k = grad_v = attended = None
        kept = []
        for head in range(2):
            mine = (lane >= HEAD) if head else (lane < HEAD)
            q_h = jnp.where(mine, q, zero)
            v_h = jnp.where(mine, v, zero)
            g_h = jnp.where(mine, g, zero)
            scores = jnp.where(same, dot_rows_t(q_h, k) * scale, -1e30)
            expo = jnp.exp(scores - jnp.max(scores, axis=1, keepdims=True))
            probs = expo * (1.0 / jnp.sum(expo, axis=1, keepdims=True))
            probs_b = probs.astype(jnp.bfloat16)
            part = dot_rows(probs_b, v_h)
            attended = part if attended is None else attended + part
            part = dot_columns(probs_b, g_h)
            grad_v = part if grad_v is None else grad_v + part
            grad_probs = dot_rows_t(g_h, v)
            kept.append((mine, q_h, probs, grad_probs))
        attended_b = attended.astype(jnp.bfloat16)
        product = g.astype(jnp.float32) * attended_b.astype(jnp.float32)
        for mine, q_h, probs, grad_probs in kept:
            k_h = jnp.where(mine, k, zero)
            delta = jnp.sum(jnp.where(mine, product, 0.0), axis=1, keepdims=True)
            grad_scores = (probs * (grad_probs - delta) * scale).astype(jnp.bfloat16)
            part = dot_rows(grad_scores, k_h)
            grad_q = part if grad_q is None else grad_q + part
            part = dot_columns(grad_scores, q_h)
            grad_k = part if grad_k is None else grad_k + part
        grad_ref[:, first : first + 2 * HEAD] = grad_q.astype(jnp.bfloat16)
        grad_ref[:, width + first : width + first + 2 * HEAD] = grad_k.astype(jnp.bfloat16)
        grad_ref[:, 2 * width + first : 2 * width + first + 2 * HEAD] = grad_v.astype(
            jnp.bfloat16
        )
        attended_ref[:, first : first + 2 * HEAD] = attended_b


def block_kernel(scale, tm_count, *refs):
    frames, cot_rows, weight_hbm, qkv_hbm, out_hbm = refs[:5]
    frames_out, conv_out, qkv_out, proj_out = refs[5:9]
    weight, qkv_weight, out_weight = refs[9:12]
    rim_rows, odd_rim, left, left_rim, hid_own, hid, cot_in = refs[12:19]
    unit, normed, qkv_rows, grad_att, gqkv, att, gh_loc = refs[19:26]
    ghf, ghx, normed_o, gqkv_o, att_o, cot_o, part = refs[26:33]
    share_c, conv_rx, conv_sx, conv_rz, conv_fin = refs[33:38]
    share_q, q_r1, q_s1, q_r2, q_sx, q_rz, q_fin = refs[38:45]
    share_p, p_r1, p_s1, p_r2, p_sx, p_rz, p_fin = refs[45:52]
    rim_out, rim_in = refs[52:54]
    send_sem, recv_sem, load_sem = refs[54:57]
    high = tm_count // 2
    hh = high // 2
    block, width = cot_rows.shape[1:]
    even, odd = frames.at[0], frames.at[1]
    rows = tm_count * block
    half = width // 2
    attn = att.shape[1]
    loc = rim_in.shape[0] // tm_count
    dp, tm = lax.axis_index("dp"), lax.axis_index("tm")
    core, my = dp % 2, dp // 2
    mx, mz = tm % 2, tm // 2
    x_peer = (dp, tm + 1 - 2 * mx)
    y_peer = (dp + 2 - 4 * my, tm)
    diagonal = (dp + 3 - 4 * my - 2 * core, tm)
    core_peer = (dp + 1 - 2 * core, tm)
    is_dest = mz // hh == core
    not_dest = mz // hh != core
    peers = [flipped(tm, d, tm_count) for d in range(1, tm_count)]

    loads = []
    for i, tap in enumerate((1, 2, 0)):
        cols = pl.ds(tap * width, width)
        loads.append(
            pltpu.make_async_copy(weight_hbm.at[:, cols], weight.at[:, cols], load_sem.at[i])
        )
    loads.append(pltpu.make_async_copy(out_hbm, out_weight, load_sem.at[3]))
    loads.append(pltpu.make_async_copy(qkv_hbm, qkv_weight, load_sem.at[4]))
    for one in loads:
        one.start()

    barrier = pltpu.get_barrier_semaphore()
    for peer in [y_peer, core_peer, diagonal] + [(dp, t) for t in peers]:
        pl.semaphore_signal(
            barrier, inc=1, device_id=peer, device_id_type=pl.DeviceIdType.MESH
        )
    pl.semaphore_wait(barrier, tm_count + 2)

    count = [0]

    def copy(source, target, peer):
        index = count[0]
        count[0] += 1
        return pltpu.make_async_remote_copy(
            src_ref=source,
            dst_ref=target,
            send_sem=send_sem.at[index],
            recv_sem=recv_sem.at[index],
            device_id=peer,
            device_id_type=pl.DeviceIdType.MESH,
        )

    def start(*copies):
        for one in copies:
            one.start()
        return copies

    sent = []

    def received(copies):
        for one in copies:
            one.wait_recv()
            sent.append(one)

    my_cols = pl.ds(pl.multiple_of(my * half, 128), half)
    other_cols = pl.ds(pl.multiple_of((1 - my) * half, 128), half)
    core_cols = pl.ds(pl.multiple_of(core * half, 128), half)
    peer_core_cols = pl.ds(pl.multiple_of((1 - core) * half, 128), half)

    def add(a, b):
        return (a.astype(jnp.float32) + b.astype(jnp.float32)).astype(jnp.bfloat16)

    last_rows = odd[...].astype(jnp.float32)[:, block - loc :]
    rim_rows[...] = last_rows.reshape(tm_count * loc, width).astype(jnp.bfloat16)
    odd_next = copy(rim_rows, odd_rim, (dp, (tm + 1) % tm_count))
    pl.when(tm < tm_count - 1)(odd_next.start)
    cot_flights = start(*[copy(cot_rows.at[t], cot_in.at[tm], (dp, t)) for t in peers])
    cot_in[tm] = cot_rows[tm]

    lefts = []
    dp_peers = ((1, core_peer, peer_core_cols), (2, y_peer, core_cols), (3, diagonal, peer_core_cols))
    for which in range(2):
        left[0, 1 + which] = frames[which, :, :, core_cols]
        for k, peer, cols in dp_peers:
            lefts += start(copy(frames.at[which, :, :, cols], left.at[k, 1 + which], peer))

    for one in loads[:2]:
        one.wait()
    even_rows = even[...].reshape(rows, width)
    odd_rows = odd[...].reshape(rows, width)
    for tile in range(2):
        cols = slice(tile * half, (tile + 1) * half)
        total = dot_rows(even_rows, weight[:, width + tile * half : width + (tile + 1) * half])
        total += dot_rows(
            odd_rows, weight[:, 2 * width + tile * half : 2 * width + (tile + 1) * half]
        )
        if tile == 0:
            loads[2].wait()
        before = dot_rows(odd_rows, weight[:, cols])
        if tile == 0:
            pl.when(tm < tm_count - 1)(odd_next.wait_send)
            pl.when(tm > 0)(odd_next.wait_recv)

            @pl.when(tm == 0)
            def _():
                odd_rim[...] = jnp.zeros_like(odd_rim)

        rims = dot_rows(odd_rim[...], weight[:, cols]).reshape(tm_count, loc, half)
        before = before.reshape(tm_count, block, half)
        total = total.reshape(tm_count, block, half)
        total += jnp.concatenate([rims, before[:, : block - loc]], axis=1)
        hid_own[:, :, cols] = total.astype(jnp.bfloat16)
    hid_flights = start(*[copy(hid_own.at[t], hid.at[tm], (dp, t)) for t in peers])
    hid[tm] = hid_own[tm]

    left_rim[0] = odd_rim[:, core_cols]
    rims = []
    for k, peer, cols in dp_peers:
        rims += start(copy(odd_rim.at[:, cols], left_rim.at[k], peer))

    def previous(k):
        later = left[k, 2].astype(jnp.float32)
        edge = left_rim[k].astype(jnp.float32).reshape(tm_count, loc, half)
        later = jnp.concatenate([edge, later[:, : block - loc]], axis=1)
        left[k, 0] = later.astype(jnp.bfloat16)

    previous(0)
    received(cot_flights)
    loads[3].wait()
    cot = cot_in.reshape(rows, width)
    swaps = list(start(copy(cot, cot_o, core_peer)))
    grad_att[...] = dot_rows_t(cot[...], out_weight[...]).astype(jnp.bfloat16)
    loads[4].wait()

    received(hid_flights)
    hidden = hid[...].reshape(rows, width).astype(jnp.float32)
    centred = hidden - jnp.mean(hidden, axis=-1, keepdims=True)
    inv_std = lax.rsqrt(jnp.mean(centred * centred, axis=-1, keepdims=True) + EPSILON)
    unit[...] = centred * inv_std
    normed[...] = unit[...].astype(jnp.bfloat16)
    swaps += start(copy(normed.at[:, peer_core_cols], normed_o, core_peer))
    for tile in range(3):
        cols = slice(tile * attn, (tile + 1) * attn)
        qkv_rows[:, cols] = dot_rows(normed[...], qkv_weight[:, cols]).astype(jnp.bfloat16)
    attend(loc, attn, qkv_rows, grad_att, gqkv, att)
    swaps += start(copy(gqkv, gqkv_o, core_peer), copy(att, att_o, core_peer))
    grad_normed = dot_rows_t(gqkv[...], qkv_weight[...])
    unit_rows = unit[...]
    correction = (
        grad_normed
        - jnp.mean(grad_normed, axis=-1, keepdims=True)
        - unit_rows * jnp.mean(grad_normed * unit_rows, axis=-1, keepdims=True)
    )
    grad_hidden = (cot[...].astype(jnp.float32) + inv_std * correction).astype(jnp.bfloat16)
    gh_loc[...] = grad_hidden.reshape(tm_count, block, width)

    back = [copy(gh_loc.at[t], ghf.at[tm], (dp, t)) for t in peers]
    start(*back)
    ghf[tm] = gh_loc[tm]

    def spread(t):
        return (
            copy(ghf.at[t, :, other_cols], ghx.at[1, t], y_peer),
            copy(ghf.at[t, :, my_cols], ghx.at[0, t], core_peer),
        )

    spreads = [start(*spread(tm))]
    received(swaps)

    q_rows = share_q.shape[3]
    for tile in range(3):
        cols = slice(tile * attn, (tile + 1) * attn)
        result = dot_columns(normed[:, core_cols], gqkv[:, cols]) + dot_columns(
            normed_o[...], gqkv_o[:, cols]
        )
        for i in range(4 * hh):
            share_q[i // 4, i // 2 % 2, i % 2, :, cols] = result[
                i * q_rows : (i + 1) * q_rows
            ].astype(jnp.bfloat16)

    def sums(share, first, total, second, result):
        steps = []
        for z in range(hh):
            if z < hh // 2:
                away, peer, stay = share.at[z, :, 1 - my], y_peer, share.at[z, :, my]
                away_2, peer_2, stay_2 = 1 - mx, x_peer, mx
            else:
                away, peer, stay = share.at[z, 1 - mx], x_peer, share.at[z, mx]
                away_2, peer_2, stay_2 = 1 - my, y_peer, my
            one = copy(away, first.at[z], peer)
            two = copy(total.at[z, away_2], second.at[z], peer_2)
            steps.append((one, stay, first.at[z], total.at[z], two, stay_2, second.at[z], result.at[z]))
        return steps

    q_steps = sums(share_q, q_r1, q_s1, q_r2, q_sx)
    start(*[one[0] for one in q_steps])
    p_rows = share_p.shape[3]
    step = attn // 2 // 128 * 128
    window = pl.ds(pl.multiple_of(core * step, 128), attn - step)
    for tile in range(2):
        cols = slice(tile * half, (tile + 1) * half)
        part[...] = dot_columns(att[:, window], cot[:, cols]) + dot_columns(
            att_o[:, window], cot_o[:, cols]
        )
        offset = pl.multiple_of(core * (attn // 2 - step), 8)
        result = part[pl.ds(offset, attn // 2), :]
        for i in range(2 * hh):
            share_p[i // 2, i % 2, tile] = result[i * p_rows : (i + 1) * p_rows].astype(
                jnp.bfloat16
            )
    p_steps = sums(share_p, p_r1, p_s1, p_r2, p_sx)
    start(*[one[0] for one in p_steps])

    for one, t in zip(back, peers):
        received([one])
        spreads.append(start(*spread(t)))
    rim_out[...] = (
        ghf[...].astype(jnp.float32)[:, :loc].reshape(tm_count * loc, width).astype(jnp.bfloat16)
    )
    rim = copy(rim_out, rim_in, (dp, (tm + tm_count - 1) % tm_count))
    pl.when(tm > 0)(rim.start)

    received(lefts + rims)
    for k in range(1, 4):
        previous(k)
    forwards = []
    for (by_y, _), t in zip(spreads, [tm] + peers):
        received([by_y])
        forwards += start(copy(ghx.at[1, t], ghx.at[2, t], core_peer))
    received([by_core for _, by_core in spreads] + forwards)

    for one, stay, came, total, two, _, _, _ in q_steps + p_steps:
        received([one])
        total[...] = add(stay[...], came[...])
        start(two)

    c_rows = share_c.shape[3]
    conv_x = {}
    for tap in range(TAPS):
        result = dot_columns(
            left[0, tap].reshape(rows, half), ghf[:, :, my_cols].reshape(rows, half)
        )
        for k in range(1, 4):
            result += dot_columns(
                left[k, tap].reshape(rows, half), ghx[k - 1].reshape(rows, half)
            )
        for i in range(2 * hh):
            share_c[tap, i // 2, i % 2] = result[i * c_rows : (i + 1) * c_rows].astype(
                jnp.bfloat16
            )
        for z in range(hh):
            conv_x[tap, z] = copy(share_c.at[tap, z, 1 - mx], conv_rx.at[tap, z], x_peer)
            if tap == 0:
                start(conv_x[tap, z])

    above = (dp, (mz + 1) % high * 2 + mx)
    below = (dp, (mz + high - 1) % high * 2 + mx)
    chains = []

    def chain(total, came):
        links = []
        for z in range(hh):
            up = copy(total.at[z], came.at[0, z], above)
            down = copy(total.at[z], came.at[1, z], below)
            links.append((core * hh + z, up, down))

            @pl.when((mz == 0) & (core * hh + z > mz))
            def _():
                up.start()

            @pl.when((mz == high - 1) & (core * hh + z < mz))
            def _():
                down.start()

        chains.append(links)
        return links, total, came

    def chain_on(links, total, came):
        for z, (owner, up, down) in enumerate(links):
            for inner, one, side in (
                ((mz > 0) & (owner > mz), up, 0),
                ((mz < high - 1) & (owner < mz), down, 1),
            ):

                @pl.when(inner)
                def _():
                    one.wait_recv()
                    total[z] = add(total[z], came[side, z])
                    one.start()

    def chain_end(links, total, came, place):
        for z, (owner, up, down) in enumerate(links):
            @pl.when((owner == mz) & (mz > 0))
            def _():
                up.wait_recv()
                total[z] = add(total[z], came[0, z])

            @pl.when((owner == mz) & (mz < high - 1))
            def _():
                down.wait_recv()
                total[z] = add(total[z], came[1, z])

            @pl.when(owner == mz)
            def _():
                place[...] = (total[z].astype(jnp.float32) * scale).astype(jnp.bfloat16)

    def conv_sum(tap):
        for z in range(hh):
            received([conv_x[tap, z]])
            if tap + 1 < TAPS:
                start(conv_x[tap + 1, z])
            conv_sx[tap, z] = add(share_c[tap, z, mx], conv_rx[tap, z])
        return chain(conv_sx.at[tap], conv_rz.at[tap])

    pl.when(tm > 0)(rim.wait_send)
    pl.when(tm < tm_count - 1)(rim.wait_recv)

    @pl.when(tm == tm_count - 1)
    def _():
        rim_in[...] = jnp.zeros_like(rim_in)

    gh_rows = ghf[...].reshape(rows, width)

    def even_part(tile):
        part_of = slice(tile * half, (tile + 1) * half)
        grad = dot_rows_t(gh_rows, weight[part_of, width : 2 * width])
        frames_out[0, :, :, part_of] = grad.astype(jnp.bfloat16).reshape(tm_count, block, half)

    def odd_part(tile):
        part_of = slice(tile * half, (tile + 1) * half)
        before = dot_rows_t(gh_rows, weight[part_of, :width]).reshape(tm_count, block, half)
        rims = dot_rows_t(rim_in[...], weight[part_of, :width]).reshape(tm_count, loc, half)
        grad = dot_rows_t(gh_rows, weight[part_of, 2 * width :]).reshape(tm_count, block, half)
        grad += jnp.concatenate([before[:, loc:], rims], axis=1)
        frames_out[1, :, :, part_of] = grad.astype(jnp.bfloat16)

    last = []

    def gather(links, total, came, fin):
        chain_end(links, total, came, fin.at[my])
        to_y = copy(fin.at[my], fin.at[my], y_peer)
        own_to_core = copy(fin.at[my], fin.at[my], core_peer)
        other_to_core = copy(fin.at[1 - my], fin.at[1 - my], core_peer)
        last.append((to_y, own_to_core, other_to_core))

        @pl.when(is_dest)
        def _():
            to_y.start()
            own_to_core.start()

    sums_z = []
    for steps, totals, came_z in ((p_steps, p_sx, p_rz), (q_steps, q_sx, q_rz)):
        for _, _, _, total, two, stay, came, result in steps:
            received([two])
            result[...] = add(total[stay], came[...])
        sums_z.append(chain(totals, came_z))
    even_part(0)
    conv_z = [conv_sum(0)]
    for one in sums_z:
        chain_on(*one)
    even_part(1)
    conv_z.append(conv_sum(1))
    chain_on(*conv_z[0])
    gather(*sums_z[0], p_fin)
    gather(*sums_z[1], q_fin)
    odd_part(0)
    conv_z.append(conv_sum(2))
    chain_on(*conv_z[1])
    gather(*conv_z[0], conv_fin.at[0])
    odd_part(1)
    chain_on(*conv_z[2])
    gather(*conv_z[1], conv_fin.at[1])
    gather(*conv_z[2], conv_fin.at[2])

    for to_y, own_to_core, other_to_core in last:

        @pl.when(is_dest)
        def _():
            to_y.wait_recv()
            other_to_core.start()

        @pl.when(not_dest)
        def _():
            own_to_core.wait_recv()
            other_to_core.wait_recv()

    for tap in range(TAPS):
        for y in range(2):
            conv_out[:, tap * width + y * half : tap * width + (y + 1) * half] = conv_fin[tap, y]
    for y in range(2):
        proj_out[:, y * half : (y + 1) * half] = p_fin[y]
    qkv_out[...] = q_fin[...]

    for one in sent:
        one.wait_send()
    for links in chains:
        for owner, up, down in links:
            pl.when(owner > mz)(up.wait_send)
            pl.when(owner < mz)(down.wait_send)

    @pl.when(is_dest)
    def _():
        for copies in last:
            for one in copies:
                one.wait_send()


def block(frames, cot, loc, conv_weight, qkv_weight, out_weight, scale):
    tm_count, block_rows, width = cot.shape
    high = tm_count // 2
    hh = high // 2
    half = width // 2
    rows = tm_count * block_rows
    attn = out_weight.shape[0]
    c_rows = width // tm_count
    q_rows = c_rows // 2
    p_rows = attn // tm_count
    edge = tm_count * loc
    bf16 = jnp.bfloat16

    def vmem(*shape, dtype=bf16):
        return pltpu.VMEM(shape, dtype)

    scratch = [
        vmem(*conv_weight.shape),
        vmem(*qkv_weight.shape),
        vmem(*out_weight.shape),
        vmem(edge, width),
        vmem(edge, width),
        vmem(4, TAPS, tm_count, block_rows, half),
        vmem(4, edge, half),
        vmem(*cot.shape),
        vmem(*cot.shape),
        vmem(*cot.shape),
        vmem(rows, width, dtype=jnp.float32),
        vmem(rows, width),
        vmem(rows, 3 * attn),
        vmem(rows, attn),
        vmem(rows, 3 * attn),
        vmem(rows, attn),
        vmem(*cot.shape),
        vmem(*cot.shape),
        vmem(3, tm_count, block_rows, half),
        vmem(rows, half),
        vmem(rows, 3 * attn),
        vmem(rows, attn),
        vmem(rows, width),
        vmem(attn - attn // 2 // 128 * 128, half, dtype=jnp.float32),
        vmem(TAPS, hh, 2, c_rows, half),
        vmem(TAPS, hh, c_rows, half),
        vmem(TAPS, hh, c_rows, half),
        vmem(TAPS, 2, hh, c_rows, half),
        vmem(TAPS, 2, c_rows, half),
        vmem(hh, 2, 2, q_rows, 3 * attn),
        vmem(hh, 2, q_rows, 3 * attn),
        vmem(hh, 2, q_rows, 3 * attn),
        vmem(hh, q_rows, 3 * attn),
        vmem(hh, q_rows, 3 * attn),
        vmem(2, hh, q_rows, 3 * attn),
        vmem(2, q_rows, 3 * attn),
        vmem(hh, 2, 2, p_rows, half),
        vmem(hh, 2, p_rows, half),
        vmem(hh, 2, p_rows, half),
        vmem(hh, p_rows, half),
        vmem(hh, p_rows, half),
        vmem(2, hh, p_rows, half),
        vmem(2, p_rows, half),
        vmem(edge, width),
        vmem(edge, width),
    ]
    copies = 2 + 2 * (tm_count - 1) + 9 + 4 + tm_count - 1 + 3 * tm_count + TAPS * hh + 4 * hh + 10 * hh + 15
    semaphores = pltpu.SemaphoreType.DMA((copies,))
    space = pl.BlockSpec(memory_space=pltpu.VMEM)
    return pl.pallas_call(
        functools.partial(block_kernel, scale, tm_count),
        out_shape=[
            jax.ShapeDtypeStruct(frames.shape, bf16),
            jax.ShapeDtypeStruct((c_rows, TAPS * width), bf16),
            jax.ShapeDtypeStruct((2, q_rows, 3 * attn), bf16),
            jax.ShapeDtypeStruct((p_rows, width), bf16),
        ],
        in_specs=[space] * 2 + [pl.BlockSpec(memory_space=pl.ANY)] * 3,
        out_specs=[space] * 4,
        scratch_shapes=scratch + [semaphores, semaphores, pltpu.SemaphoreType.DMA((5,))],
        compiler_params=pltpu.CompilerParams(
            collective_id=0, has_side_effects=True, vmem_limit_bytes=VMEM_LIMIT
        ),
        cost_estimate=pl.CostEstimate(
            flops=12_000_000_000, bytes_accessed=200_000_000, transcendentals=0
        ),
    )(frames, cot, conv_weight, qkv_weight, out_weight)


def local(latents, conv_weight, qkv_weight, out_weight, out_cotangent):
    videos, frames, places, width = latents.shape
    half = frames // 2
    dp_count = lax.axis_size("dp")
    tm_count = lax.axis_size("tm")
    loc = places // tm_count
    rows = half * places

    split = latents.reshape(half, 2, tm_count, loc, width)
    split = jnp.transpose(split, (1, 2, 0, 3, 4)).reshape(2, tm_count, half * loc, width)
    cotangent = jnp.transpose(out_cotangent.reshape(half, tm_count, loc, width), (1, 0, 2, 3))
    grad_scale = 1.0 / math.sqrt(dp_count * tm_count * rows)
    grad_frames, conv_grad, qkv_grad, proj_grad = block(
        split,
        cotangent.reshape(tm_count, half * loc, width),
        loc,
        conv_weight,
        qkv_weight,
        out_weight,
        grad_scale,
    )
    qkv_grad = qkv_grad.reshape(-1, qkv_grad.shape[-1])
    input_grad = jnp.transpose(
        grad_frames.reshape(2, tm_count, half, loc, width), (2, 0, 1, 3, 4)
    ).reshape(latents.shape)
    return (input_grad, conv_grad, qkv_grad, proj_grad)


def solution(mesh):
    return jax.shard_map(
        local,
        mesh=mesh,
        in_specs=(P("dp", "tm", None, None), P(), P(), P(), P("dp", "tm", None, None)),
        out_specs=(P("dp", "tm", None, None), P("tm", None), P("tm", None), P("tm", None)),
        check_vma=False,
    )
```

```python
import functools
import math

import jax
import jax.numpy as jnp
from jax import lax
from jax.experimental import pallas as pl
from jax.experimental.pallas import tpu as pltpu
from jax.sharding import PartitionSpec as P

HEADS = 10
HEAD = 64
EPSILON = 1e-05
TAPS = 3
VMEM_LIMIT = 62 * 1024 * 1024


def dot_rows(left_side, right_side):
    return jnp.dot(left_side, right_side, preferred_element_type=jnp.float32)


def dot_rows_t(left_side, right_side):
    return lax.dot_general(
        left_side, right_side, (((1,), (1,)), ((), ())), preferred_element_type=jnp.float32
    )


def dot_columns(left_side, right_side):
    return lax.dot_general(
        left_side, right_side, (((0,), (0,)), ((), ())), preferred_element_type=jnp.float32
    )


def flipped(index, mask, size):
    result = 0
    bit = 1
    while bit < size:
        own = index // bit % 2
        result += (1 - own if mask & bit else own) * bit
        bit *= 2
    return result


def attend(loc, width, qkv_ref, g_ref, grad_ref, attended_ref):
    rows = qkv_ref.shape[0]
    row_at = lax.broadcasted_iota(jnp.int32, (rows, rows), 0)
    column_at = lax.broadcasted_iota(jnp.int32, (rows, rows), 1)
    same = (row_at % loc) == (column_at % loc)
    lane = lax.broadcasted_iota(jnp.int32, (rows, 2 * HEAD), 1)
    scale = 1.0 / math.sqrt(HEAD)
    for pair in range(width // (2 * HEAD)):
        first = pair * 2 * HEAD
        q = qkv_ref[:, first : first + 2 * HEAD]
        k = qkv_ref[:, width + first : width + first + 2 * HEAD]
        v = qkv_ref[:, 2 * width + first : 2 * width + first + 2 * HEAD]
        g = g_ref[:, first : first + 2 * HEAD]
        zero = jnp.zeros_like(q)
        grad_q = grad_k = grad_v = attended = None
        kept = []
        for head in range(2):
            mine = (lane >= HEAD) if head else (lane < HEAD)
            q_h = jnp.where(mine, q, zero)
            v_h = jnp.where(mine, v, zero)
            g_h = jnp.where(mine, g, zero)
            scores = jnp.where(same, dot_rows_t(q_h, k) * scale, -1e30)
            expo = jnp.exp(scores - jnp.max(scores, axis=1, keepdims=True))
            probs = expo * (1.0 / jnp.sum(expo, axis=1, keepdims=True))
            probs_b = probs.astype(jnp.bfloat16)
            part = dot_rows(probs_b, v_h)
            attended = part if attended is None else attended + part
            part = dot_columns(probs_b, g_h)
            grad_v = part if grad_v is None else grad_v + part
            grad_probs = dot_rows_t(g_h, v)
            kept.append((mine, q_h, probs, grad_probs))
        attended_b = attended.astype(jnp.bfloat16)
        product = g.astype(jnp.float32) * attended_b.astype(jnp.float32)
        for mine, q_h, probs, grad_probs in kept:
            k_h = jnp.where(mine, k, zero)
            delta = jnp.sum(jnp.where(mine, product, 0.0), axis=1, keepdims=True)
            grad_scores = (probs * (grad_probs - delta) * scale).astype(jnp.bfloat16)
            part = dot_rows(grad_scores, k_h)
            grad_q = part if grad_q is None else grad_q + part
            part = dot_columns(grad_scores, q_h)
            grad_k = part if grad_k is None else grad_k + part
        grad_ref[:, first : first + 2 * HEAD] = grad_q.astype(jnp.bfloat16)
        grad_ref[:, width + first : width + first + 2 * HEAD] = grad_k.astype(jnp.bfloat16)
        grad_ref[:, 2 * width + first : 2 * width + first + 2 * HEAD] = grad_v.astype(
            jnp.bfloat16
        )
        attended_ref[:, first : first + 2 * HEAD] = attended_b


def block_kernel(scale, tm_count, chunks, *refs):
    frames, cot_rows, weight_hbm, qkv_hbm, out_hbm = refs[:5]
    frames_out, conv_out, qkv_out, proj_out = refs[5:9]
    weight, qkv_weight, out_weight = refs[9:12]
    rim_rows, odd_rim, left, left_rim, hid_own, hid, cot_in = refs[12:19]
    unit, normed, qkv_rows, grad_att, gqkv, att, gh_loc = refs[19:26]
    ghf, ghx, normed_o, gqkv_o, att_o, cot_o, part = refs[26:33]
    share_c, conv_rx, conv_sx, conv_rz, conv_fin = refs[33:38]
    share_q, q_r1, q_s1, q_r2, q_sx, q_rz, q_fin = refs[38:45]
    share_p, p_r1, p_s1, p_r2, p_sx, p_rz, p_fin = refs[45:52]
    rim_out, rim_in = refs[52:54]
    send_sem, recv_sem, load_sem = refs[54:57]
    high = tm_count // 2
    hh = high // 2
    block, width = cot_rows.shape[1:]
    even, odd = frames.at[0], frames.at[1]
    rows = tm_count * block
    half = width // 2
    attn = att.shape[1]
    loc = rim_in.shape[0] // tm_count
    groups, group, edge = tm_count * chunks, block // chunks, loc // chunks
    count_c = rows // chunks
    dp, tm = lax.axis_index("dp"), lax.axis_index("tm")
    core, my = dp % 2, dp // 2
    mx, mz = tm % 2, tm // 2
    x_peer = (dp, tm + 1 - 2 * mx)
    y_peer = (dp + 2 - 4 * my, tm)
    diagonal = (dp + 3 - 4 * my - 2 * core, tm)
    core_peer = (dp + 1 - 2 * core, tm)
    is_dest = mz // hh == core
    not_dest = mz // hh != core
    peers = [flipped(tm, d, tm_count) for d in range(1, tm_count)]

    loads = []
    for i, tap in enumerate((1, 2, 0)):
        cols = pl.ds(tap * width, width)
        loads.append(
            pltpu.make_async_copy(weight_hbm.at[:, cols], weight.at[:, cols], load_sem.at[i])
        )
    loads.append(pltpu.make_async_copy(out_hbm, out_weight, load_sem.at[3]))
    loads.append(pltpu.make_async_copy(qkv_hbm, qkv_weight, load_sem.at[4]))
    for one in loads:
        one.start()

    barrier = pltpu.get_barrier_semaphore()
    for peer in [y_peer, core_peer, diagonal] + [(dp, t) for t in peers]:
        pl.semaphore_signal(
            barrier, inc=1, device_id=peer, device_id_type=pl.DeviceIdType.MESH
        )
    pl.semaphore_wait(barrier, tm_count + 2)

    count = [0]

    def copy(source, target, peer):
        index = count[0]
        count[0] += 1
        return pltpu.make_async_remote_copy(
            src_ref=source,
            dst_ref=target,
            send_sem=send_sem.at[index],
            recv_sem=recv_sem.at[index],
            device_id=peer,
            device_id_type=pl.DeviceIdType.MESH,
        )

    def start(*copies):
        for one in copies:
            one.start()
        return copies

    sent = []

    def received(copies):
        for one in copies:
            one.wait_recv()
            sent.append(one)

    my_cols = pl.ds(pl.multiple_of(my * half, 128), half)
    other_cols = pl.ds(pl.multiple_of((1 - my) * half, 128), half)
    core_cols = pl.ds(pl.multiple_of(core * half, 128), half)
    peer_core_cols = pl.ds(pl.multiple_of((1 - core) * half, 128), half)

    def add(a, b):
        return (a.astype(jnp.float32) + b.astype(jnp.float32)).astype(jnp.bfloat16)

    last_rows = odd[...].astype(jnp.float32).reshape(groups, group, width)[:, group - edge :]
    rim_rows[...] = last_rows.reshape(tm_count * loc, width).astype(jnp.bfloat16)
    odd_next = copy(rim_rows, odd_rim, (dp, (tm + 1) % tm_count))
    pl.when(tm < tm_count - 1)(odd_next.start)
    chunk_rows = [pl.ds(c * group, group) for c in range(chunks)]
    cot_flights = []
    for c, part_of in enumerate(chunk_rows):
        for t in peers:
            cot_flights += start(copy(cot_rows.at[t, part_of], cot_in.at[c, tm], (dp, t)))
        cot_in[c, tm] = cot_rows[tm, part_of]

    lefts = []
    dp_peers = ((1, core_peer, peer_core_cols), (2, y_peer, core_cols), (3, diagonal, peer_core_cols))
    for which in range(2):
        left[0, 1 + which] = frames[which, :, :, core_cols]
        for k, peer, cols in dp_peers:
            lefts += start(copy(frames.at[which, :, :, cols], left.at[k, 1 + which], peer))

    for one in loads[:2]:
        one.wait()
    even_rows = even[...].reshape(rows, width)
    odd_rows = odd[...].reshape(rows, width)
    for tile in range(2):
        cols = slice(tile * half, (tile + 1) * half)
        total = dot_rows(even_rows, weight[:, width + tile * half : width + (tile + 1) * half])
        total += dot_rows(
            odd_rows, weight[:, 2 * width + tile * half : 2 * width + (tile + 1) * half]
        )
        if tile == 0:
            loads[2].wait()
        before = dot_rows(odd_rows, weight[:, cols])
        if tile == 0:
            pl.when(tm < tm_count - 1)(odd_next.wait_send)
            pl.when(tm > 0)(odd_next.wait_recv)

            @pl.when(tm == 0)
            def _():
                odd_rim[...] = jnp.zeros_like(odd_rim)

        rims = dot_rows(odd_rim[...], weight[:, cols]).reshape(groups, edge, half)
        before = before.reshape(groups, group, half)
        total = total.reshape(groups, group, half)
        total += jnp.concatenate([rims, before[:, : group - edge]], axis=1)
        total = total.astype(jnp.bfloat16)
        hid_own[:, :, cols] = total.reshape(tm_count, block, half)
    hid_flights = []
    for c, part_of in enumerate(chunk_rows):
        hid_flights.append([copy(hid_own.at[t, part_of], hid.at[c, tm], (dp, t)) for t in peers])
        hid[c, tm] = hid_own[tm, part_of]
    start(*hid_flights[0])

    left_rim[0] = odd_rim[:, core_cols]
    rims = []
    for k, peer, cols in dp_peers:
        rims += start(copy(odd_rim.at[:, cols], left_rim.at[k], peer))

    def previous(k):
        later = left[k, 2].astype(jnp.float32).reshape(groups, group, half)
        first = left_rim[k].astype(jnp.float32).reshape(groups, edge, half)
        later = jnp.concatenate([first, later[:, : group - edge]], axis=1)
        left[k, 0] = later.astype(jnp.bfloat16).reshape(tm_count, block, half)

    previous(0)
    received(cot_flights)
    loads[3].wait()
    cot = cot_in.reshape(rows, width)
    swaps = list(start(copy(cot, cot_o, core_peer)))
    grad_att[...] = dot_rows_t(cot[...], out_weight[...]).astype(jnp.bfloat16)
    loads[4].wait()

    spreads = []

    def spread(c, t):
        part_of = chunk_rows[c]
        flights = start(
            copy(ghf.at[t, part_of, other_cols], ghx.at[1, t, part_of], y_peer),
            copy(ghf.at[t, part_of, my_cols], ghx.at[0, t, part_of], core_peer),
        )
        spreads.append((c, t, *flights))

    back = []
    for c in range(chunks):
        received(hid_flights[c])
        if c + 1 < chunks:
            start(*hid_flights[c + 1])
        here = pl.ds(c * count_c, count_c)
        hidden = hid[c].reshape(count_c, width).astype(jnp.float32)
        centred = hidden - jnp.mean(hidden, axis=-1, keepdims=True)
        inv_std = lax.rsqrt(jnp.mean(centred * centred, axis=-1, keepdims=True) + EPSILON)
        unit[...] = centred * inv_std
        normed[here] = unit[...].astype(jnp.bfloat16)
        swaps += start(copy(normed.at[here, peer_core_cols], normed_o.at[here], core_peer))
        for tile in range(3):
            cols = slice(tile * attn, (tile + 1) * attn)
            qkv_rows[here, cols] = dot_rows(normed[here], qkv_weight[:, cols]).astype(jnp.bfloat16)
        attend(edge, attn, qkv_rows.at[here], grad_att.at[here], gqkv.at[here], att.at[here])
        swaps += start(
            copy(gqkv.at[here], gqkv_o.at[here], core_peer),
            copy(att.at[here], att_o.at[here], core_peer),
        )
        grad_normed = dot_rows_t(gqkv[here], qkv_weight[...])
        unit_rows = unit[...]
        correction = (
            grad_normed
            - jnp.mean(grad_normed, axis=-1, keepdims=True)
            - unit_rows * jnp.mean(grad_normed * unit_rows, axis=-1, keepdims=True)
        )
        cot_part = cot_in[c].reshape(count_c, width).astype(jnp.float32)
        grad_hidden = (cot_part + inv_std * correction).astype(jnp.bfloat16)
        gh_loc[c] = grad_hidden.reshape(tm_count, group, width)

        for t in peers:
            flight = copy(gh_loc.at[c, t], ghf.at[tm, chunk_rows[c]], (dp, t))
            start(flight)
            back.append((c, t, flight))
        ghf[tm, chunk_rows[c]] = gh_loc[c, tm]
        spread(c, tm)

    received(swaps)

    q_rows = share_q.shape[3]
    for tile in range(3):
        cols = slice(tile * attn, (tile + 1) * attn)
        result = dot_columns(normed[:, core_cols], gqkv[:, cols]) + dot_columns(
            normed_o[...], gqkv_o[:, cols]
        )
        for i in range(4 * hh):
            share_q[i // 4, i // 2 % 2, i % 2, :, cols] = result[
                i * q_rows : (i + 1) * q_rows
            ].astype(jnp.bfloat16)

    def sums(share, first, total, second, result):
        steps = []
        for z in range(hh):
            if z < hh // 2:
                away, peer, stay = share.at[z, :, 1 - my], y_peer, share.at[z, :, my]
                away_2, peer_2, stay_2 = 1 - mx, x_peer, mx
            else:
                away, peer, stay = share.at[z, 1 - mx], x_peer, share.at[z, mx]
                away_2, peer_2, stay_2 = 1 - my, y_peer, my
            one = copy(away, first.at[z], peer)
            two = copy(total.at[z, away_2], second.at[z], peer_2)
            steps.append((one, stay, first.at[z], total.at[z], two, stay_2, second.at[z], result.at[z]))
        return steps

    q_steps = sums(share_q, q_r1, q_s1, q_r2, q_sx)
    start(*[one[0] for one in q_steps])
    p_rows = share_p.shape[3]
    step = attn // 2 // 128 * 128
    window = pl.ds(pl.multiple_of(core * step, 128), attn - step)
    for tile in range(2):
        cols = slice(tile * half, (tile + 1) * half)
        part[...] = dot_columns(att[:, window], cot[:, cols]) + dot_columns(
            att_o[:, window], cot_o[:, cols]
        )
        offset = pl.multiple_of(core * (attn // 2 - step), 8)
        result = part[pl.ds(offset, attn // 2), :]
        for i in range(2 * hh):
            share_p[i // 2, i % 2, tile] = result[i * p_rows : (i + 1) * p_rows].astype(
                jnp.bfloat16
            )
    p_steps = sums(share_p, p_r1, p_s1, p_r2, p_sx)
    start(*[one[0] for one in p_steps])

    for c, t, one in back:
        received([one])
        spread(c, t)
    rim_out[...] = (
        ghf[...]
        .astype(jnp.float32)
        .reshape(groups, group, width)[:, :edge]
        .reshape(tm_count * loc, width)
        .astype(jnp.bfloat16)
    )
    rim = copy(rim_out, rim_in, (dp, (tm + tm_count - 1) % tm_count))
    pl.when(tm > 0)(rim.start)

    received(lefts + rims)
    for k in range(1, 4):
        previous(k)
    forwards = []
    for c, t, by_y, _ in spreads:
        received([by_y])
        part_of = chunk_rows[c]
        forwards += start(copy(ghx.at[1, t, part_of], ghx.at[2, t, part_of], core_peer))
    received([by_core for _, _, _, by_core in spreads] + forwards)

    for one, stay, came, total, two, _, _, _ in q_steps + p_steps:
        received([one])
        total[...] = add(stay[...], came[...])
        start(two)

    c_rows = share_c.shape[3]
    conv_x = {}
    for tap in range(TAPS):
        result = dot_columns(
            left[0, tap].reshape(rows, half), ghf[:, :, my_cols].reshape(rows, half)
        )
        for k in range(1, 4):
            result += dot_columns(
                left[k, tap].reshape(rows, half), ghx[k - 1].reshape(rows, half)
            )
        for i in range(2 * hh):
            share_c[tap, i // 2, i % 2] = result[i * c_rows : (i + 1) * c_rows].astype(
                jnp.bfloat16
            )
        for z in range(hh):
            conv_x[tap, z] = copy(share_c.at[tap, z, 1 - mx], conv_rx.at[tap, z], x_peer)
            if tap == 0:
                start(conv_x[tap, z])

    above = (dp, (mz + 1) % high * 2 + mx)
    below = (dp, (mz + high - 1) % high * 2 + mx)
    chains = []

    def chain(total, came):
        links = []
        for z in range(hh):
            up = copy(total.at[z], came.at[0, z], above)
            down = copy(total.at[z], came.at[1, z], below)
            links.append((core * hh + z, up, down))

            @pl.when((mz == 0) & (core * hh + z > mz))
            def _():
                up.start()

            @pl.when((mz == high - 1) & (core * hh + z < mz))
            def _():
                down.start()

        chains.append(links)
        return links, total, came

    def chain_on(links, total, came):
        for z, (owner, up, down) in enumerate(links):
            for inner, one, side in (
                ((mz > 0) & (owner > mz), up, 0),
                ((mz < high - 1) & (owner < mz), down, 1),
            ):

                @pl.when(inner)
                def _():
                    one.wait_recv()
                    total[z] = add(total[z], came[side, z])
                    one.start()

    def chain_end(links, total, came, place):
        for z, (owner, up, down) in enumerate(links):
            @pl.when((owner == mz) & (mz > 0))
            def _():
                up.wait_recv()
                total[z] = add(total[z], came[0, z])

            @pl.when((owner == mz) & (mz < high - 1))
            def _():
                down.wait_recv()
                total[z] = add(total[z], came[1, z])

            @pl.when(owner == mz)
            def _():
                place[...] = (total[z].astype(jnp.float32) * scale).astype(jnp.bfloat16)

    def conv_sum(tap):
        for z in range(hh):
            received([conv_x[tap, z]])
            if tap + 1 < TAPS:
                start(conv_x[tap + 1, z])
            conv_sx[tap, z] = add(share_c[tap, z, mx], conv_rx[tap, z])
        return chain(conv_sx.at[tap], conv_rz.at[tap])

    pl.when(tm > 0)(rim.wait_send)
    pl.when(tm < tm_count - 1)(rim.wait_recv)

    @pl.when(tm == tm_count - 1)
    def _():
        rim_in[...] = jnp.zeros_like(rim_in)

    gh_rows = ghf[...].reshape(rows, width)

    def even_part(tile):
        part_of = slice(tile * half, (tile + 1) * half)
        grad = dot_rows_t(gh_rows, weight[part_of, width : 2 * width])
        frames_out[0, :, :, part_of] = grad.astype(jnp.bfloat16).reshape(tm_count, block, half)

    def odd_part(tile):
        part_of = slice(tile * half, (tile + 1) * half)
        before = dot_rows_t(gh_rows, weight[part_of, :width]).reshape(groups, group, half)
        rims = dot_rows_t(rim_in[...], weight[part_of, :width]).reshape(groups, edge, half)
        grad = dot_rows_t(gh_rows, weight[part_of, 2 * width :]).reshape(groups, group, half)
        grad += jnp.concatenate([before[:, edge:], rims], axis=1)
        grad = grad.astype(jnp.bfloat16)
        frames_out[1, :, :, part_of] = grad.reshape(tm_count, block, half)

    last = []

    def gather(links, total, came, fin):
        chain_end(links, total, came, fin.at[my])
        to_y = copy(fin.at[my], fin.at[my], y_peer)
        own_to_core = copy(fin.at[my], fin.at[my], core_peer)
        other_to_core = copy(fin.at[1 - my], fin.at[1 - my], core_peer)
        last.append((to_y, own_to_core, other_to_core))

        @pl.when(is_dest)
        def _():
            to_y.start()
            own_to_core.start()

    sums_z = []
    for steps, totals, came_z in ((p_steps, p_sx, p_rz), (q_steps, q_sx, q_rz)):
        for _, _, _, total, two, stay, came, result in steps:
            received([two])
            result[...] = add(total[stay], came[...])
        sums_z.append(chain(totals, came_z))
    even_part(0)
    conv_z = [conv_sum(0)]
    for one in sums_z:
        chain_on(*one)
    even_part(1)
    conv_z.append(conv_sum(1))
    chain_on(*conv_z[0])
    gather(*sums_z[0], p_fin)
    gather(*sums_z[1], q_fin)
    odd_part(0)
    conv_z.append(conv_sum(2))
    chain_on(*conv_z[1])
    gather(*conv_z[0], conv_fin.at[0])
    odd_part(1)
    chain_on(*conv_z[2])
    gather(*conv_z[1], conv_fin.at[1])
    gather(*conv_z[2], conv_fin.at[2])

    for to_y, own_to_core, other_to_core in last:

        @pl.when(is_dest)
        def _():
            to_y.wait_recv()
            other_to_core.start()

        @pl.when(not_dest)
        def _():
            own_to_core.wait_recv()
            other_to_core.wait_recv()

    for tap in range(TAPS):
        for y in range(2):
            conv_out[:, tap * width + y * half : tap * width + (y + 1) * half] = conv_fin[tap, y]
    for y in range(2):
        proj_out[:, y * half : (y + 1) * half] = p_fin[y]
    qkv_out[...] = q_fin[...]

    for one in sent:
        one.wait_send()
    for links in chains:
        for owner, up, down in links:
            pl.when(owner > mz)(up.wait_send)
            pl.when(owner < mz)(down.wait_send)

    @pl.when(is_dest)
    def _():
        for copies in last:
            for one in copies:
                one.wait_send()


def block(frames, cot, loc, chunks, conv_weight, qkv_weight, out_weight, scale):
    tm_count, block_rows, width = cot.shape
    high = tm_count // 2
    hh = high // 2
    half = width // 2
    rows = tm_count * block_rows
    attn = out_weight.shape[0]
    c_rows = width // tm_count
    q_rows = c_rows // 2
    p_rows = attn // tm_count
    edge = tm_count * loc
    bf16 = jnp.bfloat16

    def vmem(*shape, dtype=bf16):
        return pltpu.VMEM(shape, dtype)

    scratch = [
        vmem(*conv_weight.shape),
        vmem(*qkv_weight.shape),
        vmem(*out_weight.shape),
        vmem(edge, width),
        vmem(edge, width),
        vmem(4, TAPS, tm_count, block_rows, half),
        vmem(4, edge, half),
        vmem(*cot.shape),
        vmem(chunks, tm_count, block_rows // chunks, width),
        vmem(chunks, tm_count, block_rows // chunks, width),
        vmem(rows // chunks, width, dtype=jnp.float32),
        vmem(rows, width),
        vmem(rows, 3 * attn),
        vmem(rows, attn),
        vmem(rows, 3 * attn),
        vmem(rows, attn),
        vmem(chunks, tm_count, block_rows // chunks, width),
        vmem(*cot.shape),
        vmem(3, tm_count, block_rows, half),
        vmem(rows, half),
        vmem(rows, 3 * attn),
        vmem(rows, attn),
        vmem(rows, width),
        vmem(attn - attn // 2 // 128 * 128, half, dtype=jnp.float32),
        vmem(TAPS, hh, 2, c_rows, half),
        vmem(TAPS, hh, c_rows, half),
        vmem(TAPS, hh, c_rows, half),
        vmem(TAPS, 2, hh, c_rows, half),
        vmem(TAPS, 2, c_rows, half),
        vmem(hh, 2, 2, q_rows, 3 * attn),
        vmem(hh, 2, q_rows, 3 * attn),
        vmem(hh, 2, q_rows, 3 * attn),
        vmem(hh, q_rows, 3 * attn),
        vmem(hh, q_rows, 3 * attn),
        vmem(2, hh, q_rows, 3 * attn),
        vmem(2, q_rows, 3 * attn),
        vmem(hh, 2, 2, p_rows, half),
        vmem(hh, 2, p_rows, half),
        vmem(hh, 2, p_rows, half),
        vmem(hh, p_rows, half),
        vmem(hh, p_rows, half),
        vmem(2, hh, p_rows, half),
        vmem(2, p_rows, half),
        vmem(edge, width),
        vmem(edge, width),
    ]
    per_chunk = 3 * (tm_count - 1) + 3 + 3 * tm_count
    copies = 12 + chunks * per_chunk + TAPS * hh + 4 * hh + 10 * hh + 15
    semaphores = pltpu.SemaphoreType.DMA((copies,))
    space = pl.BlockSpec(memory_space=pltpu.VMEM)
    return pl.pallas_call(
        functools.partial(block_kernel, scale, tm_count, chunks),
        out_shape=[
            jax.ShapeDtypeStruct(frames.shape, bf16),
            jax.ShapeDtypeStruct((c_rows, TAPS * width), bf16),
            jax.ShapeDtypeStruct((2, q_rows, 3 * attn), bf16),
            jax.ShapeDtypeStruct((p_rows, width), bf16),
        ],
        in_specs=[space] * 2 + [pl.BlockSpec(memory_space=pl.ANY)] * 3,
        out_specs=[space] * 4,
        scratch_shapes=scratch + [semaphores, semaphores, pltpu.SemaphoreType.DMA((5,))],
        compiler_params=pltpu.CompilerParams(
            collective_id=0, has_side_effects=True, vmem_limit_bytes=VMEM_LIMIT
        ),
        cost_estimate=pl.CostEstimate(
            flops=12_000_000_000, bytes_accessed=200_000_000, transcendentals=0
        ),
    )(frames, cot, conv_weight, qkv_weight, out_weight)


def local(latents, conv_weight, qkv_weight, out_weight, out_cotangent):
    videos, frames, places, width = latents.shape
    half = frames // 2
    dp_count = lax.axis_size("dp")
    tm_count = lax.axis_size("tm")
    loc = places // tm_count
    rows = half * places

    chunks = 2 if loc % 2 == 0 and half * loc % 32 == 0 else 1
    part = loc // chunks

    split = jnp.transpose(
        latents.reshape(half, 2, tm_count, chunks, part, width), (1, 2, 3, 0, 4, 5)
    ).reshape(2, tm_count, half * loc, width)
    cotangent = jnp.transpose(
        out_cotangent.reshape(half, tm_count, chunks, part, width), (1, 2, 0, 3, 4)
    )
    grad_scale = 1.0 / math.sqrt(dp_count * tm_count * rows)
    grad_frames, conv_grad, qkv_grad, proj_grad = block(
        split,
        cotangent.reshape(tm_count, half * loc, width),
        loc,
        chunks,
        conv_weight,
        qkv_weight,
        out_weight,
        grad_scale,
    )
    qkv_grad = qkv_grad.reshape(-1, qkv_grad.shape[-1])
    input_grad = jnp.transpose(
        grad_frames.reshape(2, tm_count, chunks, half, part, width), (3, 0, 1, 2, 4, 5)
    ).reshape(latents.shape)
    return (input_grad, conv_grad, qkv_grad, proj_grad)


def solution(mesh):
    return jax.shard_map(
        local,
        mesh=mesh,
        in_specs=(P("dp", "tm", None, None), P(), P(), P(), P("dp", "tm", None, None)),
        out_specs=(P("dp", "tm", None, None), P("tm", None), P("tm", None), P("tm", None)),
        check_vma=False,
    )
```

```python
import functools
import math

import jax
import jax.numpy as jnp
from jax import lax
from jax.experimental import pallas as pl
from jax.experimental.pallas import tpu as pltpu
from jax.sharding import PartitionSpec as P

HEADS = 10
HEAD = 64
EPSILON = 1e-05
TAPS = 3
VMEM_LIMIT = 62 * 1024 * 1024


def dot_rows(left_side, right_side):
    return jnp.dot(left_side, right_side, preferred_element_type=jnp.float32)


def dot_rows_t(left_side, right_side):
    return lax.dot_general(
        left_side, right_side, (((1,), (1,)), ((), ())), preferred_element_type=jnp.float32
    )


def dot_columns(left_side, right_side):
    return lax.dot_general(
        left_side, right_side, (((0,), (0,)), ((), ())), preferred_element_type=jnp.float32
    )


def flipped(index, mask, size):
    result = 0
    bit = 1
    while bit < size:
        own = index // bit % 2
        result += (1 - own if mask & bit else own) * bit
        bit *= 2
    return result


def attend(loc, width, qkv_ref, g_ref, grad_ref, attended_ref):
    rows = qkv_ref.shape[0]
    row_at = lax.broadcasted_iota(jnp.int32, (rows, rows), 0)
    column_at = lax.broadcasted_iota(jnp.int32, (rows, rows), 1)
    same = (row_at % loc) == (column_at % loc)
    lane = lax.broadcasted_iota(jnp.int32, (rows, 2 * HEAD), 1)
    scale = 1.0 / math.sqrt(HEAD)
    for pair in range(width // (2 * HEAD)):
        first = pair * 2 * HEAD
        q = qkv_ref[:, first : first + 2 * HEAD]
        k = qkv_ref[:, width + first : width + first + 2 * HEAD]
        v = qkv_ref[:, 2 * width + first : 2 * width + first + 2 * HEAD]
        g = g_ref[:, first : first + 2 * HEAD]
        zero = jnp.zeros_like(q)
        grad_q = grad_k = grad_v = attended = None
        kept = []
        for head in range(2):
            mine = (lane >= HEAD) if head else (lane < HEAD)
            q_h = jnp.where(mine, q, zero)
            v_h = jnp.where(mine, v, zero)
            g_h = jnp.where(mine, g, zero)
            scores = jnp.where(same, dot_rows_t(q_h, k) * scale, -1e30)
            expo = jnp.exp(scores - jnp.max(scores, axis=1, keepdims=True))
            probs = expo * (1.0 / jnp.sum(expo, axis=1, keepdims=True))
            probs_b = probs.astype(jnp.bfloat16)
            part = dot_rows(probs_b, v_h)
            attended = part if attended is None else attended + part
            part = dot_columns(probs_b, g_h)
            grad_v = part if grad_v is None else grad_v + part
            grad_probs = dot_rows_t(g_h, v)
            kept.append((mine, q_h, probs, grad_probs))
        attended_b = attended.astype(jnp.bfloat16)
        product = g.astype(jnp.float32) * attended_b.astype(jnp.float32)
        for mine, q_h, probs, grad_probs in kept:
            k_h = jnp.where(mine, k, zero)
            delta = jnp.sum(jnp.where(mine, product, 0.0), axis=1, keepdims=True)
            grad_scores = (probs * (grad_probs - delta) * scale).astype(jnp.bfloat16)
            part = dot_rows(grad_scores, k_h)
            grad_q = part if grad_q is None else grad_q + part
            part = dot_columns(grad_scores, q_h)
            grad_k = part if grad_k is None else grad_k + part
        grad_ref[:, first : first + 2 * HEAD] = grad_q.astype(jnp.bfloat16)
        grad_ref[:, width + first : width + first + 2 * HEAD] = grad_k.astype(jnp.bfloat16)
        grad_ref[:, 2 * width + first : 2 * width + first + 2 * HEAD] = grad_v.astype(
            jnp.bfloat16
        )
        attended_ref[:, first : first + 2 * HEAD] = attended_b


def block_kernel(scale, tm_count, *refs):
    frames, cot_rows, weight_hbm, qkv_hbm, out_hbm = refs[:5]
    frames_out, conv_out, qkv_out, proj_out = refs[5:9]
    weight, qkv_weight, out_weight = refs[9:12]
    rim_rows, odd_rim, left, left_rim, hid_own, hid, cot_in = refs[12:19]
    unit, normed, qkv_rows, grad_att, gqkv, att, gh_loc = refs[19:26]
    ghf, ghx, normed_o, gqkv_o, att_o, cot_o, part = refs[26:33]
    share_c, conv_rx, conv_sx, conv_rz, conv_fin = refs[33:38]
    share_q, q_r1, q_s1, q_r2, q_sx, q_rz, q_fin = refs[38:45]
    share_p, p_r1, p_s1, p_r2, p_sx, p_rz, p_fin = refs[45:52]
    rim_out, rim_in = refs[52:54]
    send_sem, recv_sem, load_sem = refs[54:57]
    high = tm_count // 2
    hh = high // 2
    block, width = cot_rows.shape[1:]
    even, odd = frames.at[0], frames.at[1]
    rows = tm_count * block
    half = width // 2
    attn = att.shape[1]
    loc = rim_in.shape[0] // tm_count
    dp, tm = lax.axis_index("dp"), lax.axis_index("tm")
    core, my = dp % 2, dp // 2
    mx, mz = tm % 2, tm // 2
    x_peer = (dp, tm + 1 - 2 * mx)
    y_peer = (dp + 2 - 4 * my, tm)
    diagonal = (dp + 3 - 4 * my - 2 * core, tm)
    core_peer = (dp + 1 - 2 * core, tm)
    is_dest = mz // hh == core
    not_dest = mz // hh != core
    peers = [flipped(tm, d, tm_count) for d in range(1, tm_count)]

    loads = []
    for i, tap in enumerate((1, 2, 0)):
        cols = pl.ds(tap * width, width)
        loads.append(
            pltpu.make_async_copy(weight_hbm.at[:, cols], weight.at[:, cols], load_sem.at[i])
        )
    loads.append(pltpu.make_async_copy(out_hbm, out_weight, load_sem.at[3]))
    loads.append(pltpu.make_async_copy(qkv_hbm, qkv_weight, load_sem.at[4]))
    for one in loads:
        one.start()

    barrier = pltpu.get_barrier_semaphore()
    for peer in [y_peer, core_peer, diagonal] + [(dp, t) for t in peers]:
        pl.semaphore_signal(
            barrier, inc=1, device_id=peer, device_id_type=pl.DeviceIdType.MESH
        )
    pl.semaphore_wait(barrier, tm_count + 2)

    count = [0]

    def copy(source, target, peer):
        index = count[0]
        count[0] += 1
        return pltpu.make_async_remote_copy(
            src_ref=source,
            dst_ref=target,
            send_sem=send_sem.at[index],
            recv_sem=recv_sem.at[index],
            device_id=peer,
            device_id_type=pl.DeviceIdType.MESH,
        )

    def start(*copies):
        for one in copies:
            one.start()
        return copies

    sent = []

    def received(copies):
        for one in copies:
            one.wait_recv()
            sent.append(one)

    my_cols = pl.ds(pl.multiple_of(my * half, 128), half)
    other_cols = pl.ds(pl.multiple_of((1 - my) * half, 128), half)
    core_cols = pl.ds(pl.multiple_of(core * half, 128), half)
    peer_core_cols = pl.ds(pl.multiple_of((1 - core) * half, 128), half)

    def add(a, b):
        return (a.astype(jnp.float32) + b.astype(jnp.float32)).astype(jnp.bfloat16)

    last_rows = odd[...].astype(jnp.float32)[:, block - loc :]
    rim_rows[...] = last_rows.reshape(tm_count * loc, width).astype(jnp.bfloat16)
    odd_next = copy(rim_rows, odd_rim, (dp, (tm + 1) % tm_count))
    pl.when(tm < tm_count - 1)(odd_next.start)
    cot_flights = start(*[copy(cot_rows.at[t], cot_in.at[tm], (dp, t)) for t in peers])
    cot_in[tm] = cot_rows[tm]

    lefts = []
    dp_peers = ((1, core_peer, peer_core_cols), (2, y_peer, core_cols), (3, diagonal, peer_core_cols))
    for which in range(2):
        left[0, 1 + which] = frames[which, :, :, core_cols]
        for k, peer, cols in dp_peers:
            lefts += start(copy(frames.at[which, :, :, cols], left.at[k, 1 + which], peer))

    for one in loads[:2]:
        one.wait()
    even_rows = even[...].reshape(rows, width)
    odd_rows = odd[...].reshape(rows, width)
    for tile in range(2):
        cols = slice(tile * half, (tile + 1) * half)
        total = dot_rows(even_rows, weight[:, width + tile * half : width + (tile + 1) * half])
        total += dot_rows(
            odd_rows, weight[:, 2 * width + tile * half : 2 * width + (tile + 1) * half]
        )
        if tile == 0:
            loads[2].wait()
        before = dot_rows(odd_rows, weight[:, cols])
        if tile == 0:
            pl.when(tm < tm_count - 1)(odd_next.wait_send)
            pl.when(tm > 0)(odd_next.wait_recv)

            @pl.when(tm == 0)
            def _():
                odd_rim[...] = jnp.zeros_like(odd_rim)

        rims = dot_rows(odd_rim[...], weight[:, cols]).reshape(tm_count, loc, half)
        before = before.reshape(tm_count, block, half)
        total = total.reshape(tm_count, block, half)
        total += jnp.concatenate([rims, before[:, : block - loc]], axis=1)
        hid_own[:, :, cols] = total.astype(jnp.bfloat16)
    hid_flights = start(*[copy(hid_own.at[t], hid.at[tm], (dp, t)) for t in peers])
    hid[tm] = hid_own[tm]

    left_rim[0] = odd_rim[:, core_cols]
    rims = []
    for k, peer, cols in dp_peers:
        rims += start(copy(odd_rim.at[:, cols], left_rim.at[k], peer))

    def previous(k):
        later = left[k, 2].astype(jnp.float32)
        edge = left_rim[k].astype(jnp.float32).reshape(tm_count, loc, half)
        later = jnp.concatenate([edge, later[:, : block - loc]], axis=1)
        left[k, 0] = later.astype(jnp.bfloat16)

    previous(0)
    received(cot_flights)
    loads[3].wait()
    cot = cot_in.reshape(rows, width)
    swaps = list(start(copy(cot, cot_o, core_peer)))
    grad_att[...] = dot_rows_t(cot[...], out_weight[...]).astype(jnp.bfloat16)
    loads[4].wait()

    received(hid_flights)
    hidden = hid[...].reshape(rows, width).astype(jnp.float32)
    centred = hidden - jnp.mean(hidden, axis=-1, keepdims=True)
    inv_std = lax.rsqrt(jnp.mean(centred * centred, axis=-1, keepdims=True) + EPSILON)
    unit[...] = centred * inv_std
    normed[...] = unit[...].astype(jnp.bfloat16)
    swaps += start(copy(normed.at[:, peer_core_cols], normed_o, core_peer))
    for tile in range(3):
        cols = slice(tile * attn, (tile + 1) * attn)
        qkv_rows[:, cols] = dot_rows(normed[...], qkv_weight[:, cols]).astype(jnp.bfloat16)
    attend(loc, attn, qkv_rows, grad_att, gqkv, att)
    swaps += start(copy(gqkv, gqkv_o, core_peer), copy(att, att_o, core_peer))
    grad_normed = dot_rows_t(gqkv[...], qkv_weight[...])
    unit_rows = unit[...]
    correction = (
        grad_normed
        - jnp.mean(grad_normed, axis=-1, keepdims=True)
        - unit_rows * jnp.mean(grad_normed * unit_rows, axis=-1, keepdims=True)
    )
    grad_hidden = (cot[...].astype(jnp.float32) + inv_std * correction).astype(jnp.bfloat16)
    gh_loc[...] = grad_hidden.reshape(tm_count, block, width)

    back = [copy(gh_loc.at[t], ghf.at[tm], (dp, t)) for t in peers]
    start(*back)
    ghf[tm] = gh_loc[tm]

    def spread(t):
        return (
            copy(ghf.at[t, :, other_cols], ghx.at[1, t], y_peer),
            copy(ghf.at[t, :, my_cols], ghx.at[0, t], core_peer),
        )

    spreads = [start(*spread(tm))]
    received(swaps)

    q_rows = share_q.shape[3]
    for tile in range(3):
        cols = slice(tile * attn, (tile + 1) * attn)
        result = dot_columns(normed[:, core_cols], gqkv[:, cols]) + dot_columns(
            normed_o[...], gqkv_o[:, cols]
        )
        for i in range(4 * hh):
            share_q[i // 4, i // 2 % 2, i % 2, :, cols] = result[
                i * q_rows : (i + 1) * q_rows
            ].astype(jnp.bfloat16)

    def sums(share, first, total, second, result, y_first):
        steps = []
        for z in range(hh):
            if z < y_first:
                away, peer, stay = share.at[z, :, 1 - my], y_peer, share.at[z, :, my]
                away_2, peer_2, stay_2 = 1 - mx, x_peer, mx
            else:
                away, peer, stay = share.at[z, 1 - mx], x_peer, share.at[z, mx]
                away_2, peer_2, stay_2 = 1 - my, y_peer, my
            one = copy(away, first.at[z], peer)
            two = copy(total.at[z, away_2], second.at[z], peer_2)
            steps.append((one, stay, first.at[z], total.at[z], two, stay_2, second.at[z], result.at[z]))
        return steps

    q_steps = sums(share_q, q_r1, q_s1, q_r2, q_sx, hh // 2)
    start(*[one[0] for one in q_steps])
    p_rows = share_p.shape[3]
    step = attn // 2 // 128 * 128
    window = pl.ds(pl.multiple_of(core * step, 128), attn - step)
    for tile in range(2):
        cols = slice(tile * half, (tile + 1) * half)
        part[...] = dot_columns(att[:, window], cot[:, cols]) + dot_columns(
            att_o[:, window], cot_o[:, cols]
        )
        offset = pl.multiple_of(core * (attn // 2 - step), 8)
        result = part[pl.ds(offset, attn // 2), :]
        for i in range(2 * hh):
            share_p[i // 2, i % 2, tile] = result[i * p_rows : (i + 1) * p_rows].astype(
                jnp.bfloat16
            )
    p_steps = sums(share_p, p_r1, p_s1, p_r2, p_sx, hh)

    for one, t in zip(back, peers):
        received([one])
        spreads.append(start(*spread(t)))
    rim_out[...] = (
        ghf[...].astype(jnp.float32)[:, :loc].reshape(tm_count * loc, width).astype(jnp.bfloat16)
    )
    start(*[one[0] for one in p_steps])
    rim = copy(rim_out, rim_in, (dp, (tm + tm_count - 1) % tm_count))
    pl.when(tm > 0)(rim.start)

    received(lefts + rims)
    for k in range(1, 4):
        previous(k)
    forwards = []
    for (by_y, _), t in zip(spreads, [tm] + peers):
        received([by_y])
        forwards += start(copy(ghx.at[1, t], ghx.at[2, t], core_peer))
    received([by_core for _, by_core in spreads] + forwards)

    for one, stay, came, total, two, _, _, _ in q_steps + p_steps:
        received([one])
        total[...] = add(stay[...], came[...])
        start(two)

    c_rows = share_c.shape[3]
    conv_x = {}
    for tap in range(TAPS):
        result = dot_columns(
            left[0, tap].reshape(rows, half), ghf[:, :, my_cols].reshape(rows, half)
        )
        for k in range(1, 4):
            result += dot_columns(
                left[k, tap].reshape(rows, half), ghx[k - 1].reshape(rows, half)
            )
        for i in range(2 * hh):
            share_c[tap, i // 2, i % 2] = result[i * c_rows : (i + 1) * c_rows].astype(
                jnp.bfloat16
            )
        for z in range(hh):
            conv_x[tap, z] = copy(share_c.at[tap, z, 1 - mx], conv_rx.at[tap, z], x_peer)
            if tap == 0:
                start(conv_x[tap, z])

    above = (dp, (mz + 1) % high * 2 + mx)
    below = (dp, (mz + high - 1) % high * 2 + mx)
    chains = []

    def chain(total, came, ready=None):
        links = []
        for z in range(hh):
            if ready is not None:
                ready(z)
            up = copy(total.at[z], came.at[0, z], above)
            down = copy(total.at[z], came.at[1, z], below)
            links.append((core * hh + z, up, down))

            @pl.when((mz == 0) & (core * hh + z > mz))
            def _():
                up.start()

            @pl.when((mz == high - 1) & (core * hh + z < mz))
            def _():
                down.start()

        chains.append(links)
        return links, total, came

    def chain_on(links, total, came):
        for z, (owner, up, down) in enumerate(links):
            for inner, one, side in (
                ((mz > 0) & (owner > mz), up, 0),
                ((mz < high - 1) & (owner < mz), down, 1),
            ):

                @pl.when(inner)
                def _():
                    one.wait_recv()
                    total[z] = add(total[z], came[side, z])
                    one.start()

    def chain_end(links, total, came, place):
        for z, (owner, up, down) in enumerate(links):
            @pl.when((owner == mz) & (mz > 0))
            def _():
                up.wait_recv()
                total[z] = add(total[z], came[0, z])

            @pl.when((owner == mz) & (mz < high - 1))
            def _():
                down.wait_recv()
                total[z] = add(total[z], came[1, z])

            @pl.when(owner == mz)
            def _():
                place[...] = (total[z].astype(jnp.float32) * scale).astype(jnp.bfloat16)

    def conv_sum(tap):
        def ready(z):
            received([conv_x[tap, z]])
            if tap + 1 < TAPS:
                start(conv_x[tap + 1, z])
            conv_sx[tap, z] = add(share_c[tap, z, mx], conv_rx[tap, z])

        return chain(conv_sx.at[tap], conv_rz.at[tap], ready)

    pl.when(tm > 0)(rim.wait_send)
    pl.when(tm < tm_count - 1)(rim.wait_recv)

    @pl.when(tm == tm_count - 1)
    def _():
        rim_in[...] = jnp.zeros_like(rim_in)

    gh_rows = ghf[...].reshape(rows, width)

    def even_part(tile):
        part_of = slice(tile * half, (tile + 1) * half)
        grad = dot_rows_t(gh_rows, weight[part_of, width : 2 * width])
        frames_out[0, :, :, part_of] = grad.astype(jnp.bfloat16).reshape(tm_count, block, half)

    def odd_part(tile):
        part_of = slice(tile * half, (tile + 1) * half)
        before = dot_rows_t(gh_rows, weight[part_of, :width]).reshape(tm_count, block, half)
        rims = dot_rows_t(rim_in[...], weight[part_of, :width]).reshape(tm_count, loc, half)
        grad = dot_rows_t(gh_rows, weight[part_of, 2 * width :]).reshape(tm_count, block, half)
        grad += jnp.concatenate([before[:, loc:], rims], axis=1)
        frames_out[1, :, :, part_of] = grad.astype(jnp.bfloat16)

    last = []

    def gather(links, total, came, fin):
        chain_end(links, total, came, fin.at[my])
        to_y = copy(fin.at[my], fin.at[my], y_peer)
        own_to_core = copy(fin.at[my], fin.at[my], core_peer)
        other_to_core = copy(fin.at[1 - my], fin.at[1 - my], core_peer)
        last.append((to_y, own_to_core, other_to_core))

        @pl.when(is_dest)
        def _():
            to_y.start()
            own_to_core.start()

    sums_z = []
    for steps, totals, came_z in ((p_steps, p_sx, p_rz), (q_steps, q_sx, q_rz)):
        for _, _, _, total, two, stay, came, result in steps:
            received([two])
            result[...] = add(total[stay], came[...])
        sums_z.append(chain(totals, came_z))
    even_part(0)
    conv_z = [conv_sum(0)]
    for one in sums_z:
        chain_on(*one)
    even_part(1)
    conv_z.append(conv_sum(1))
    chain_on(*conv_z[0])
    gather(*sums_z[0], p_fin)
    gather(*sums_z[1], q_fin)
    odd_part(0)
    conv_z.append(conv_sum(2))
    chain_on(*conv_z[1])
    gather(*conv_z[0], conv_fin.at[0])
    odd_part(1)
    chain_on(*conv_z[2])
    gather(*conv_z[1], conv_fin.at[1])
    gather(*conv_z[2], conv_fin.at[2])

    def write_conv(tap):
        for y in range(2):
            conv_out[:, tap * width + y * half : tap * width + (y + 1) * half] = conv_fin[tap, y]

    def write_proj():
        for y in range(2):
            proj_out[:, y * half : (y + 1) * half] = p_fin[y]

    def write_qkv():
        qkv_out[...] = q_fin[...]

    writes = [write_proj, write_qkv] + [functools.partial(write_conv, tap) for tap in range(TAPS)]

    def land(index):
        to_y, own_to_core, other_to_core = last[index]

        @pl.when(is_dest)
        def _():
            to_y.wait_recv()
            other_to_core.start()

        @pl.when(not_dest)
        def _():
            own_to_core.wait_recv()
            other_to_core.wait_recv()

        writes[index]()

    for index in range(len(writes)):
        land(index)

    for one in sent:
        one.wait_send()
    for links in chains:
        for owner, up, down in links:
            pl.when(owner > mz)(up.wait_send)
            pl.when(owner < mz)(down.wait_send)

    @pl.when(is_dest)
    def _():
        for copies in last:
            for one in copies:
                one.wait_send()


def block(frames, cot, loc, conv_weight, qkv_weight, out_weight, scale):
    tm_count, block_rows, width = cot.shape
    high = tm_count // 2
    hh = high // 2
    half = width // 2
    rows = tm_count * block_rows
    attn = out_weight.shape[0]
    c_rows = width // tm_count
    q_rows = c_rows // 2
    p_rows = attn // tm_count
    edge = tm_count * loc
    bf16 = jnp.bfloat16

    def vmem(*shape, dtype=bf16):
        return pltpu.VMEM(shape, dtype)

    scratch = [
        vmem(*conv_weight.shape),
        vmem(*qkv_weight.shape),
        vmem(*out_weight.shape),
        vmem(edge, width),
        vmem(edge, width),
        vmem(4, TAPS, tm_count, block_rows, half),
        vmem(4, edge, half),
        vmem(*cot.shape),
        vmem(*cot.shape),
        vmem(*cot.shape),
        vmem(rows, width, dtype=jnp.float32),
        vmem(rows, width),
        vmem(rows, 3 * attn),
        vmem(rows, attn),
        vmem(rows, 3 * attn),
        vmem(rows, attn),
        vmem(*cot.shape),
        vmem(*cot.shape),
        vmem(3, tm_count, block_rows, half),
        vmem(rows, half),
        vmem(rows, 3 * attn),
        vmem(rows, attn),
        vmem(rows, width),
        vmem(attn - attn // 2 // 128 * 128, half, dtype=jnp.float32),
        vmem(TAPS, hh, 2, c_rows, half),
        vmem(TAPS, hh, c_rows, half),
        vmem(TAPS, hh, c_rows, half),
        vmem(TAPS, 2, hh, c_rows, half),
        vmem(TAPS, 2, c_rows, half),
        vmem(hh, 2, 2, q_rows, 3 * attn),
        vmem(hh, 2, q_rows, 3 * attn),
        vmem(hh, 2, q_rows, 3 * attn),
        vmem(hh, q_rows, 3 * attn),
        vmem(hh, q_rows, 3 * attn),
        vmem(2, hh, q_rows, 3 * attn),
        vmem(2, q_rows, 3 * attn),
        vmem(hh, 2, 2, p_rows, half),
        vmem(hh, 2, p_rows, half),
        vmem(hh, 2, p_rows, half),
        vmem(hh, p_rows, half),
        vmem(hh, p_rows, half),
        vmem(2, hh, p_rows, half),
        vmem(2, p_rows, half),
        vmem(edge, width),
        vmem(edge, width),
    ]
    copies = 2 + 2 * (tm_count - 1) + 9 + 4 + tm_count - 1 + 3 * tm_count + TAPS * hh + 4 * hh + 10 * hh + 15
    semaphores = pltpu.SemaphoreType.DMA((copies,))
    space = pl.BlockSpec(memory_space=pltpu.VMEM)
    return pl.pallas_call(
        functools.partial(block_kernel, scale, tm_count),
        out_shape=[
            jax.ShapeDtypeStruct(frames.shape, bf16),
            jax.ShapeDtypeStruct((c_rows, TAPS * width), bf16),
            jax.ShapeDtypeStruct((2, q_rows, 3 * attn), bf16),
            jax.ShapeDtypeStruct((p_rows, width), bf16),
        ],
        in_specs=[space] * 2 + [pl.BlockSpec(memory_space=pl.ANY)] * 3,
        out_specs=[space] * 4,
        scratch_shapes=scratch + [semaphores, semaphores, pltpu.SemaphoreType.DMA((5,))],
        compiler_params=pltpu.CompilerParams(
            collective_id=0, has_side_effects=True, vmem_limit_bytes=VMEM_LIMIT
        ),
        cost_estimate=pl.CostEstimate(
            flops=12_000_000_000, bytes_accessed=200_000_000, transcendentals=0
        ),
    )(frames, cot, conv_weight, qkv_weight, out_weight)


def local(latents, conv_weight, qkv_weight, out_weight, out_cotangent):
    videos, frames, places, width = latents.shape
    half = frames // 2
    dp_count = lax.axis_size("dp")
    tm_count = lax.axis_size("tm")
    loc = places // tm_count
    rows = half * places

    split = latents.reshape(half, 2, tm_count, loc, width)
    split = jnp.transpose(split, (1, 2, 0, 3, 4)).reshape(2, tm_count, half * loc, width)
    cotangent = jnp.transpose(out_cotangent.reshape(half, tm_count, loc, width), (1, 0, 2, 3))
    grad_scale = 1.0 / math.sqrt(dp_count * tm_count * rows)
    grad_frames, conv_grad, qkv_grad, proj_grad = block(
        split,
        cotangent.reshape(tm_count, half * loc, width),
        loc,
        conv_weight,
        qkv_weight,
        out_weight,
        grad_scale,
    )
    qkv_grad = qkv_grad.reshape(-1, qkv_grad.shape[-1])
    input_grad = jnp.transpose(
        grad_frames.reshape(2, tm_count, half, loc, width), (2, 0, 1, 3, 4)
    ).reshape(latents.shape)
    return (input_grad, conv_grad, qkv_grad, proj_grad)


def solution(mesh):
    return jax.shard_map(
        local,
        mesh=mesh,
        in_specs=(P("dp", "tm", None, None), P(), P(), P(), P("dp", "tm", None, None)),
        out_specs=(P("dp", "tm", None, None), P("tm", None), P("tm", None), P("tm", None)),
        check_vma=False,
    )
```

```python
import functools
import math

import jax
import jax.numpy as jnp
from jax import lax
from jax.experimental import pallas as pl
from jax.experimental.pallas import tpu as pltpu
from jax.sharding import PartitionSpec as P

HEADS = 10
HEAD = 64
EPSILON = 1e-05
TAPS = 3
VMEM_LIMIT = 62 * 1024 * 1024


def dot_rows(left_side, right_side):
    return jnp.dot(left_side, right_side, preferred_element_type=jnp.float32)


def dot_rows_t(left_side, right_side):
    return lax.dot_general(
        left_side, right_side, (((1,), (1,)), ((), ())), preferred_element_type=jnp.float32
    )


def dot_columns(left_side, right_side):
    return lax.dot_general(
        left_side, right_side, (((0,), (0,)), ((), ())), preferred_element_type=jnp.float32
    )


def flipped(index, mask, size):
    result = 0
    bit = 1
    while bit < size:
        own = index // bit % 2
        result += (1 - own if mask & bit else own) * bit
        bit *= 2
    return result


def attend(loc, width, qkv_ref, g_ref, grad_ref, attended_ref):
    rows = qkv_ref.shape[0]
    row_at = lax.broadcasted_iota(jnp.int32, (rows, rows), 0)
    column_at = lax.broadcasted_iota(jnp.int32, (rows, rows), 1)
    same = (row_at % loc) == (column_at % loc)
    lane = lax.broadcasted_iota(jnp.int32, (rows, 2 * HEAD), 1)
    scale = 1.0 / math.sqrt(HEAD)
    for pair in range(width // (2 * HEAD)):
        first = pair * 2 * HEAD
        q = qkv_ref[:, first : first + 2 * HEAD]
        k = qkv_ref[:, width + first : width + first + 2 * HEAD]
        v = qkv_ref[:, 2 * width + first : 2 * width + first + 2 * HEAD]
        g = g_ref[:, first : first + 2 * HEAD]
        zero = jnp.zeros_like(q)
        grad_q = grad_k = grad_v = attended = None
        kept = []
        for head in range(2):
            mine = (lane >= HEAD) if head else (lane < HEAD)
            q_h = jnp.where(mine, q, zero)
            v_h = jnp.where(mine, v, zero)
            g_h = jnp.where(mine, g, zero)
            scores = jnp.where(same, dot_rows_t(q_h, k) * scale, -1e30)
            expo = jnp.exp(scores - jnp.max(scores, axis=1, keepdims=True))
            probs = expo * (1.0 / jnp.sum(expo, axis=1, keepdims=True))
            probs_b = probs.astype(jnp.bfloat16)
            part = dot_rows(probs_b, v_h)
            attended = part if attended is None else attended + part
            part = dot_columns(probs_b, g_h)
            grad_v = part if grad_v is None else grad_v + part
            grad_probs = dot_rows_t(g_h, v)
            kept.append((mine, q_h, probs, grad_probs))
        attended_b = attended.astype(jnp.bfloat16)
        product = g.astype(jnp.float32) * attended_b.astype(jnp.float32)
        for mine, q_h, probs, grad_probs in kept:
            k_h = jnp.where(mine, k, zero)
            delta = jnp.sum(jnp.where(mine, product, 0.0), axis=1, keepdims=True)
            grad_scores = (probs * (grad_probs - delta) * scale).astype(jnp.bfloat16)
            part = dot_rows(grad_scores, k_h)
            grad_q = part if grad_q is None else grad_q + part
            part = dot_columns(grad_scores, q_h)
            grad_k = part if grad_k is None else grad_k + part
        grad_ref[:, first : first + 2 * HEAD] = grad_q.astype(jnp.bfloat16)
        grad_ref[:, width + first : width + first + 2 * HEAD] = grad_k.astype(jnp.bfloat16)
        grad_ref[:, 2 * width + first : 2 * width + first + 2 * HEAD] = grad_v.astype(
            jnp.bfloat16
        )
        attended_ref[:, first : first + 2 * HEAD] = attended_b


def block_kernel(scale, tm_count, *refs):
    frames, cot_rows, weight_hbm, qkv_hbm, out_hbm = refs[:5]
    frames_out, conv_out, qkv_out, proj_out = refs[5:9]
    weight, qkv_weight, out_weight = refs[9:12]
    rim_rows, odd_rim, left, left_rim, hid_own, hid, cot_in = refs[12:19]
    unit, normed, qkv_rows, grad_att, gqkv, att, gh_loc = refs[19:26]
    ghf, ghx, normed_o, gqkv_o, att_o, cot_o, part = refs[26:33]
    share_c, conv_rx, conv_sx, conv_rz, conv_fin = refs[33:38]
    share_q, q_r1, q_s1, q_r2, q_sx, q_rz, q_fin = refs[38:45]
    share_p, p_r1, p_s1, p_r2, p_sx, p_rz, p_fin = refs[45:52]
    rim_out, rim_in = refs[52:54]
    send_sem, recv_sem, load_sem = refs[54:57]
    high = tm_count // 2
    hh = high // 2
    block, width = cot_rows.shape[1:]
    even, odd = frames.at[0], frames.at[1]
    rows = tm_count * block
    half = width // 2
    attn = att.shape[1]
    loc = rim_in.shape[0] // tm_count
    dp, tm = lax.axis_index("dp"), lax.axis_index("tm")
    core, my = dp % 2, dp // 2
    mx, mz = tm % 2, tm // 2
    x_peer = (dp, tm + 1 - 2 * mx)
    y_peer = (dp + 2 - 4 * my, tm)
    diagonal = (dp + 3 - 4 * my - 2 * core, tm)
    core_peer = (dp + 1 - 2 * core, tm)
    is_dest = mz // hh == core
    not_dest = mz // hh != core
    peers = [flipped(tm, d, tm_count) for d in range(1, tm_count)]

    loads = []
    for i, tap in enumerate((1, 2, 0)):
        cols = pl.ds(tap * width, width)
        loads.append(
            pltpu.make_async_copy(weight_hbm.at[:, cols], weight.at[:, cols], load_sem.at[i])
        )
    loads.append(pltpu.make_async_copy(out_hbm, out_weight, load_sem.at[3]))
    loads.append(pltpu.make_async_copy(qkv_hbm, qkv_weight, load_sem.at[4]))
    for one in loads:
        one.start()

    barrier = pltpu.get_barrier_semaphore()
    for peer in [y_peer, core_peer, diagonal] + [(dp, t) for t in peers]:
        pl.semaphore_signal(
            barrier, inc=1, device_id=peer, device_id_type=pl.DeviceIdType.MESH
        )
    pl.semaphore_wait(barrier, tm_count + 2)

    count = [0]

    def copy(source, target, peer):
        index = count[0]
        count[0] += 1
        return pltpu.make_async_remote_copy(
            src_ref=source,
            dst_ref=target,
            send_sem=send_sem.at[index],
            recv_sem=recv_sem.at[index],
            device_id=peer,
            device_id_type=pl.DeviceIdType.MESH,
        )

    def start(*copies):
        for one in copies:
            one.start()
        return copies

    sent = []

    def received(copies):
        for one in copies:
            one.wait_recv()
            sent.append(one)

    my_cols = pl.ds(pl.multiple_of(my * half, 128), half)
    other_cols = pl.ds(pl.multiple_of((1 - my) * half, 128), half)
    core_cols = pl.ds(pl.multiple_of(core * half, 128), half)
    peer_core_cols = pl.ds(pl.multiple_of((1 - core) * half, 128), half)

    def add(a, b):
        return (a.astype(jnp.float32) + b.astype(jnp.float32)).astype(jnp.bfloat16)

    last_rows = odd[...].astype(jnp.float32)[:, block - loc :]
    rim_rows[...] = last_rows.reshape(tm_count * loc, width).astype(jnp.bfloat16)
    odd_next = copy(rim_rows, odd_rim, (dp, (tm + 1) % tm_count))
    pl.when(tm < tm_count - 1)(odd_next.start)
    cot_flights = start(*[copy(cot_rows.at[t], cot_in.at[tm], (dp, t)) for t in peers])
    cot_in[tm] = cot_rows[tm]

    lefts = []
    dp_peers = ((1, core_peer, peer_core_cols), (2, y_peer, core_cols), (3, diagonal, peer_core_cols))
    for which in range(2):
        for k, peer, cols in dp_peers:
            lefts += start(copy(frames.at[which, :, :, cols], left.at[k, 1 + which], peer))

    for one in loads[:2]:
        one.wait()
    even_rows = even[...].reshape(rows, width)
    odd_rows = odd[...].reshape(rows, width)
    for tile in range(2):
        cols = slice(tile * half, (tile + 1) * half)
        total = dot_rows(even_rows, weight[:, width + tile * half : width + (tile + 1) * half])
        total += dot_rows(
            odd_rows, weight[:, 2 * width + tile * half : 2 * width + (tile + 1) * half]
        )
        if tile == 0:
            loads[2].wait()
        before = dot_rows(odd_rows, weight[:, cols])
        if tile == 0:
            pl.when(tm < tm_count - 1)(odd_next.wait_send)
            pl.when(tm > 0)(odd_next.wait_recv)

            @pl.when(tm == 0)
            def _():
                odd_rim[...] = jnp.zeros_like(odd_rim)

        rims = dot_rows(odd_rim[...], weight[:, cols]).reshape(tm_count, loc, half)
        before = before.reshape(tm_count, block, half)
        total = total.reshape(tm_count, block, half)
        total += jnp.concatenate([rims, before[:, : block - loc]], axis=1)
        hid_own[:, :, cols] = total.astype(jnp.bfloat16)
    hid_flights = start(*[copy(hid_own.at[t], hid.at[tm], (dp, t)) for t in peers])
    hid[tm] = hid_own[tm]

    for which in range(2):
        left[0, 1 + which] = frames[which, :, :, core_cols]
    left_rim[0] = odd_rim[:, core_cols]
    rims = []
    for k, peer, cols in dp_peers:
        rims += start(copy(odd_rim.at[:, cols], left_rim.at[k], peer))

    def previous(k):
        later = left[k, 2].astype(jnp.float32)
        edge = left_rim[k].astype(jnp.float32).reshape(tm_count, loc, half)
        later = jnp.concatenate([edge, later[:, : block - loc]], axis=1)
        left[k, 0] = later.astype(jnp.bfloat16)

    previous(0)
    received(cot_flights)
    loads[3].wait()
    cot = cot_in.reshape(rows, width)
    swaps = list(start(copy(cot, cot_o, core_peer)))
    grad_att[...] = dot_rows_t(cot[...], out_weight[...]).astype(jnp.bfloat16)
    loads[4].wait()

    received(hid_flights)
    hidden = hid[...].reshape(rows, width).astype(jnp.float32)
    centred = hidden - jnp.mean(hidden, axis=-1, keepdims=True)
    inv_std = lax.rsqrt(jnp.mean(centred * centred, axis=-1, keepdims=True) + EPSILON)
    unit[...] = centred * inv_std
    normed[...] = unit[...].astype(jnp.bfloat16)
    swaps += start(copy(normed.at[:, peer_core_cols], normed_o, core_peer))
    for tile in range(3):
        cols = slice(tile * attn, (tile + 1) * attn)
        qkv_rows[:, cols] = dot_rows(normed[...], qkv_weight[:, cols]).astype(jnp.bfloat16)
    attend(loc, attn, qkv_rows, grad_att, gqkv, att)
    swaps += start(copy(gqkv, gqkv_o, core_peer), copy(att, att_o, core_peer))
    grad_normed = dot_rows_t(gqkv[...], qkv_weight[...])
    unit_rows = unit[...]
    correction = (
        grad_normed
        - jnp.mean(grad_normed, axis=-1, keepdims=True)
        - unit_rows * jnp.mean(grad_normed * unit_rows, axis=-1, keepdims=True)
    )
    grad_hidden = (cot[...].astype(jnp.float32) + inv_std * correction).astype(jnp.bfloat16)
    gh_loc[...] = grad_hidden.reshape(tm_count, block, width)

    back = [copy(gh_loc.at[t], ghf.at[tm], (dp, t)) for t in peers]
    start(*back)
    ghf[tm] = gh_loc[tm]

    def spread(t):
        return (
            copy(ghf.at[t, :, other_cols], ghx.at[1, t], y_peer),
            copy(ghf.at[t, :, my_cols], ghx.at[0, t], core_peer),
        )

    spreads = [start(*spread(tm))]
    received(swaps)

    q_rows = share_q.shape[3]
    for tile in range(3):
        cols = slice(tile * attn, (tile + 1) * attn)
        result = dot_columns(normed[:, core_cols], gqkv[:, cols]) + dot_columns(
            normed_o[...], gqkv_o[:, cols]
        )
        for i in range(4 * hh):
            share_q[i // 4, i // 2 % 2, i % 2, :, cols] = result[
                i * q_rows : (i + 1) * q_rows
            ].astype(jnp.bfloat16)

    def sums(share, first, total, second, result, y_first):
        steps = []
        for z in range(hh):
            if z < y_first:
                away, peer, stay = share.at[z, :, 1 - my], y_peer, share.at[z, :, my]
                away_2, peer_2, stay_2 = 1 - mx, x_peer, mx
            else:
                away, peer, stay = share.at[z, 1 - mx], x_peer, share.at[z, mx]
                away_2, peer_2, stay_2 = 1 - my, y_peer, my
            one = copy(away, first.at[z], peer)
            two = copy(total.at[z, away_2], second.at[z], peer_2)
            steps.append((one, stay, first.at[z], total.at[z], two, stay_2, second.at[z], result.at[z]))
        return steps

    q_steps = sums(share_q, q_r1, q_s1, q_r2, q_sx, hh // 2)
    start(*[one[0] for one in q_steps])
    p_rows = share_p.shape[3]
    step = attn // 2 // 128 * 128
    window = pl.ds(pl.multiple_of(core * step, 128), attn - step)
    for tile in range(2):
        cols = slice(tile * half, (tile + 1) * half)
        part[...] = dot_columns(att[:, window], cot[:, cols]) + dot_columns(
            att_o[:, window], cot_o[:, cols]
        )
        offset = pl.multiple_of(core * (attn // 2 - step), 8)
        result = part[pl.ds(offset, attn // 2), :]
        for i in range(2 * hh):
            share_p[i // 2, i % 2, tile] = result[i * p_rows : (i + 1) * p_rows].astype(
                jnp.bfloat16
            )
    p_steps = sums(share_p, p_r1, p_s1, p_r2, p_sx, hh)

    for one, t in zip(back, peers):
        received([one])
        spreads.append(start(*spread(t)))
    rim_out[...] = (
        ghf[...].astype(jnp.float32)[:, :loc].reshape(tm_count * loc, width).astype(jnp.bfloat16)
    )
    start(*[one[0] for one in p_steps])
    rim = copy(rim_out, rim_in, (dp, (tm + tm_count - 1) % tm_count))
    pl.when(tm > 0)(rim.start)

    received(lefts + rims)
    for k in range(1, 4):
        previous(k)
    forwards = []
    for (by_y, _), t in zip(spreads, [tm] + peers):
        received([by_y])
        forwards += start(copy(ghx.at[1, t], ghx.at[2, t], core_peer))
    received([by_core for _, by_core in spreads] + forwards)

    for one, stay, came, total, two, _, _, _ in q_steps + p_steps:
        received([one])
        total[...] = add(stay[...], came[...])
        start(two)

    c_rows = share_c.shape[3]
    conv_x = {}
    for tap in range(TAPS):
        result = dot_columns(
            left[0, tap].reshape(rows, half), ghf[:, :, my_cols].reshape(rows, half)
        )
        for k in range(1, 4):
            result += dot_columns(
                left[k, tap].reshape(rows, half), ghx[k - 1].reshape(rows, half)
            )
        for i in range(2 * hh):
            share_c[tap, i // 2, i % 2] = result[i * c_rows : (i + 1) * c_rows].astype(
                jnp.bfloat16
            )
        for z in range(hh):
            conv_x[tap, z] = copy(share_c.at[tap, z, 1 - mx], conv_rx.at[tap, z], x_peer)
            if tap == 0:
                start(conv_x[tap, z])

    above = (dp, (mz + 1) % high * 2 + mx)
    below = (dp, (mz + high - 1) % high * 2 + mx)
    chains = []

    def chain(total, came, ready=None):
        links = []
        for z in range(hh):
            if ready is not None:
                ready(z)
            up = copy(total.at[z], came.at[0, z], above)
            down = copy(total.at[z], came.at[1, z], below)
            links.append((core * hh + z, up, down))

            @pl.when((mz == 0) & (core * hh + z > mz))
            def _():
                up.start()

            @pl.when((mz == high - 1) & (core * hh + z < mz))
            def _():
                down.start()

        chains.append(links)
        return links, total, came

    def chain_on(links, total, came):
        for z, (owner, up, down) in enumerate(links):
            for inner, one, side in (
                ((mz > 0) & (owner > mz), up, 0),
                ((mz < high - 1) & (owner < mz), down, 1),
            ):

                @pl.when(inner)
                def _():
                    one.wait_recv()
                    total[z] = add(total[z], came[side, z])
                    one.start()

    def chain_end(links, total, came, place):
        for z, (owner, up, down) in enumerate(links):
            @pl.when((owner == mz) & (mz > 0))
            def _():
                up.wait_recv()
                total[z] = add(total[z], came[0, z])

            @pl.when((owner == mz) & (mz < high - 1))
            def _():
                down.wait_recv()
                total[z] = add(total[z], came[1, z])

            @pl.when(owner == mz)
            def _():
                place[...] = (total[z].astype(jnp.float32) * scale).astype(jnp.bfloat16)

    def conv_sum(tap):
        def ready(z):
            received([conv_x[tap, z]])
            if tap + 1 < TAPS:
                start(conv_x[tap + 1, z])
            conv_sx[tap, z] = add(share_c[tap, z, mx], conv_rx[tap, z])

        return chain(conv_sx.at[tap], conv_rz.at[tap], ready)

    pl.when(tm > 0)(rim.wait_send)
    pl.when(tm < tm_count - 1)(rim.wait_recv)

    @pl.when(tm == tm_count - 1)
    def _():
        rim_in[...] = jnp.zeros_like(rim_in)

    gh_rows = ghf[...].reshape(rows, width)

    def even_part(tile):
        part_of = slice(tile * half, (tile + 1) * half)
        grad = dot_rows_t(gh_rows, weight[part_of, width : 2 * width])
        frames_out[0, :, :, part_of] = grad.astype(jnp.bfloat16).reshape(tm_count, block, half)

    def odd_part(tile):
        part_of = slice(tile * half, (tile + 1) * half)
        before = dot_rows_t(gh_rows, weight[part_of, :width]).reshape(tm_count, block, half)
        rims = dot_rows_t(rim_in[...], weight[part_of, :width]).reshape(tm_count, loc, half)
        grad = dot_rows_t(gh_rows, weight[part_of, 2 * width :]).reshape(tm_count, block, half)
        grad += jnp.concatenate([before[:, loc:], rims], axis=1)
        frames_out[1, :, :, part_of] = grad.astype(jnp.bfloat16)

    last = []

    def gather(links, total, came, fin):
        chain_end(links, total, came, fin.at[my])
        to_y = copy(fin.at[my], fin.at[my], y_peer)
        own_to_core = copy(fin.at[my], fin.at[my], core_peer)
        other_to_core = copy(fin.at[1 - my], fin.at[1 - my], core_peer)
        last.append((to_y, own_to_core, other_to_core))

        @pl.when(is_dest)
        def _():
            to_y.start()
            own_to_core.start()

    def write_conv(tap):
        for y in range(2):
            conv_out[:, tap * width + y * half : tap * width + (y + 1) * half] = conv_fin[tap, y]

    def write_proj():
        for y in range(2):
            proj_out[:, y * half : (y + 1) * half] = p_fin[y]

    def write_qkv():
        qkv_out[...] = q_fin[...]

    writes = [write_proj, write_qkv] + [functools.partial(write_conv, tap) for tap in range(TAPS)]

    def land(index):
        to_y, own_to_core, other_to_core = last[index]

        @pl.when(is_dest)
        def _():
            to_y.wait_recv()
            other_to_core.start()

        @pl.when(not_dest)
        def _():
            own_to_core.wait_recv()
            other_to_core.wait_recv()

        writes[index]()

    sums_z = []
    for steps, totals, came_z in ((p_steps, p_sx, p_rz), (q_steps, q_sx, q_rz)):
        for _, _, _, total, two, stay, came, result in steps:
            received([two])
            result[...] = add(total[stay], came[...])
        sums_z.append(chain(totals, came_z))
    even_part(0)
    conv_z = [conv_sum(0)]
    for one in sums_z:
        chain_on(*one)
    even_part(1)
    conv_z.append(conv_sum(1))
    chain_on(*conv_z[0])
    gather(*sums_z[0], p_fin)
    gather(*sums_z[1], q_fin)
    odd_part(0)
    conv_z.append(conv_sum(2))
    chain_on(*conv_z[1])
    gather(*conv_z[0], conv_fin.at[0])
    odd_part(1)
    land(0)
    land(1)
    chain_on(*conv_z[2])
    land(2)
    gather(*conv_z[1], conv_fin.at[1])
    gather(*conv_z[2], conv_fin.at[2])

    for index in range(3, len(writes)):
        land(index)

    for one in sent:
        one.wait_send()
    for links in chains:
        for owner, up, down in links:
            pl.when(owner > mz)(up.wait_send)
            pl.when(owner < mz)(down.wait_send)

    @pl.when(is_dest)
    def _():
        for copies in last:
            for one in copies:
                one.wait_send()


def block(frames, cot, loc, conv_weight, qkv_weight, out_weight, scale):
    tm_count, block_rows, width = cot.shape
    high = tm_count // 2
    hh = high // 2
    half = width // 2
    rows = tm_count * block_rows
    attn = out_weight.shape[0]
    c_rows = width // tm_count
    q_rows = c_rows // 2
    p_rows = attn // tm_count
    edge = tm_count * loc
    bf16 = jnp.bfloat16

    def vmem(*shape, dtype=bf16):
        return pltpu.VMEM(shape, dtype)

    scratch = [
        vmem(*conv_weight.shape),
        vmem(*qkv_weight.shape),
        vmem(*out_weight.shape),
        vmem(edge, width),
        vmem(edge, width),
        vmem(4, TAPS, tm_count, block_rows, half),
        vmem(4, edge, half),
        vmem(*cot.shape),
        vmem(*cot.shape),
        vmem(*cot.shape),
        vmem(rows, width, dtype=jnp.float32),
        vmem(rows, width),
        vmem(rows, 3 * attn),
        vmem(rows, attn),
        vmem(rows, 3 * attn),
        vmem(rows, attn),
        vmem(*cot.shape),
        vmem(*cot.shape),
        vmem(3, tm_count, block_rows, half),
        vmem(rows, half),
        vmem(rows, 3 * attn),
        vmem(rows, attn),
        vmem(rows, width),
        vmem(attn - attn // 2 // 128 * 128, half, dtype=jnp.float32),
        vmem(TAPS, hh, 2, c_rows, half),
        vmem(TAPS, hh, c_rows, half),
        vmem(TAPS, hh, c_rows, half),
        vmem(TAPS, 2, hh, c_rows, half),
        vmem(TAPS, 2, c_rows, half),
        vmem(hh, 2, 2, q_rows, 3 * attn),
        vmem(hh, 2, q_rows, 3 * attn),
        vmem(hh, 2, q_rows, 3 * attn),
        vmem(hh, q_rows, 3 * attn),
        vmem(hh, q_rows, 3 * attn),
        vmem(2, hh, q_rows, 3 * attn),
        vmem(2, q_rows, 3 * attn),
        vmem(hh, 2, 2, p_rows, half),
        vmem(hh, 2, p_rows, half),
        vmem(hh, 2, p_rows, half),
        vmem(hh, p_rows, half),
        vmem(hh, p_rows, half),
        vmem(2, hh, p_rows, half),
        vmem(2, p_rows, half),
        vmem(edge, width),
        vmem(edge, width),
    ]
    copies = 2 + 2 * (tm_count - 1) + 9 + 4 + tm_count - 1 + 3 * tm_count + TAPS * hh + 4 * hh + 10 * hh + 15
    semaphores = pltpu.SemaphoreType.DMA((copies,))
    space = pl.BlockSpec(memory_space=pltpu.VMEM)
    return pl.pallas_call(
        functools.partial(block_kernel, scale, tm_count),
        out_shape=[
            jax.ShapeDtypeStruct(frames.shape, bf16),
            jax.ShapeDtypeStruct((c_rows, TAPS * width), bf16),
            jax.ShapeDtypeStruct((2, q_rows, 3 * attn), bf16),
            jax.ShapeDtypeStruct((p_rows, width), bf16),
        ],
        in_specs=[space] * 2 + [pl.BlockSpec(memory_space=pl.ANY)] * 3,
        out_specs=[space] * 4,
        scratch_shapes=scratch + [semaphores, semaphores, pltpu.SemaphoreType.DMA((5,))],
        compiler_params=pltpu.CompilerParams(
            collective_id=0, has_side_effects=True, vmem_limit_bytes=VMEM_LIMIT
        ),
        cost_estimate=pl.CostEstimate(
            flops=12_000_000_000, bytes_accessed=200_000_000, transcendentals=0
        ),
    )(frames, cot, conv_weight, qkv_weight, out_weight)


def local(latents, conv_weight, qkv_weight, out_weight, out_cotangent):
    videos, frames, places, width = latents.shape
    half = frames // 2
    dp_count = lax.axis_size("dp")
    tm_count = lax.axis_size("tm")
    loc = places // tm_count
    rows = half * places

    split = latents.reshape(half, 2, tm_count, loc, width)
    split = jnp.transpose(split, (1, 2, 0, 3, 4)).reshape(2, tm_count, half * loc, width)
    cotangent = jnp.transpose(out_cotangent.reshape(half, tm_count, loc, width), (1, 0, 2, 3))
    grad_scale = 1.0 / math.sqrt(dp_count * tm_count * rows)
    grad_frames, conv_grad, qkv_grad, proj_grad = block(
        split,
        cotangent.reshape(tm_count, half * loc, width),
        loc,
        conv_weight,
        qkv_weight,
        out_weight,
        grad_scale,
    )
    qkv_grad = qkv_grad.reshape(-1, qkv_grad.shape[-1])
    input_grad = jnp.transpose(
        grad_frames.reshape(2, tm_count, half, loc, width), (2, 0, 1, 3, 4)
    ).reshape(latents.shape)
    return (input_grad, conv_grad, qkv_grad, proj_grad)


def solution(mesh):
    return jax.shard_map(
        local,
        mesh=mesh,
        in_specs=(P("dp", "tm", None, None), P(), P(), P(), P("dp", "tm", None, None)),
        out_specs=(P("dp", "tm", None, None), P("tm", None), P("tm", None), P("tm", None)),
        check_vma=False,
    )
```
